32 devices in a mesh: gx: 2 (over x), gy: 4 (over z), gz: 4 (over y, core).
Axes of the slice: x: 2, y: 2, z: 4, core: 2. Of those that a mesh axis runs over, the one named last changes fastest.
Arguments:
- pressure_zero: float32 [32, 64, 1024], P('gx', 'gy', 'gz'), may hold values from -1.2 to 1.2
- pressure_one: float32 [32, 64, 1024], P('gx', 'gy', 'gz'), may hold values from -1.2 to 1.2
- adjoint_upper: float32 [32, 64, 1024], P('gx', 'gy', 'gz'), may hold values from -6 to 6
- adjoint_top: float32 [32, 64, 1024], P('gx', 'gy', 'gz'), may hold values from -6 to 6
- courant_factor: float32 [32, 64, 1024], P('gx', 'gy', 'gz'), may hold values from 0.08 to 0.19
- residual: float32 [4, 1024], P(None, 'gz'), may hold values from -6 to 6
- receiver_cell: int32 [3, 1024], replicated, may hold values from 4 to 1019, as said below
- tap_offset: int32 [3, 16, 1024], replicated, may hold values from -4 to 4
- tap_weight: float32 [16, 1024], replicated, may hold values from -3 to 3
- trace_receiver: int32 [1024], replicated, may hold values from 0 to 1023, each once
Outputs:
- gradient: float32 [32, 64, 1024], P('gx', 'gy', 'gz')
- adjoint_one: float32 [32, 64, 1024], P('gx', 'gy', 'gz')
- adjoint_zero: float32 [32, 64, 1024], P('gx', 'gy', 'gz')
The draws below stay inside these ranges and needn't reach their ends.
Inputs may be any that keep to these rules, and one draw needn't show every extreme that they name: `receiver_cell`: coordinate 0 of a receiver cell lies in 4 to 27, coordinate 1 in 4 to 59, coordinate 2 in 4 to 1019.
All inputs are finite; a program needn't handle non-finite values.
Results may differ from the reference program's by a relative error of at most 0.00002.
Values sent between devices are 32-bit elements; how exact they have to be, the bound alone decides.
A program may use at most 128 MiB of HBM per device.

```python
import math
import jax
import jax.numpy as jnp

STEPS = 4
TAPS = 16
MICS = 1024
NX = 32
NY = 64
NZ = 1024


def draw_receiver_cell(key, part):
    key_centre, key_pick, key_spread = jax.random.split(key, 3)
    limits = jnp.array([NX, NY, NZ], dtype=jnp.int32)[:, None]
    centres = jax.random.randint(key_centre, (3, 8), 0, 1 << 20) % (limits - 8) + 4
    choose = jax.random.randint(key_pick, (MICS,), 0, 8)
    spread = jax.random.randint(key_spread, (3, MICS), -24, 25)
    picked = jnp.take(centres, choose, axis=1) + spread
    placed = jnp.clip(picked, 4, limits - 5)
    placed = placed.at[:, 0].set(limits[:, 0] - 5).at[:, 1].set(4)
    return placed.astype(jnp.int32)


def set_ends(result, rng, smallest, top_value):
    longest = result.shape.index(max(result.shape))
    spots = []
    for shift in (0, 1):
        where = [jax.random.randint(jax.random.fold_in(rng, axis), (), 0, length) for axis, length in enumerate(result.shape)]
        where[longest] = (where[longest] + shift) % result.shape[longest]
        spots.append(tuple(where))
    return result.at[spots[0]].set(smallest).at[spots[1]].set(top_value)


def block_scale(own_key, extent, shards, low, top_value):
    gain, own = 1.0, jax.random.fold_in(own_key, 6)
    for axis_at, parts in shards:
        draws = jnp.exp(jax.random.uniform(jax.random.fold_in(own, axis_at), (parts,), jnp.float32, low / len(shards), top_value / len(shards)))
        gain = gain * jnp.repeat(draws, extent[axis_at] // parts).reshape([-1 if axis == axis_at else 1 for axis in range(len(extent))])
    return gain


def normal_values(stream_key, extent, width, most, cuts=(), kind=jnp.bfloat16):
    loudness = block_scale(stream_key, extent, cuts, -0.22, 0.18) if cuts else 1.0
    entries = jax.random.normal(stream_key, extent, jnp.float32) * width * loudness
    return jnp.minimum(jnp.maximum(entries, -most), most).astype(kind)


def setup_inputs(seed: int = 0) -> dict:
    key_of = jax.random.split(jax.random.key(seed), 11)
    return {
        "pressure_zero": normal_values(key_of[0], (NX, NY, NZ), 0.2, 1.2, ((0, 2), (1, 4), (2, 4)), jnp.float32),
        "pressure_one": normal_values(key_of[1], (NX, NY, NZ), 0.2, 1.2, ((0, 2), (1, 4), (2, 4)), jnp.float32),
        "adjoint_upper": normal_values(key_of[2], (NX, NY, NZ), 1.0, 6.0, ((0, 2), (1, 4), (2, 4)), jnp.float32),
        "adjoint_top": normal_values(key_of[3], (NX, NY, NZ), 1.0, 6.0, ((0, 2), (1, 4), (2, 4)), jnp.float32),
        "courant_factor": jnp.clip(jnp.exp(math.log(0.19) - 0.86499745 * jax.random.uniform(key_of[4], (NX, NY, NZ), jnp.float32) ** block_scale(key_of[4], (NX, NY, NZ), ((0, 2), (1, 4), (2, 4)), -0.2, 0.2)), 0.08, 0.19),
        "residual": normal_values(key_of[5], (STEPS, MICS), 1.0, 6.0, ((1, 4),), jnp.float32),
        "receiver_cell": draw_receiver_cell(jax.random.fold_in(key_of[10], 71), 0),
        "tap_offset": set_ends(jax.random.randint(key_of[7], (3, TAPS, MICS), -4, 5), jax.random.fold_in(key_of[7], 1), -4, 4).astype(jnp.int32),
        "tap_weight": normal_values(key_of[8], (TAPS, MICS), 0.5, 3.0, (), jnp.float32),
        "trace_receiver": jax.random.permutation(key_of[9], MICS).astype(jnp.int32),
    }


STENCIL_WEIGHTS = (-205.0 / 72.0, 8.0 / 5.0, -1.0 / 5.0, 8.0 / 315.0, -1.0 / 560.0)


def laplace(grid_field):
    size_x, size_y, size_z = grid_field.shape[-3:]
    centre = grid_field[..., 4:size_x - 4, 4:size_y - 4, 4:size_z - 4]
    summed = (3.0 * STENCIL_WEIGHTS[0]) * centre
    for reach in range(1, 5):
        summed = summed + STENCIL_WEIGHTS[reach] * (
            grid_field[..., 4 + reach:size_x - 4 + reach, 4:size_y - 4, 4:size_z - 4]
            + grid_field[..., 4 - reach:size_x - 4 - reach, 4:size_y - 4, 4:size_z - 4]
            + grid_field[..., 4:size_x - 4, 4 + reach:size_y - 4 + reach, 4:size_z - 4]
            + grid_field[..., 4:size_x - 4, 4 - reach:size_y - 4 - reach, 4:size_z - 4]
            + grid_field[..., 4:size_x - 4, 4:size_y - 4, 4 + reach:size_z - 4 + reach]
            + grid_field[..., 4:size_x - 4, 4:size_y - 4, 4 - reach:size_z - 4 - reach])
    return summed


def laplace_full(grid_field):
    return laplace(jnp.pad(grid_field, 4))


def reference(pressure_zero, pressure_one, adjoint_upper, adjoint_top, courant_factor, residual, receiver_cell, tap_offset, tap_weight, trace_receiver):
    step_count = residual.shape[0]
    earlier, current = pressure_zero, pressure_one
    laplacians = []
    for level in range(step_count):
        curvature = laplace_full(current)
        laplacians.append(curvature)
        if level + 1 < step_count:
            earlier, current = current, 2.0 * current - earlier + courant_factor * curvature
    mic_cells = jnp.take(receiver_cell, trace_receiver, axis=1)
    tap_cells = jnp.take(tap_offset, trace_receiver, axis=2)
    weights = jnp.take(tap_weight, trace_receiver, axis=1)
    position = mic_cells[:, None, :] + tap_cells
    flat_index = ((position[0] * NY + position[1]) * NZ + position[2]).reshape(-1).astype(jnp.int32)
    amounts = weights[None, :, :] * residual[:, None, :]
    upper_level, level_now = adjoint_upper, adjoint_top
    gradient = jnp.zeros_like(adjoint_top)
    for level in range(step_count, 0, -1):
        gradient = gradient + level_now * laplacians[level - 1]
        lowered = 2.0 * level_now - upper_level + laplace_full(courant_factor * level_now)
        lowered = lowered.reshape(-1).at[flat_index].add(amounts[level - 1].reshape(-1)).reshape(level_now.shape)
        upper_level, level_now = level_now, lowered
    return gradient, upper_level, level_now
```

```python
import functools

import jax
import jax.numpy as jnp
from jax import lax
from jax.experimental import pallas as pl
from jax.experimental.pallas import tpu as pltpu
from jax.sharding import PartitionSpec as P

C = (-205.0 / 72.0, 8.0 / 5.0, -1.0 / 5.0, 8.0 / 315.0, -1.0 / 560.0)
AXES = ("gx", "gy", "gz")
MESH = pl.DeviceIdType.MESH


def split3(v):
    hi = v.astype(jnp.bfloat16)
    rest = v - hi.astype(jnp.float32)
    mid = rest.astype(jnp.bfloat16)
    lo = (rest - mid.astype(jnp.float32)).astype(jnp.bfloat16)
    return [hi, mid, lo]


def nt(a, b):
    return lax.dot_general(a, b, (((1,), (1,)), ((), ())), preferred_element_type=jnp.float32)


def source_kernel(block, res_ref, cell_ref, off_ref, w_ref, tr_ref, out_ref, table, info):
    bx, by, bz = block
    starts = [lax.axis_index(a) * n for a, n in zip(AXES, block)]
    taps, mics = w_ref.shape
    steps = res_ref.shape[1]
    rel = [cell_ref[d : d + 1, :] - starts[d] for d in range(3)]
    near = functools.reduce(
        jnp.logical_and, [(rel[d] >= -4) & (rel[d] < block[d] + 4) for d in range(3)]
    )
    at = [rel[d] + off_ref[d] for d in range(3)]
    inside = functools.reduce(
        jnp.logical_and, [(at[d] >= 0) & (at[d] < block[d]) for d in range(3)]
    )
    row = jnp.where(inside, at[0] * by + at[1], -1)
    col = jnp.where(inside, at[2], -1)
    table[0:taps, :] = row.astype(jnp.float32).astype(jnp.bfloat16)
    table[taps : 2 * taps, :] = col.astype(jnp.float32).astype(jnp.bfloat16)
    for i, part in enumerate(split3(w_ref[...])):
        table[(2 + i) * taps : (3 + i) * taps, :] = part
    near_f = jnp.where(near, 1.0, 0.0)
    lanes = 128
    blocks = mics // lanes
    tri = (
        lax.broadcasted_iota(jnp.int32, (lanes, lanes), 0)
        < lax.broadcasted_iota(jnp.int32, (lanes, lanes), 1)
    )
    tri = jnp.where(tri, 1.0, 0.0).astype(jnp.bfloat16)
    base = jnp.float32(0.0)
    for i in range(blocks):
        part = near_f[:, i * lanes : (i + 1) * lanes]
        before = jnp.dot(
            jnp.broadcast_to(part, (8, lanes)).astype(jnp.bfloat16),
            tri,
            preferred_element_type=jnp.float32,
        )[0:1]
        slot = jnp.where(part > 0.5, before + base, -1.0)
        info[0:1, i * lanes : (i + 1) * lanes] = slot
        base = base + jnp.sum(part)
    count = base.astype(jnp.int32)
    out_ref[...] = jnp.zeros_like(out_ref)
    share = 2
    held = lanes // share
    per = taps // share
    part_of = lax.broadcasted_iota(jnp.int32, (per, lanes), 1) // held

    def spread(v):
        out = v[0:per]
        for i in range(1, share):
            out = jnp.where(part_of == i, v[i * per : (i + 1) * per], out)
        return out

    def chunk(j, carry):
        slots = (lax.broadcasted_iota(jnp.int32, (held, mics), 0) + j * held).astype(jnp.float32)
        sel = jnp.where(slots == info[0:1, :], 1.0, 0.0)
        mic_id = lax.broadcasted_iota(jnp.int32, (1, mics), 1).astype(jnp.float32)
        mic = jnp.sum(sel * (mic_id + 1.0), axis=1, keepdims=True) - 1.0
        sel_r = jnp.where(tr_ref[...].astype(jnp.float32) == mic, 1.0, 0.0).astype(jnp.bfloat16)
        tab = jnp.concatenate([nt(table[...], sel.astype(jnp.bfloat16))] * share, axis=1)
        rows = spread(tab[0:taps])
        cols = spread(tab[taps : 2 * taps])
        weights = spread(
            tab[2 * taps : 3 * taps] + tab[3 * taps : 4 * taps] + tab[4 * taps : 5 * taps]
        )
        whole = jnp.concatenate([res_ref[g] for g in range(res_ref.shape[0])], axis=1)
        res = sum(nt(part, sel_r) for part in split3(whole))
        res = jnp.concatenate([res] * share, axis=1)
        iota_row = lax.broadcasted_iota(jnp.int32, (bx * by, lanes), 0).astype(jnp.float32)
        iota_col = lax.broadcasted_iota(jnp.int32, (bz, lanes), 0).astype(jnp.float32)
        group = 4
        for t0 in range(0, per, group):
            left, right = [[] for _ in range(steps)], []
            for t in range(t0, t0 + group):
                row_hot = iota_row == rows[t : t + 1]
                col_hot = jnp.where(iota_col == cols[t : t + 1], 1.0, 0.0).astype(jnp.bfloat16)
                right += [col_hot, col_hot]
                for n in range(steps):
                    amount = weights[t : t + 1] * res[n : n + 1]
                    hi = amount.astype(jnp.bfloat16).astype(jnp.float32)
                    lo = amount - hi
                    left[n].append(jnp.where(row_hot, hi, 0.0).astype(jnp.bfloat16))
                    left[n].append(jnp.where(row_hot, lo, 0.0).astype(jnp.bfloat16))
            right = jnp.concatenate(right, axis=1)
            for n in range(steps):
                out_ref[n] += nt(jnp.concatenate(left[n], axis=1), right)
        return carry

    lax.fori_loop(0, (count + held - 1) // held, chunk, 0)


def build_sources(block, residual, receiver_cell, tap_offset, tap_weight, trace_receiver):
    steps = residual.shape[1]
    taps, mics = tap_weight.shape
    return pl.pallas_call(
        functools.partial(source_kernel, block),
        out_shape=jax.ShapeDtypeStruct((steps, block[0] * block[1], block[2]), jnp.float32),
        in_specs=[pl.BlockSpec(memory_space=pltpu.VMEM)] * 5,
        out_specs=pl.BlockSpec(memory_space=pltpu.VMEM),
        scratch_shapes=[
            pltpu.VMEM((5 * taps, mics), jnp.bfloat16),
            pltpu.VMEM((8, mics), jnp.float32),
        ],
        compiler_params=pltpu.CompilerParams(vmem_limit_bytes=32 * 2**20),
        name="sources",
    )(residual, receiver_cell, tap_offset, tap_weight, trace_receiver.reshape(1, mics))


def stencil(d):
    d = jnp.abs(d)
    return sum(jnp.where(d == k, float(round(5040 * C[k])), 0.0) for k in range(1, 5))


def cross(dx, dy):
    return jnp.where(dy == 0, stencil(dx), 0.0) + jnp.where(dx == 0, stencil(dy), 0.0)


def matrices(nx, ny, m_in, m_face, m_z, m_end):
    def grid(ref):
        return [lax.broadcasted_iota(jnp.int32, ref.shape, d) for d in range(2)]

    to, at = grid(m_in)
    m_in[...] = cross(to // ny - at // ny, to % ny - at % ny).astype(jnp.bfloat16)
    to, at = grid(m_face)
    x, y = to // ny, to % ny
    upper = at >= 4 * ny
    face = at - jnp.where(upper, 4 * ny, 0)
    in_x = cross(x - (face // ny + jnp.where(upper, nx, -4)), y - face % ny)
    pack = at - 8 * ny
    upper = pack >= 4 * nx
    pack = pack - jnp.where(upper, 4 * nx, 0)
    far = jnp.where(pack % 8 < 4, 0, 1) == jnp.where(upper, 1, 0)
    face_x = pack // 8 + jnp.where(far, nx // 2, 0)
    in_y = cross(x - face_x, y - (pack % 4 + jnp.where(upper, ny, -4)))
    m_face[...] = jnp.where(at < 8 * ny, in_x, in_y).astype(jnp.bfloat16)
    at, to = grid(m_z)
    m_z[...] = stencil(to - at).astype(jnp.bfloat16)
    at, to = grid(m_end)
    m_end[...] = stencil(to - jnp.where(at < 64, at + m_z.shape[0], at - 128)).astype(jnp.bfloat16)


def gather_kernel(n, block, res, out, m_in, m_face, m_z, m_end, land, send_sem, recv_sem):
    gz = lax.axis_index("gz")
    ahead = [{"gz": lax.rem(gz + k, n)} for k in range(1, n)]
    barrier = pltpu.get_barrier_semaphore()
    for other in ahead:
        pl.semaphore_signal(barrier, inc=1, device_id=other, device_id_type=MESH)
    pl.semaphore_wait(barrier, n - 1)
    moves = [
        pltpu.make_async_remote_copy(
            src_ref=res, dst_ref=land.at[gz],
            send_sem=send_sem.at[k], recv_sem=recv_sem.at[k],
            device_id=ahead[k], device_id_type=MESH,
        )
        for k in range(n - 1)
    ]
    for move in moves:
        move.start()
    matrices(block[0], block[1], m_in, m_face, m_z, m_end)
    land[gz] = res[...]
    for k in range(n - 1):
        dst = land.at[lax.rem(gz + n - 1 - k, n)]
        pltpu.make_async_remote_copy(
            src_ref=dst, dst_ref=dst,
            send_sem=send_sem.at[k], recv_sem=recv_sem.at[k],
            device_id=ahead[k], device_id_type=MESH,
        ).wait_recv()
    out[...] = land[...]
    for move in moves:
        move.wait_send()


def gather(sizes, block, residual):
    nx, ny, nz = block
    n = sizes[2]
    vmem = pl.BlockSpec(memory_space=pltpu.VMEM)
    shape = (n,) + residual.shape
    mats = [(nx * ny, nx * ny), (nx * ny, 8 * (nx + ny)), (nz, nz), (128, nz)]
    return pl.pallas_call(
        functools.partial(gather_kernel, n, block),
        out_shape=[jax.ShapeDtypeStruct(shape, jnp.float32)]
        + [jax.ShapeDtypeStruct(m, jnp.bfloat16) for m in mats],
        in_specs=[vmem],
        out_specs=[vmem] * 5,
        scratch_shapes=[
            pltpu.VMEM(shape, jnp.float32),
            pltpu.SemaphoreType.DMA((n,)),
            pltpu.SemaphoreType.DMA((n,)),
        ],
        compiler_params=pltpu.CompilerParams(
            collective_id=1, has_side_effects=True, vmem_limit_bytes=16 * 2**20
        ),
        cost_estimate=pl.CostEstimate(flops=4 * 10**9, bytes_accessed=12 * 10**6, transcendentals=0),
        name="gather",
    )(residual)


def nn(a, b):
    return jnp.dot(a, b, preferred_element_type=jnp.float32)


def wave_kernel(
    sizes, ny, p0, p1, q5, q4, cf, src, m_in, m_face, m_z, m_end, grad, one, zero,
    fp, fq, lap, lq, qb, hl, zl, ys, send_sem, recv_sem,
):
    steps = src.shape[0]
    rows, nz = p0.shape
    nx = rows // ny
    faces_rows = (4 * ny, 4 * ny, 4 * nx, 4 * nx)
    me = [lax.axis_index(a) for a in AXES]
    has = []
    for d in range(3):
        has += [me[d] > 0, me[d] < sizes[d] - 1]
    to = []
    for d in range(3):
        to += [{AXES[d]: jnp.maximum(me[d] - 1, 0)}, {AXES[d]: jnp.minimum(me[d] + 1, sizes[d] - 1)}]

    barrier = pltpu.get_barrier_semaphore()
    for f in range(6):
        @pl.when(has[f])
        def _(f=f):
            pl.semaphore_signal(barrier, inc=1, device_id=to[f], device_id_type=MESH)
    pl.semaphore_wait(barrier, sum(h.astype(jnp.int32) for h in has))

    sub = lax.broadcasted_iota(jnp.int32, (8, nz), 0)
    lane = lax.broadcasted_iota(jnp.int32, (rows, 128), 1)

    def field(ch, r):
        if r == 0 and ch == 0:
            return p1
        return (fp, fq)[ch].at[r]

    def landing(ch, r, f):
        if f >= 4:
            return zl.at[ch, r, f - 4]
        return hl.at[ch, r, pl.ds(sum(faces_rows[:f]), faces_rows[f])]

    def copies(ch, r):
        f_ref = field(ch, r)
        srcs = [
            f_ref.at[pl.ds(0, 4 * ny)],
            f_ref.at[pl.ds(rows - 4 * ny, 4 * ny)],
            ys.at[ch, r, 0],
            ys.at[ch, r, 1],
            f_ref.at[pl.ds(0, rows), pl.ds(0, 128)],
            f_ref.at[pl.ds(0, rows), pl.ds(nz - 128, 128)],
        ]
        return [
            pltpu.make_async_remote_copy(
                src_ref=srcs[f],
                dst_ref=landing(ch, r, f ^ 1),
                send_sem=send_sem.at[ch, r, f],
                recv_sem=recv_sem.at[ch, r, f ^ 1],
                device_id=to[f],
                device_id_type=MESH,
            )
            for f in range(6)
        ]

    def send(ch, r):
        f_ref = field(ch, r)
        moves = copies(ch, r)
        for f in (0, 1, 4, 5):
            @pl.when(has[f])
            def _(f=f):
                moves[f].start()
        for i in range(nx // 2):
            lo, far = i * ny, (i + nx // 2) * ny
            a, b = f_ref[lo : lo + 8], f_ref[far : far + 8]
            ys[ch, r, 0, 8 * i : 8 * i + 8] = jnp.where(sub < 4, a, pltpu.roll(b, 4, 0))
            a, b = f_ref[lo + ny - 8 : lo + ny], f_ref[far + ny - 8 : far + ny]
            ys[ch, r, 1, 8 * i : 8 * i + 8] = jnp.where(sub >= 4, a, pltpu.roll(b, 4, 0))
        for f in (2, 3):
            @pl.when(has[f])
            def _(f=f):
                moves[f].start()

    def land(ch, r):
        for f in range(6):
            @pl.when(has[f])
            def _(f=f):
                dst = landing(ch, r, f)
                pltpu.make_async_remote_copy(
                    src_ref=dst, dst_ref=dst,
                    send_sem=send_sem.at[ch, r, f], recv_sem=recv_sem.at[ch, r, f],
                    device_id=to[f], device_id_type=MESH,
                ).wait_recv()

    def local(ch, r, out):
        f = field(ch, r)[...]
        acc = 0.0
        for part in split3(f):
            acc = acc + nn(m_in[...], part) + nn(part, m_z[...])
        out[...] = acc * (1.0 / 5040.0) + (3.0 * C[0]) * f

    def finish(ch, r, out):
        land(ch, r)
        acc = 0.0
        for part in split3(hl[ch, r]):
            acc = acc + nn(m_face[...], part)
        for part in split3(jnp.where(lane < 64, zl[ch, r, 1], zl[ch, r, 0])):
            acc = acc + nn(part, m_end[...])
        return out[...] + acc * (1.0 / 5040.0)

    send(0, 0)
    fq[0] = cf[...] * q4[...]
    send(1, 0)
    for f in range(6):
        @pl.when(jnp.logical_not(has[f]))
        def _(f=f):
            for ch in range(2):
                for r in range(steps):
                    dst = landing(ch, r, f)
                    dst[...] = jnp.zeros(dst.shape, jnp.float32)

    local(0, 0, lap.at[0])
    local(1, 0, lq)
    for r in range(steps):
        full = finish(0, r, lap.at[r])
        lap[r] = full
        if r + 1 < steps:
            old = p0 if r == 0 else field(0, r - 1)
            fp[r + 1] = 2.0 * field(0, r)[...] - old[...] + cf[...] * full
            send(0, r + 1)
            local(0, r + 1, lap.at[r + 1])

        full = finish(1, r, lq)
        now = q4 if r == 0 else qb.at[r - 1]
        old = q5 if r == 0 else (q4 if r == 1 else qb.at[r - 2])
        new = 2.0 * now[...] - old[...] + full + src[steps - 1 - r]
        if r + 1 < steps:
            qb[r] = new
            fq[r + 1] = cf[...] * new
            send(1, r + 1)
            local(1, r + 1, lq)
        else:
            zero[...] = new
            one[...] = now[...]
            total = q4[...] * lap[steps - 1]
            for n in range(1, steps):
                total = total + qb[n - 1] * lap[steps - 1 - n]
            grad[...] = total

    for ch in range(2):
        for r in range(steps):
            moves = copies(ch, r)
            for f in range(6):
                @pl.when(has[f])
                def _(f=f):
                    moves[f].wait_send()


def wave(sizes, p0, p1, q5, q4, cf, src, mats):
    nx, ny, nz = p0.shape
    steps = src.shape[0]
    rows = nx * ny
    f32 = jnp.float32
    flat = [a.reshape(rows, nz) for a in (p0, p1, q5, q4, cf)]
    outs = pl.pallas_call(
        functools.partial(wave_kernel, sizes, ny),
        out_shape=[jax.ShapeDtypeStruct((rows, nz), f32)] * 3,
        in_specs=[pl.BlockSpec(memory_space=pltpu.VMEM)] * 10,
        out_specs=[pl.BlockSpec(memory_space=pltpu.VMEM)] * 3,
        scratch_shapes=[
            pltpu.VMEM((steps, rows, nz), f32),
            pltpu.VMEM((steps, rows, nz), f32),
            pltpu.VMEM((steps, rows, nz), f32),
            pltpu.VMEM((rows, nz), f32),
            pltpu.VMEM((steps, rows, nz), f32),
            pltpu.VMEM((2, steps, 8 * (nx + ny), nz), f32),
            pltpu.VMEM((2, steps, 2, rows, 128), f32),
            pltpu.VMEM((2, steps, 2, 4 * nx, nz), f32),
            pltpu.SemaphoreType.DMA((2, steps, 6)),
            pltpu.SemaphoreType.DMA((2, steps, 6)),
        ],
        compiler_params=pltpu.CompilerParams(
            collective_id=0, has_side_effects=True, vmem_limit_bytes=32 * 2**20
        ),
        name="wave",
    )(*flat, src, *mats)
    return [o.reshape(nx, ny, nz) for o in outs]


CHUNKS = 5
HELD = 64
LANES = 128


def roll(v, shift, axis):
    shift = shift % v.shape[axis]
    return v if shift == 0 else pltpu.roll(v, shift, axis)


def near_counts(sizes, block, cells):
    near = []
    for d in range(2):
        at = lax.broadcasted_iota(jnp.int32, (sizes[d], cells[d].shape[1]), 0) * block[d]
        rel = cells[d] - at
        near.append(jnp.where((rel >= -4) & (rel < block[d] + 4), 1.0, 0.0))
    xy = jnp.concatenate([near[0][i : i + 1] * near[1] for i in range(sizes[0])], axis=0)
    counts = []
    for h in range(block[2] // LANES):
        at = lax.broadcasted_iota(jnp.int32, (sizes[2], cells[2].shape[1]), 0) * block[2] + h * LANES
        rel = cells[2] - at
        z = jnp.where((rel >= -4) & (rel < LANES + 4), 1.0, 0.0)
        counts.append(nt(xy.astype(jnp.bfloat16), z.astype(jnp.bfloat16)))
    return counts


def chunks_of(count):
    return jnp.floor((count + (HELD - 1.0)) * (1.0 / HELD))


def fused_kernel(
    sizes, ny,
    p0_h, p1_h, q5_h, q4_h, cf_h, res_h, cell_h, off_h, w_h, tr_h,
    grad, one, zero, flag,
    p0, p1, q5, q4, cf, cell, off, w, tr, load_sem,
    m_in, m_z, fp, fq, lap, base, ahead, qb, src, total,
    hx, hy, hz, ys, zs, send_sem, recv_sem,
    res, res_send, res_recv,
    sel_mic, table, tap_row, tap_col, tap_w, tap_res, hot, which,
):
    steps = res.shape[1]
    rows, nz = p1.shape
    nx = rows // ny
    block = (nx, ny, nz)
    tiles = rows // 8
    ytiles = ny // 8
    groups = tiles // 32
    halves = nz // LANES
    taps, mics = w.shape
    bf16, f32 = jnp.bfloat16, jnp.float32
    per = taps * HELD // LANES
    zero_slot = 2 * steps

    loads = [
        pltpu.make_async_copy(a, b, load_sem.at[i])
        for i, (a, b) in enumerate(
            [(p1_h, p1), (q4_h, q4), (cf_h, cf), (cell_h, cell), (off_h, off), (w_h, w), (tr_h, tr), (p0_h, p0), (q5_h, q5)]
        )
    ]
    for load in loads:
        load.start()

    me = [lax.axis_index(a) for a in AXES]
    has = []
    for d in range(3):
        has += [me[d] > 0, me[d] < sizes[d] - 1]
    to = []
    for d in range(3):
        to += [{AXES[d]: jnp.maximum(me[d] - 1, 0)}, {AXES[d]: jnp.minimum(me[d] + 1, sizes[d] - 1)}]
    peers = [{"gz": lax.rem(me[2] + k, sizes[2])} for k in range(1, sizes[2])]

    barrier = pltpu.get_barrier_semaphore()
    for f in range(4):
        @pl.when(has[f])
        def _(f=f):
            pl.semaphore_signal(barrier, inc=1, device_id=to[f], device_id_type=MESH)
    for peer in peers:
        pl.semaphore_signal(barrier, inc=1, device_id=peer, device_id_type=MESH)

    sub = lax.broadcasted_iota(jnp.int32, (8, nz), 0)
    lane = lax.broadcasted_iota(jnp.int32, (8, LANES), 1)
    lane_group = lane // 4

    def field(ch, r):
        if r == 0 and ch == 0:
            return p1
        return (fp, fq)[ch].at[r]

    def landing(ch, r, f, slot=None):
        slot = ch * steps + r if slot is None else slot
        return (hx, hy, hz)[f // 2].at[slot, f % 2]

    def copy(ch, r, f):
        f_ref = field(ch, r)
        if f == 0:
            face = f_ref.at[pl.ds(0, 4 * ny)]
        elif f == 1:
            face = f_ref.at[pl.ds(rows - 4 * ny, 4 * ny)]
        else:
            face = (ys, zs)[f // 2 - 1].at[ch, r, f % 2]
        return pltpu.make_async_remote_copy(
            src_ref=face,
            dst_ref=landing(ch, r, f ^ 1),
            send_sem=send_sem.at[ch, r, f],
            recv_sem=recv_sem.at[ch, r, f ^ 1],
            device_id=to[f],
            device_id_type=MESH,
        )

    def start(ch, r, faces):
        for f in faces:
            @pl.when(has[f])
            def _(f=f):
                copy(ch, r, f).start()

    def pack_y(ch, r):
        f_ref = field(ch, r)
        for i in range(nx // 2):
            lo, far = i * ny, (i + nx // 2) * ny
            a, b = f_ref[lo : lo + 8], f_ref[far : far + 8]
            ys[ch, r, 0, 8 * i : 8 * i + 8] = jnp.where(sub < 4, a, roll(b, 4, 0))
            a, b = f_ref[lo + ny - 8 : lo + ny], f_ref[far + ny - 8 : far + ny]
            ys[ch, r, 1, 8 * i : 8 * i + 8] = jnp.where(sub >= 4, a, roll(b, 4, 0))

    def pack_z(ch, r):
        f_ref = field(ch, r)
        for g in range(groups):
            low = jnp.zeros((8, LANES), f32)
            high = low
            for i in range(32):
                at = 8 * (32 * g + i)
                mine = lane_group == i
                low = jnp.where(mine, roll(f_ref[at : at + 8, 0:LANES], 4 * i, 1), low)
                high = jnp.where(mine, roll(f_ref[at : at + 8, nz - LANES : nz], 4 * i + 4, 1), high)
            zs[ch, r, 0, 8 * g : 8 * g + 8] = low
            zs[ch, r, 1, 8 * g : 8 * g + 8] = high

    def land(ch, r, faces):
        for f in faces:
            @pl.when(has[f])
            def _(f=f):
                dst = landing(ch, r, f)
                pltpu.make_async_remote_copy(
                    src_ref=dst, dst_ref=dst,
                    send_sem=send_sem.at[ch, r, f], recv_sem=recv_sem.at[ch, r, f],
                    device_id=to[f], device_id_type=MESH,
                ).wait_recv()

    def near_slot(ch, r, f):
        return jnp.where(has[f], ch * steps + r, zero_slot)

    def ramp(v, axis, at, upward):
        at = at % 4
        acc = 0.0
        for s in range(4):
            if upward:
                acc = acc + jnp.where(at + s < 4, C[4 - s], 0.0) * roll(v, -s, axis)
            else:
                acc = acc + jnp.where(at >= s, C[4 - s], 0.0) * roll(v, s, axis)
        return acc

    def local(ch, r):
        f = field(ch, r)[...]
        acc = 0.0
        for part in split3(f):
            acc = acc + nn(m_in[...], part) + nn(part, m_z[...])
        acc = acc * (1.0 / 5040.0) + (3.0 * C[0]) * f
        if ch == 0:
            if r + 1 < steps:
                old = p0 if r == 0 else field(0, r - 1)
                ahead[...] = 2.0 * f - old[...]
        else:
            now = q4 if r == 0 else (one if r == steps - 1 else qb.at[r - 1])
            old = q5 if r == 0 else (q4 if r == 1 else qb.at[r - 2])
            acc = acc + (2.0 * now[...] - old[...])
            if r > 0:
                acc = acc + src[steps - 1 - r]
        base[ch] = acc

    def finish(ch, r):
        land(ch, r, (4, 5))
        for side in range(2):
            ref = landing(ch, r, 4 + side, near_slot(ch, r, 4 + side))
            for g in range(groups):
                v = ramp(ref[8 * g : 8 * g + 8], 1, lane, side == 0)
                for i in range(32):
                    at = 8 * (32 * g + i)
                    if side == 0:
                        base[ch, at : at + 8, 0:LANES] += jnp.where(lane < 4, roll(v, -4 * i, 1), 0.0)
                    else:
                        base[ch, at : at + 8, nz - LANES : nz] += jnp.where(
                            lane >= LANES - 4, roll(v, -4 - 4 * i, 1), 0.0
                        )
        land(ch, r, (0, 1, 2, 3))
        x_ref = [landing(ch, r, f, near_slot(ch, r, f)) for f in (0, 1)]
        y_ref = [landing(ch, r, f, near_slot(ch, r, f)) for f in (2, 3)]
        for i in range(nx // 2):
            y_part = [ramp(y_ref[side][8 * i : 8 * i + 8], 0, sub, side == 0) for side in range(2)]
            for x in (i, i + nx // 2):
                for yt in range(ytiles):
                    at = x * ny + 8 * yt
                    t = base[ch, at : at + 8]
                    if x < 4:
                        for j in range(x, 4):
                            t = t + C[x + 4 - j] * x_ref[0][j * ny + 8 * yt : j * ny + 8 * yt + 8]
                    if x >= nx - 4:
                        for j in range(x - nx + 5):
                            t = t + C[nx + j - x] * x_ref[1][j * ny + 8 * yt : j * ny + 8 * yt + 8]
                    if yt == 0:
                        part = y_part[0] if x != i else roll(y_part[0], 4, 0)
                        t = t + jnp.where(sub < 4, part, 0.0)
                    if yt == ytiles - 1:
                        part = y_part[1] if x != i else roll(y_part[1], 4, 0)
                        t = t + jnp.where(sub >= 4, part, 0.0)
                    if ch == 0:
                        lap[r, at : at + 8] = t
                        if r + 1 < steps:
                            fp[r + 1, at : at + 8] = ahead[at : at + 8] + cf[at : at + 8] * t
                    else:
                        out = zero if r == steps - 1 else (one if r == steps - 2 else qb.at[r])
                        out[at : at + 8] = t
                        if r + 1 < steps:
                            fq[r + 1, at : at + 8] = cf[at : at + 8] * t

    def send(ch, r):
        pack_y(ch, r)
        start(ch, r, (2, 3))
        start(ch, r, (0, 1))
        pack_z(ch, r)
        start(ch, r, (4, 5))

    def select():
        cells = [cell[d : d + 1, :] for d in range(3)]
        rel = [cells[d] - me[d] * block[d] for d in range(3)]
        side = functools.reduce(jnp.logical_and, [(rel[d] >= -4) & (rel[d] < block[d] + 4) for d in range(2)])
        near = [
            jnp.where(side & (rel[2] >= h * LANES - 4) & (rel[2] < (h + 1) * LANES + 4), 1.0, 0.0)
            for h in range(halves)
        ]
        near = jnp.concatenate(near, axis=0)
        tri = (
            lax.broadcasted_iota(jnp.int32, (LANES, LANES), 0)
            < lax.broadcasted_iota(jnp.int32, (LANES, LANES), 1)
        )
        tri = jnp.where(tri, 1.0, 0.0).astype(bf16)
        count = jnp.zeros((halves, 1), f32)
        order = []
        for i in range(mics // LANES):
            part = near[:, i * LANES : (i + 1) * LANES]
            order.append(nn(part.astype(bf16), tri) + count)
            count = count + jnp.sum(part, axis=1, keepdims=True)
        order = jnp.concatenate(order, axis=1)
        full = chunks_of(count)
        first = [jnp.zeros((1, 1), f32)]
        for h in range(halves):
            first.append(first[-1] + full[h : h + 1])
        slot = [
            jnp.where(near[h : h + 1] > 0.5, order[h : h + 1] + HELD * first[h], -1.0) for h in range(halves)
        ]
        every = near_counts(sizes, block, cells)
        most = jnp.max(functools.reduce(jnp.add, [chunks_of(c) for c in every]))
        flag[0] = (most > CHUNKS).astype(jnp.int32)

        at = [rel[d] + off[d] for d in range(3)]
        inside = functools.reduce(jnp.logical_and, [(at[d] >= 0) & (at[d] < block[d]) for d in range(3)])
        table[0:taps, :] = jnp.where(inside, at[0] * ny + at[1], -1).astype(f32).astype(bf16)
        table[taps : 2 * taps, :] = jnp.where(inside, at[2], -1).astype(f32).astype(bf16)
        for i, part in enumerate(split3(w[...])):
            table[(2 + i) * taps : (3 + i) * taps, :] = part

        mic_id = lax.broadcasted_iota(jnp.int32, (1, mics), 1).astype(f32) + 1.0
        trace_mic = tr[...].astype(f32) + 1.0
        part_of = lax.broadcasted_iota(jnp.int32, (per, LANES), 1) // HELD

        def spread(v):
            out = v[0:per]
            for i in range(1, LANES // HELD):
                out = jnp.where(part_of == i, v[i * per : (i + 1) * per], out)
            return out

        def chunk(j, carry):
            slots = (lax.broadcasted_iota(jnp.int32, (HELD, mics), 0) + j * HELD).astype(f32)
            hit = functools.reduce(jnp.logical_or, [slots == slot[h] for h in range(halves)])
            mic = jnp.sum(jnp.where(hit, mic_id, 0.0), axis=1, keepdims=True)
            sel_mic[j] = jnp.where(trace_mic == mic, 1.0, 0.0).astype(bf16)
            tab = nt(table[...], jnp.where(hit, 1.0, 0.0).astype(bf16))
            tab = jnp.concatenate([tab] * (LANES // HELD), axis=1)
            mine = jnp.zeros((1, 1), f32)
            for h in range(1, halves):
                mine = mine + jnp.where(j.astype(f32) >= first[h], 1.0, 0.0)
            which[j] = jnp.broadcast_to(mine, (8, LANES))
            rows_j = spread(tab[0:taps])
            tap_col[j] = spread(tab[taps : 2 * taps]) - LANES * mine
            tap_w[j] = spread(
                tab[2 * taps : 3 * taps] + tab[3 * taps : 4 * taps] + tab[4 * taps : 5 * taps]
            )
            iota_row = lax.broadcasted_iota(jnp.int32, (rows, LANES), 0).astype(f32)
            for t in range(per):
                hot[j, :, t * LANES : (t + 1) * LANES] = jnp.where(
                    iota_row == rows_j[t : t + 1], 1.0, 0.0
                ).astype(bf16)
            return carry

        lax.fori_loop(0, CHUNKS, chunk, 0)

    def residuals():
        whole = jnp.concatenate([res[g] for g in range(sizes[2])], axis=1)
        parts = split3(whole)
        for j in range(CHUNKS):
            v = sum(nt(part, sel_mic[j]) for part in parts)
            tap_res[j] = jnp.concatenate([v] * (LANES // HELD), axis=1)

    def sources(first, count):
        levels = range(first, first + count)
        for n in levels:
            src[n] = jnp.zeros((rows, nz), f32)

        def chunk(j, carry):
            iota_col = lax.broadcasted_iota(jnp.int32, (LANES, LANES), 0).astype(f32)
            cols, weights, values = tap_col[j], tap_w[j], tap_res[j]
            right = [[[], []] for _ in levels]
            for t in range(per):
                col_hot = iota_col == cols[t : t + 1]
                for k, n in enumerate(levels):
                    amount = weights[t : t + 1] * values[n : n + 1]
                    hi = amount.astype(bf16).astype(f32)
                    right[k][0].append(jnp.where(col_hot, hi, 0.0).astype(bf16))
                    right[k][1].append(jnp.where(col_hot, amount - hi, 0.0).astype(bf16))
            acc = 0.0
            for s in range(2):
                both = jnp.concatenate([jnp.concatenate(right[k][s], axis=1) for k in range(count)], axis=0)
                acc = acc + nt(hot[j], both)
            mine = which[j, 0:1, :]
            for h in range(halves):
                for k, n in enumerate(levels):
                    src[n, :, h * LANES : (h + 1) * LANES] += jnp.where(
                        mine == float(h), acc[:, k * LANES : (k + 1) * LANES], 0.0
                    )
            return carry

        lax.fori_loop(0, CHUNKS, chunk, 0)

    def stencils():
        to_, at_ = [lax.broadcasted_iota(jnp.int32, m_in.shape, d) for d in range(2)]
        m_in[...] = cross(to_ // ny - at_ // ny, to_ % ny - at_ % ny).astype(bf16)
        at_, to_ = [lax.broadcasted_iota(jnp.int32, m_z.shape, d) for d in range(2)]
        m_z[...] = stencil(to_ - at_).astype(bf16)

    stencils()
    for ref in (hx, hy, hz):
        for side in range(2):
            ref[zero_slot, side] = jnp.zeros(ref.shape[2:], f32)
    loads[0].wait()
    pack_y(0, 0)
    pack_z(0, 0)
    loads[1].wait()
    loads[2].wait()
    fq[0] = cf[...] * q4[...]
    pack_y(1, 0)
    pack_z(1, 0)
    pl.semaphore_wait(barrier, sum(h.astype(jnp.int32) for h in has[:4]) + len(peers))
    res_moves = [
        pltpu.make_async_remote_copy(
            src_ref=res_h, dst_ref=res.at[me[2]],
            send_sem=res_send.at[k], recv_sem=res_recv.at[k],
            device_id=peers[k], device_id_type=MESH,
        )
        for k in range(len(peers))
    ]
    start(0, 0, (2, 3, 0, 1))
    for move in res_moves:
        move.start()
    start(1, 0, (2, 3, 0, 1))
    start(0, 0, (4, 5))
    start(1, 0, (4, 5))
    own = pltpu.make_async_copy(res_h, res.at[me[2]], load_sem.at[len(loads)])
    own.start()

    for load in loads[3:]:
        load.wait()
    select()
    local(0, 0)
    local(1, 0)
    own.wait()
    for k in range(len(peers)):
        dst = res.at[lax.rem(me[2] + sizes[2] - 1 - k, sizes[2])]
        pltpu.make_async_remote_copy(
            src_ref=dst, dst_ref=dst,
            send_sem=res_send.at[k], recv_sem=res_recv.at[k],
            device_id=peers[k], device_id_type=MESH,
        ).wait_recv()
    residuals()
    late = steps // 2
    sources(late, steps - late)
    base[1] += src[steps - 1]

    for r in range(steps):
        more = r + 1 < steps
        finish(0, r)
        if more:
            send(0, r + 1)
        finish(1, r)
        if more:
            send(1, r + 1)
            local(0, r + 1)
            if r == 0:
                sources(0, late)
            local(1, r + 1)
        if r == steps - 2:
            part = one[...] * lap[0]
            for n in range(1, steps - 1):
                part = part + qb[steps - 2 - n] * lap[n]
            total[...] = part
    grad[...] = total[...] + q4[...] * lap[steps - 1]

    for move in res_moves:
        move.wait_send()
    for ch in range(2):
        for r in range(steps):
            for f in range(6):
                @pl.when(has[f])
                def _(f=f):
                    copy(ch, r, f).wait_send()


def fused(sizes, p0, p1, q5, q4, cf, residual, receiver_cell, tap_offset, tap_weight, trace_receiver):
    nx, ny, nz = p0.shape
    steps = residual.shape[0]
    taps, mics = tap_weight.shape
    rows = nx * ny
    f32, bf16 = jnp.float32, jnp.bfloat16
    trace = trace_receiver.reshape(1, mics)
    flat = [a.reshape(rows, nz) for a in (p0, p1, q5, q4, cf)]
    plane = pltpu.VMEM((rows, nz), f32)
    slots = 2 * steps + 1
    packed = rows // 32
    return pl.pallas_call(
        functools.partial(fused_kernel, sizes, ny),
        out_shape=[jax.ShapeDtypeStruct((rows, nz), f32)] * 3 + [jax.ShapeDtypeStruct((1,), jnp.int32)],
        in_specs=[pl.BlockSpec(memory_space=pltpu.HBM)] * 10,
        out_specs=[pl.BlockSpec(memory_space=pltpu.VMEM)] * 3 + [pl.BlockSpec(memory_space=pltpu.SMEM)],
        scratch_shapes=[plane] * 5
        + [
            pltpu.VMEM(receiver_cell.shape, jnp.int32),
            pltpu.VMEM(tap_offset.shape, jnp.int32),
            pltpu.VMEM(tap_weight.shape, f32),
            pltpu.VMEM(trace.shape, jnp.int32),
            pltpu.SemaphoreType.DMA((10,)),
            pltpu.VMEM((rows, rows), bf16),
            pltpu.VMEM((nz, nz), bf16),
            pltpu.VMEM((steps, rows, nz), f32),
            pltpu.VMEM((steps, rows, nz), f32),
            pltpu.VMEM((steps, rows, nz), f32),
            pltpu.VMEM((2, rows, nz), f32),
            plane,
            pltpu.VMEM((steps - 2, rows, nz), f32),
            pltpu.VMEM((steps, rows, nz), f32),
            plane,
            pltpu.VMEM((slots, 2, 4 * ny, nz), f32),
            pltpu.VMEM((slots, 2, 4 * nx, nz), f32),
            pltpu.VMEM((slots, 2, packed, LANES), f32),
            pltpu.VMEM((2, steps, 2, 4 * nx, nz), f32),
            pltpu.VMEM((2, steps, 2, packed, LANES), f32),
            pltpu.SemaphoreType.DMA((2, steps, 6)),
            pltpu.SemaphoreType.DMA((2, steps, 6)),
            pltpu.VMEM((sizes[2],) + residual.shape, f32),
            pltpu.SemaphoreType.DMA((sizes[2],)),
            pltpu.SemaphoreType.DMA((sizes[2],)),
            pltpu.VMEM((CHUNKS, HELD, mics), bf16),
            pltpu.VMEM((5 * taps, mics), bf16),
            pltpu.VMEM((CHUNKS, taps * HELD // LANES, LANES), f32),
            pltpu.VMEM((CHUNKS, taps * HELD // LANES, LANES), f32),
            pltpu.VMEM((CHUNKS, taps * HELD // LANES, LANES), f32),
            pltpu.VMEM((CHUNKS, steps, LANES), f32),
            pltpu.VMEM((CHUNKS, rows, taps * HELD), bf16),
            pltpu.VMEM((CHUNKS, 8, LANES), f32),
        ],
        compiler_params=pltpu.CompilerParams(
            collective_id=2, has_side_effects=True, vmem_limit_bytes=40 * 2**20
        ),
        name="fused",
    )(*flat, residual, receiver_cell, tap_offset, tap_weight, trace)


def store_kernel(a, b, c, out_a, out_b, out_c, sem):
    moves = [
        pltpu.make_async_copy(s, d, sem.at[i])
        for i, (s, d) in enumerate(((a, out_a), (b, out_b), (c, out_c)))
    ]
    for move in moves:
        move.start()
    for move in moves:
        move.wait()


def store(block, *results):
    outs = pl.pallas_call(
        store_kernel,
        out_shape=[jax.ShapeDtypeStruct(a.shape, a.dtype) for a in results],
        in_specs=[pl.BlockSpec(memory_space=pltpu.VMEM)] * 3,
        out_specs=[pl.BlockSpec(memory_space=pltpu.HBM)] * 3,
        scratch_shapes=[pltpu.SemaphoreType.DMA((3,))],
        name="store",
    )(*results)
    return tuple(o.reshape(block) for o in outs)


def general(sizes, p0, p1, q5, q4, cf, residual, receiver_cell, tap_offset, tap_weight, trace_receiver):
    gathered, *mats = gather(sizes, p0.shape, residual)
    src = build_sources(p0.shape, gathered, receiver_cell, tap_offset, tap_weight, trace_receiver)
    return tuple(wave(sizes, p0, p1, q5, q4, cf, src, mats))


def shards(sizes, *args):
    grad, one, zero, flag = fused(sizes, *args)
    return lax.cond(
        flag[0] == 0,
        lambda results, args: store(args[0].shape, *results),
        lambda results, args: general(sizes, *args),
        (grad, one, zero),
        args,
    )


def solution(mesh):
    field = P(*AXES)
    return jax.shard_map(
        functools.partial(shards, tuple(mesh.shape[a] for a in AXES)),
        mesh=mesh,
        in_specs=(field,) * 5 + (P(None, "gz"), P(), P(), P(), P()),
        out_specs=(field,) * 3,
        check_vma=False,
    )
```

```python
import functools

import jax
import jax.numpy as jnp
from jax import lax
from jax.experimental import pallas as pl
from jax.experimental.pallas import tpu as pltpu
from jax.sharding import PartitionSpec as P

C = (-205.0 / 72.0, 8.0 / 5.0, -1.0 / 5.0, 8.0 / 315.0, -1.0 / 560.0)
AXES = ("gx", "gy", "gz")
MESH = pl.DeviceIdType.MESH


def split3(v):
    hi = v.astype(jnp.bfloat16)
    rest = v - hi.astype(jnp.float32)
    mid = rest.astype(jnp.bfloat16)
    lo = (rest - mid.astype(jnp.float32)).astype(jnp.bfloat16)
    return [hi, mid, lo]


def nt(a, b):
    return lax.dot_general(a, b, (((1,), (1,)), ((), ())), preferred_element_type=jnp.float32)


def source_kernel(block, res_ref, cell_ref, off_ref, w_ref, tr_ref, out_ref, table, info):
    bx, by, bz = block
    starts = [lax.axis_index(a) * n for a, n in zip(AXES, block)]
    taps, mics = w_ref.shape
    steps = res_ref.shape[1]
    rel = [cell_ref[d : d + 1, :] - starts[d] for d in range(3)]
    near = functools.reduce(
        jnp.logical_and, [(rel[d] >= -4) & (rel[d] < block[d] + 4) for d in range(3)]
    )
    at = [rel[d] + off_ref[d] for d in range(3)]
    inside = functools.reduce(
        jnp.logical_and, [(at[d] >= 0) & (at[d] < block[d]) for d in range(3)]
    )
    row = jnp.where(inside, at[0] * by + at[1], -1)
    col = jnp.where(inside, at[2], -1)
    table[0:taps, :] = row.astype(jnp.float32).astype(jnp.bfloat16)
    table[taps : 2 * taps, :] = col.astype(jnp.float32).astype(jnp.bfloat16)
    for i, part in enumerate(split3(w_ref[...])):
        table[(2 + i) * taps : (3 + i) * taps, :] = part
    near_f = jnp.where(near, 1.0, 0.0)
    lanes = 128
    blocks = mics // lanes
    tri = (
        lax.broadcasted_iota(jnp.int32, (lanes, lanes), 0)
        < lax.broadcasted_iota(jnp.int32, (lanes, lanes), 1)
    )
    tri = jnp.where(tri, 1.0, 0.0).astype(jnp.bfloat16)
    base = jnp.float32(0.0)
    for i in range(blocks):
        part = near_f[:, i * lanes : (i + 1) * lanes]
        before = jnp.dot(
            jnp.broadcast_to(part, (8, lanes)).astype(jnp.bfloat16),
            tri,
            preferred_element_type=jnp.float32,
        )[0:1]
        slot = jnp.where(part > 0.5, before + base, -1.0)
        info[0:1, i * lanes : (i + 1) * lanes] = slot
        base = base + jnp.sum(part)
    count = base.astype(jnp.int32)
    out_ref[...] = jnp.zeros_like(out_ref)
    share = 2
    held = lanes // share
    per = taps // share
    part_of = lax.broadcasted_iota(jnp.int32, (per, lanes), 1) // held

    def spread(v):
        out = v[0:per]
        for i in range(1, share):
            out = jnp.where(part_of == i, v[i * per : (i + 1) * per], out)
        return out

    def chunk(j, carry):
        slots = (lax.broadcasted_iota(jnp.int32, (held, mics), 0) + j * held).astype(jnp.float32)
        sel = jnp.where(slots == info[0:1, :], 1.0, 0.0)
        mic_id = lax.broadcasted_iota(jnp.int32, (1, mics), 1).astype(jnp.float32)
        mic = jnp.sum(sel * (mic_id + 1.0), axis=1, keepdims=True) - 1.0
        sel_r = jnp.where(tr_ref[...].astype(jnp.float32) == mic, 1.0, 0.0).astype(jnp.bfloat16)
        tab = jnp.concatenate([nt(table[...], sel.astype(jnp.bfloat16))] * share, axis=1)
        rows = spread(tab[0:taps])
        cols = spread(tab[taps : 2 * taps])
        weights = spread(
            tab[2 * taps : 3 * taps] + tab[3 * taps : 4 * taps] + tab[4 * taps : 5 * taps]
        )
        whole = jnp.concatenate([res_ref[g] for g in range(res_ref.shape[0])], axis=1)
        res = sum(nt(part, sel_r) for part in split3(whole))
        res = jnp.concatenate([res] * share, axis=1)
        iota_row = lax.broadcasted_iota(jnp.int32, (bx * by, lanes), 0).astype(jnp.float32)
        iota_col = lax.broadcasted_iota(jnp.int32, (bz, lanes), 0).astype(jnp.float32)
        group = 4
        for t0 in range(0, per, group):
            left, right = [[] for _ in range(steps)], []
            for t in range(t0, t0 + group):
                row_hot = iota_row == rows[t : t + 1]
                col_hot = jnp.where(iota_col == cols[t : t + 1], 1.0, 0.0).astype(jnp.bfloat16)
                right += [col_hot, col_hot]
                for n in range(steps):
                    amount = weights[t : t + 1] * res[n : n + 1]
                    hi = amount.astype(jnp.bfloat16).astype(jnp.float32)
                    lo = amount - hi
                    left[n].append(jnp.where(row_hot, hi, 0.0).astype(jnp.bfloat16))
                    left[n].append(jnp.where(row_hot, lo, 0.0).astype(jnp.bfloat16))
            right = jnp.concatenate(right, axis=1)
            for n in range(steps):
                out_ref[n] += nt(jnp.concatenate(left[n], axis=1), right)
        return carry

    lax.fori_loop(0, (count + held - 1) // held, chunk, 0)


def build_sources(block, residual, receiver_cell, tap_offset, tap_weight, trace_receiver):
    steps = residual.shape[1]
    taps, mics = tap_weight.shape
    return pl.pallas_call(
        functools.partial(source_kernel, block),
        out_shape=jax.ShapeDtypeStruct((steps, block[0] * block[1], block[2]), jnp.float32),
        in_specs=[pl.BlockSpec(memory_space=pltpu.VMEM)] * 5,
        out_specs=pl.BlockSpec(memory_space=pltpu.VMEM),
        scratch_shapes=[
            pltpu.VMEM((5 * taps, mics), jnp.bfloat16),
            pltpu.VMEM((8, mics), jnp.float32),
        ],
        compiler_params=pltpu.CompilerParams(vmem_limit_bytes=32 * 2**20),
        name="sources",
    )(residual, receiver_cell, tap_offset, tap_weight, trace_receiver)


def stencil(d):
    d = jnp.abs(d)
    return sum(jnp.where(d == k, float(round(5040 * C[k])), 0.0) for k in range(1, 5))


def cross(dx, dy):
    return jnp.where(dy == 0, stencil(dx), 0.0) + jnp.where(dx == 0, stencil(dy), 0.0)


def matrices(nx, ny, m_in, m_face, m_z, m_end):
    def grid(ref):
        return [lax.broadcasted_iota(jnp.int32, ref.shape, d) for d in range(2)]

    to, at = grid(m_in)
    m_in[...] = cross(to // ny - at // ny, to % ny - at % ny).astype(jnp.bfloat16)
    to, at = grid(m_face)
    x, y = to // ny, to % ny
    upper = at >= 4 * ny
    face = at - jnp.where(upper, 4 * ny, 0)
    in_x = cross(x - (face // ny + jnp.where(upper, nx, -4)), y - face % ny)
    pack = at - 8 * ny
    upper = pack >= 4 * nx
    pack = pack - jnp.where(upper, 4 * nx, 0)
    far = jnp.where(pack % 8 < 4, 0, 1) == jnp.where(upper, 1, 0)
    face_x = pack // 8 + jnp.where(far, nx // 2, 0)
    in_y = cross(x - face_x, y - (pack % 4 + jnp.where(upper, ny, -4)))
    m_face[...] = jnp.where(at < 8 * ny, in_x, in_y).astype(jnp.bfloat16)
    at, to = grid(m_z)
    m_z[...] = stencil(to - at).astype(jnp.bfloat16)
    at, to = grid(m_end)
    m_end[...] = stencil(to - jnp.where(at < 64, at + m_z.shape[0], at - 128)).astype(jnp.bfloat16)


def gather_kernel(n, block, res, out, m_in, m_face, m_z, m_end, land, send_sem, recv_sem):
    gz = lax.axis_index("gz")
    ahead = [{"gz": lax.rem(gz + k, n)} for k in range(1, n)]
    barrier = pltpu.get_barrier_semaphore()
    for other in ahead:
        pl.semaphore_signal(barrier, inc=1, device_id=other, device_id_type=MESH)
    pl.semaphore_wait(barrier, n - 1)
    moves = [
        pltpu.make_async_remote_copy(
            src_ref=res, dst_ref=land.at[gz],
            send_sem=send_sem.at[k], recv_sem=recv_sem.at[k],
            device_id=ahead[k], device_id_type=MESH,
        )
        for k in range(n - 1)
    ]
    for move in moves:
        move.start()
    matrices(block[0], block[1], m_in, m_face, m_z, m_end)
    land[gz] = res[...]
    for k in range(n - 1):
        dst = land.at[lax.rem(gz + n - 1 - k, n)]
        pltpu.make_async_remote_copy(
            src_ref=dst, dst_ref=dst,
            send_sem=send_sem.at[k], recv_sem=recv_sem.at[k],
            device_id=ahead[k], device_id_type=MESH,
        ).wait_recv()
    out[...] = land[...]
    for move in moves:
        move.wait_send()


def gather(sizes, block, residual):
    nx, ny, nz = block
    n = sizes[2]
    vmem = pl.BlockSpec(memory_space=pltpu.VMEM)
    shape = (n,) + residual.shape
    mats = [(nx * ny, nx * ny), (nx * ny, 8 * (nx + ny)), (nz, nz), (128, nz)]
    return pl.pallas_call(
        functools.partial(gather_kernel, n, block),
        out_shape=[jax.ShapeDtypeStruct(shape, jnp.float32)]
        + [jax.ShapeDtypeStruct(m, jnp.bfloat16) for m in mats],
        in_specs=[vmem],
        out_specs=[vmem] * 5,
        scratch_shapes=[
            pltpu.VMEM(shape, jnp.float32),
            pltpu.SemaphoreType.DMA((n,)),
            pltpu.SemaphoreType.DMA((n,)),
        ],
        compiler_params=pltpu.CompilerParams(
            collective_id=1, has_side_effects=True, vmem_limit_bytes=16 * 2**20
        ),
        cost_estimate=pl.CostEstimate(flops=4 * 10**9, bytes_accessed=12 * 10**6, transcendentals=0),
        name="gather",
    )(residual)


def nn(a, b):
    return jnp.dot(a, b, preferred_element_type=jnp.float32)


def wave_kernel(
    sizes, ny, p0, p1, q5, q4, cf, src, m_in, m_face, m_z, m_end, grad, one, zero,
    fp, fq, lap, lq, qb, hl, zl, ys, send_sem, recv_sem,
):
    steps = src.shape[0]
    rows, nz = p0.shape
    nx = rows // ny
    faces_rows = (4 * ny, 4 * ny, 4 * nx, 4 * nx)
    me = [lax.axis_index(a) for a in AXES]
    has = []
    for d in range(3):
        has += [me[d] > 0, me[d] < sizes[d] - 1]
    to = []
    for d in range(3):
        to += [{AXES[d]: jnp.maximum(me[d] - 1, 0)}, {AXES[d]: jnp.minimum(me[d] + 1, sizes[d] - 1)}]

    barrier = pltpu.get_barrier_semaphore()
    for f in range(6):
        @pl.when(has[f])
        def _(f=f):
            pl.semaphore_signal(barrier, inc=1, device_id=to[f], device_id_type=MESH)
    pl.semaphore_wait(barrier, sum(h.astype(jnp.int32) for h in has))

    sub = lax.broadcasted_iota(jnp.int32, (8, nz), 0)
    lane = lax.broadcasted_iota(jnp.int32, (rows, 128), 1)

    def field(ch, r):
        if r == 0 and ch == 0:
            return p1
        return (fp, fq)[ch].at[r]

    def landing(ch, r, f):
        if f >= 4:
            return zl.at[ch, r, f - 4]
        return hl.at[ch, r, pl.ds(sum(faces_rows[:f]), faces_rows[f])]

    def copies(ch, r):
        f_ref = field(ch, r)
        srcs = [
            f_ref.at[pl.ds(0, 4 * ny)],
            f_ref.at[pl.ds(rows - 4 * ny, 4 * ny)],
            ys.at[ch, r, 0],
            ys.at[ch, r, 1],
            f_ref.at[pl.ds(0, rows), pl.ds(0, 128)],
            f_ref.at[pl.ds(0, rows), pl.ds(nz - 128, 128)],
        ]
        return [
            pltpu.make_async_remote_copy(
                src_ref=srcs[f],
                dst_ref=landing(ch, r, f ^ 1),
                send_sem=send_sem.at[ch, r, f],
                recv_sem=recv_sem.at[ch, r, f ^ 1],
                device_id=to[f],
                device_id_type=MESH,
            )
            for f in range(6)
        ]

    def send(ch, r):
        f_ref = field(ch, r)
        moves = copies(ch, r)
        for f in (0, 1, 4, 5):
            @pl.when(has[f])
            def _(f=f):
                moves[f].start()
        for i in range(nx // 2):
            lo, far = i * ny, (i + nx // 2) * ny
            a, b = f_ref[lo : lo + 8], f_ref[far : far + 8]
            ys[ch, r, 0, 8 * i : 8 * i + 8] = jnp.where(sub < 4, a, pltpu.roll(b, 4, 0))
            a, b = f_ref[lo + ny - 8 : lo + ny], f_ref[far + ny - 8 : far + ny]
            ys[ch, r, 1, 8 * i : 8 * i + 8] = jnp.where(sub >= 4, a, pltpu.roll(b, 4, 0))
        for f in (2, 3):
            @pl.when(has[f])
            def _(f=f):
                moves[f].start()

    def land(ch, r):
        for f in range(6):
            @pl.when(has[f])
            def _(f=f):
                dst = landing(ch, r, f)
                pltpu.make_async_remote_copy(
                    src_ref=dst, dst_ref=dst,
                    send_sem=send_sem.at[ch, r, f], recv_sem=recv_sem.at[ch, r, f],
                    device_id=to[f], device_id_type=MESH,
                ).wait_recv()

    def local(ch, r, out):
        f = field(ch, r)[...]
        acc = 0.0
        for part in split3(f):
            acc = acc + nn(m_in[...], part) + nn(part, m_z[...])
        out[...] = acc * (1.0 / 5040.0) + (3.0 * C[0]) * f

    def finish(ch, r, out):
        land(ch, r)
        acc = 0.0
        for part in split3(hl[ch, r]):
            acc = acc + nn(m_face[...], part)
        for part in split3(jnp.where(lane < 64, zl[ch, r, 1], zl[ch, r, 0])):
            acc = acc + nn(part, m_end[...])
        return out[...] + acc * (1.0 / 5040.0)

    send(0, 0)
    fq[0] = cf[...] * q4[...]
    send(1, 0)
    for f in range(6):
        @pl.when(jnp.logical_not(has[f]))
        def _(f=f):
            for ch in range(2):
                for r in range(steps):
                    dst = landing(ch, r, f)
                    dst[...] = jnp.zeros(dst.shape, jnp.float32)

    local(0, 0, lap.at[0])
    local(1, 0, lq)
    for r in range(steps):
        full = finish(0, r, lap.at[r])
        lap[r] = full
        if r + 1 < steps:
            old = p0 if r == 0 else field(0, r - 1)
            fp[r + 1] = 2.0 * field(0, r)[...] - old[...] + cf[...] * full
            send(0, r + 1)
            local(0, r + 1, lap.at[r + 1])

        full = finish(1, r, lq)
        now = q4 if r == 0 else qb.at[r - 1]
        old = q5 if r == 0 else (q4 if r == 1 else qb.at[r - 2])
        new = 2.0 * now[...] - old[...] + full + src[steps - 1 - r]
        if r + 1 < steps:
            qb[r] = new
            fq[r + 1] = cf[...] * new
            send(1, r + 1)
            local(1, r + 1, lq)
        else:
            zero[...] = new
            one[...] = now[...]
            total = q4[...] * lap[steps - 1]
            for n in range(1, steps):
                total = total + qb[n - 1] * lap[steps - 1 - n]
            grad[...] = total

    for ch in range(2):
        for r in range(steps):
            moves = copies(ch, r)
            for f in range(6):
                @pl.when(has[f])
                def _(f=f):
                    moves[f].wait_send()


def wave(sizes, block, p0, p1, q5, q4, cf, src, mats):
    nx, ny, nz = block
    steps = src.shape[0]
    rows = nx * ny
    f32 = jnp.float32
    outs = pl.pallas_call(
        functools.partial(wave_kernel, sizes, ny),
        out_shape=[jax.ShapeDtypeStruct((rows, nz), f32)] * 3,
        in_specs=[pl.BlockSpec(memory_space=pltpu.VMEM)] * 10,
        out_specs=[pl.BlockSpec(memory_space=pltpu.VMEM)] * 3,
        scratch_shapes=[
            pltpu.VMEM((steps, rows, nz), f32),
            pltpu.VMEM((steps, rows, nz), f32),
            pltpu.VMEM((steps, rows, nz), f32),
            pltpu.VMEM((rows, nz), f32),
            pltpu.VMEM((steps, rows, nz), f32),
            pltpu.VMEM((2, steps, 8 * (nx + ny), nz), f32),
            pltpu.VMEM((2, steps, 2, rows, 128), f32),
            pltpu.VMEM((2, steps, 2, 4 * nx, nz), f32),
            pltpu.SemaphoreType.DMA((2, steps, 6)),
            pltpu.SemaphoreType.DMA((2, steps, 6)),
        ],
        compiler_params=pltpu.CompilerParams(
            collective_id=0, has_side_effects=True, vmem_limit_bytes=32 * 2**20
        ),
        name="wave",
    )(p0, p1, q5, q4, cf, src, *mats)
    return outs


CHUNKS = 5
HELD = 64
LANES = 128


def roll(v, shift, axis):
    shift = shift % v.shape[axis]
    return v if shift == 0 else pltpu.roll(v, shift, axis)


def near_counts(sizes, block, cells):
    near = []
    for d in range(2):
        at = lax.broadcasted_iota(jnp.int32, (sizes[d], cells[d].shape[1]), 0) * block[d]
        rel = cells[d] - at
        near.append(jnp.where((rel >= -4) & (rel < block[d] + 4), 1.0, 0.0))
    xy = jnp.concatenate([near[0][i : i + 1] * near[1] for i in range(sizes[0])], axis=0)
    counts = []
    for h in range(block[2] // LANES):
        at = lax.broadcasted_iota(jnp.int32, (sizes[2], cells[2].shape[1]), 0) * block[2] + h * LANES
        rel = cells[2] - at
        z = jnp.where((rel >= -4) & (rel < LANES + 4), 1.0, 0.0)
        counts.append(nt(xy.astype(jnp.bfloat16), z.astype(jnp.bfloat16)))
    return counts


def chunks_of(count):
    return jnp.floor((count + (HELD - 1.0)) * (1.0 / HELD))


def fused_kernel(
    sizes, ny,
    p0_h, p1_h, q5_h, q4_h, cf_h, res_h, cell_h, off_h, w_h, tr_h,
    grad, one, zero, p0, p1, q5, q4, cf, res_again, cell, off, w, tr, flag,
    load_sem,
    m_in, m_z, fp, fq, lap, base, ahead, qb, src, total,
    hx, hy, hz, ys, zs, send_sem, recv_sem,
    res, res_send, res_recv,
    sel_mic, table, tap_row, tap_col, tap_w, tap_res, hot, which,
):
    steps = res.shape[1]
    rows, nz = p1.shape
    nx = rows // ny
    block = (nx, ny, nz)
    tiles = rows // 8
    ytiles = ny // 8
    groups = tiles // 32
    halves = nz // LANES
    taps, mics = w.shape
    bf16, f32 = jnp.bfloat16, jnp.float32
    per = taps * HELD // LANES
    zero_slot = 2 * steps

    loads = [
        pltpu.make_async_copy(a, b, load_sem.at[i])
        for i, (a, b) in enumerate(
            [(p1_h, p1), (q4_h, q4), (cf_h, cf), (cell_h, cell), (off_h, off), (w_h, w), (tr_h, tr), (p0_h, p0), (q5_h, q5)]
        )
    ]
    for load in loads:
        load.start()

    me = [lax.axis_index(a) for a in AXES]
    has = []
    for d in range(3):
        has += [me[d] > 0, me[d] < sizes[d] - 1]
    to = []
    for d in range(3):
        to += [{AXES[d]: jnp.maximum(me[d] - 1, 0)}, {AXES[d]: jnp.minimum(me[d] + 1, sizes[d] - 1)}]
    peers = [{"gz": lax.rem(me[2] + k, sizes[2])} for k in range(1, sizes[2])]

    barrier = pltpu.get_barrier_semaphore()
    for f in range(4):
        @pl.when(has[f])
        def _(f=f):
            pl.semaphore_signal(barrier, inc=1, device_id=to[f], device_id_type=MESH)
    for peer in peers:
        pl.semaphore_signal(barrier, inc=1, device_id=peer, device_id_type=MESH)

    sub = lax.broadcasted_iota(jnp.int32, (8, nz), 0)
    lane = lax.broadcasted_iota(jnp.int32, (8, LANES), 1)
    lane_group = lane // 4

    def field(ch, r):
        if r == 0 and ch == 0:
            return p1
        return (fp, fq)[ch].at[r]

    def landing(ch, r, f, slot=None):
        slot = ch * steps + r if slot is None else slot
        return (hx, hy, hz)[f // 2].at[slot, f % 2]

    def copy(ch, r, f):
        f_ref = field(ch, r)
        if f == 0:
            face = f_ref.at[pl.ds(0, 4 * ny)]
        elif f == 1:
            face = f_ref.at[pl.ds(rows - 4 * ny, 4 * ny)]
        else:
            face = (ys, zs)[f // 2 - 1].at[ch, r, f % 2]
        return pltpu.make_async_remote_copy(
            src_ref=face,
            dst_ref=landing(ch, r, f ^ 1),
            send_sem=send_sem.at[ch, r, f],
            recv_sem=recv_sem.at[ch, r, f ^ 1],
            device_id=to[f],
            device_id_type=MESH,
        )

    def start(ch, r, faces):
        for f in faces:
            @pl.when(has[f])
            def _(f=f):
                copy(ch, r, f).start()

    def pack_y(ch, r):
        f_ref = field(ch, r)
        for i in range(nx // 2):
            lo, far = i * ny, (i + nx // 2) * ny
            a, b = f_ref[lo : lo + 8], f_ref[far : far + 8]
            ys[ch, r, 0, 8 * i : 8 * i + 8] = jnp.where(sub < 4, a, roll(b, 4, 0))
            a, b = f_ref[lo + ny - 8 : lo + ny], f_ref[far + ny - 8 : far + ny]
            ys[ch, r, 1, 8 * i : 8 * i + 8] = jnp.where(sub >= 4, a, roll(b, 4, 0))

    def pack_z(ch, r):
        f_ref = field(ch, r)
        for g in range(groups):
            low = jnp.zeros((8, LANES), f32)
            high = low
            for i in range(32):
                at = 8 * (32 * g + i)
                mine = lane_group == i
                low = jnp.where(mine, roll(f_ref[at : at + 8, 0:LANES], 4 * i, 1), low)
                high = jnp.where(mine, roll(f_ref[at : at + 8, nz - LANES : nz], 4 * i + 4, 1), high)
            zs[ch, r, 0, 8 * g : 8 * g + 8] = low
            zs[ch, r, 1, 8 * g : 8 * g + 8] = high

    def land(ch, r, faces):
        for f in faces:
            @pl.when(has[f])
            def _(f=f):
                dst = landing(ch, r, f)
                pltpu.make_async_remote_copy(
                    src_ref=dst, dst_ref=dst,
                    send_sem=send_sem.at[ch, r, f], recv_sem=recv_sem.at[ch, r, f],
                    device_id=to[f], device_id_type=MESH,
                ).wait_recv()

    def near_slot(ch, r, f):
        return jnp.where(has[f], ch * steps + r, zero_slot)

    def ramp(v, axis, at, upward):
        at = at % 4
        acc = 0.0
        for s in range(4):
            if upward:
                acc = acc + jnp.where(at + s < 4, C[4 - s], 0.0) * roll(v, -s, axis)
            else:
                acc = acc + jnp.where(at >= s, C[4 - s], 0.0) * roll(v, s, axis)
        return acc

    def local(ch, r):
        f = field(ch, r)[...]
        acc = 0.0
        for part in split3(f):
            acc = acc + nn(m_in[...], part) + nn(part, m_z[...])
        acc = acc * (1.0 / 5040.0) + (3.0 * C[0]) * f
        if ch == 0:
            if r + 1 < steps:
                old = p0 if r == 0 else field(0, r - 1)
                ahead[...] = 2.0 * f - old[...]
        else:
            now = q4 if r == 0 else (one if r == steps - 1 else qb.at[r - 1])
            old = q5 if r == 0 else (q4 if r == 1 else qb.at[r - 2])
            acc = acc + (2.0 * now[...] - old[...])
            if r > 0:
                acc = acc + src[steps - 1 - r].T
        base[ch] = acc

    def finish(ch, r):
        land(ch, r, (4, 5))
        for side in range(2):
            ref = landing(ch, r, 4 + side, near_slot(ch, r, 4 + side))
            for g in range(groups):
                v = ramp(ref[8 * g : 8 * g + 8], 1, lane, side == 0)
                for i in range(32):
                    at = 8 * (32 * g + i)
                    if side == 0:
                        base[ch, at : at + 8, 0:LANES] += jnp.where(lane < 4, roll(v, -4 * i, 1), 0.0)
                    else:
                        base[ch, at : at + 8, nz - LANES : nz] += jnp.where(
                            lane >= LANES - 4, roll(v, -4 - 4 * i, 1), 0.0
                        )
        land(ch, r, (0, 1, 2, 3))
        x_ref = [landing(ch, r, f, near_slot(ch, r, f)) for f in (0, 1)]
        y_ref = [landing(ch, r, f, near_slot(ch, r, f)) for f in (2, 3)]
        for i in range(nx // 2):
            y_part = [ramp(y_ref[side][8 * i : 8 * i + 8], 0, sub, side == 0) for side in range(2)]
            for x in (i, i + nx // 2):
                for yt in range(ytiles):
                    at = x * ny + 8 * yt
                    t = base[ch, at : at + 8]
                    if x < 4:
                        for j in range(x, 4):
                            t = t + C[x + 4 - j] * x_ref[0][j * ny + 8 * yt : j * ny + 8 * yt + 8]
                    if x >= nx - 4:
                        for j in range(x - nx + 5):
                            t = t + C[nx + j - x] * x_ref[1][j * ny + 8 * yt : j * ny + 8 * yt + 8]
                    if yt == 0:
                        part = y_part[0] if x != i else roll(y_part[0], 4, 0)
                        t = t + jnp.where(sub < 4, part, 0.0)
                    if yt == ytiles - 1:
                        part = y_part[1] if x != i else roll(y_part[1], 4, 0)
                        t = t + jnp.where(sub >= 4, part, 0.0)
                    if ch == 0:
                        lap[r, at : at + 8] = t
                        if r + 1 < steps:
                            fp[r + 1, at : at + 8] = ahead[at : at + 8] + cf[at : at + 8] * t
                    else:
                        out = zero if r == steps - 1 else (one if r == steps - 2 else qb.at[r])
                        out[at : at + 8] = t
                        if r + 1 < steps:
                            fq[r + 1, at : at + 8] = cf[at : at + 8] * t

    def send(ch, r):
        pack_y(ch, r)
        start(ch, r, (2, 3))
        start(ch, r, (0, 1))
        pack_z(ch, r)
        start(ch, r, (4, 5))

    def select():
        cells = [cell[d : d + 1, :] for d in range(3)]
        rel = [cells[d] - me[d] * block[d] for d in range(3)]
        side = functools.reduce(jnp.logical_and, [(rel[d] >= -4) & (rel[d] < block[d] + 4) for d in range(2)])
        near = [
            jnp.where(side & (rel[2] >= h * LANES - 4) & (rel[2] < (h + 1) * LANES + 4), 1.0, 0.0)
            for h in range(halves)
        ]
        near = jnp.concatenate(near, axis=0)
        tri = (
            lax.broadcasted_iota(jnp.int32, (LANES, LANES), 0)
            < lax.broadcasted_iota(jnp.int32, (LANES, LANES), 1)
        )
        tri = jnp.where(tri, 1.0, 0.0).astype(bf16)
        count = jnp.zeros((halves, 1), f32)
        order = []
        for i in range(mics // LANES):
            part = near[:, i * LANES : (i + 1) * LANES]
            order.append(nn(part.astype(bf16), tri) + count)
            count = count + jnp.sum(part, axis=1, keepdims=True)
        order = jnp.concatenate(order, axis=1)
        full = chunks_of(count)
        first = [jnp.zeros((1, 1), f32)]
        for h in range(halves):
            first.append(first[-1] + full[h : h + 1])
        slot = [
            jnp.where(near[h : h + 1] > 0.5, order[h : h + 1] + HELD * first[h], -1.0) for h in range(halves)
        ]
        every = near_counts(sizes, block, cells)
        most = jnp.max(functools.reduce(jnp.add, [chunks_of(c) for c in every]))
        flag[0] = (most > CHUNKS).astype(jnp.int32)

        at = [rel[d] + off[d] for d in range(3)]
        inside = functools.reduce(jnp.logical_and, [(at[d] >= 0) & (at[d] < block[d]) for d in range(3)])
        table[0:taps, :] = jnp.where(inside, at[0] * ny + at[1], -1).astype(f32).astype(bf16)
        table[taps : 2 * taps, :] = jnp.where(inside, at[2], -1).astype(f32).astype(bf16)
        for i, part in enumerate(split3(w[...])):
            table[(2 + i) * taps : (3 + i) * taps, :] = part

        mic_id = lax.broadcasted_iota(jnp.int32, (1, mics), 1).astype(f32) + 1.0
        trace_mic = tr[...].astype(f32) + 1.0
        part_of = lax.broadcasted_iota(jnp.int32, (per, LANES), 1) // HELD

        def spread(v):
            out = v[0:per]
            for i in range(1, LANES // HELD):
                out = jnp.where(part_of == i, v[i * per : (i + 1) * per], out)
            return out

        def chunk(j, carry):
            slots = (lax.broadcasted_iota(jnp.int32, (HELD, mics), 0) + j * HELD).astype(f32)
            hit = functools.reduce(jnp.logical_or, [slots == slot[h] for h in range(halves)])
            mic = jnp.sum(jnp.where(hit, mic_id, 0.0), axis=1, keepdims=True)
            sel_mic[j] = jnp.where(trace_mic == mic, 1.0, 0.0).astype(bf16)
            tab = nt(table[...], jnp.where(hit, 1.0, 0.0).astype(bf16))
            tab = jnp.concatenate([tab] * (LANES // HELD), axis=1)
            mine = jnp.zeros((1, 1), f32)
            for h in range(1, halves):
                mine = mine + jnp.where(j.astype(f32) >= first[h], 1.0, 0.0)
            which[j] = jnp.broadcast_to(mine, (8, LANES))
            rows_j = spread(tab[0:taps])
            tap_col[j] = spread(tab[taps : 2 * taps]) - LANES * mine
            tap_w[j] = spread(
                tab[2 * taps : 3 * taps] + tab[3 * taps : 4 * taps] + tab[4 * taps : 5 * taps]
            )
            iota_row = lax.broadcasted_iota(jnp.int32, (rows, LANES), 0).astype(f32)
            for t in range(per):
                hot[j, :, t * LANES : (t + 1) * LANES] = jnp.where(
                    iota_row == rows_j[t : t + 1], 1.0, 0.0
                ).astype(bf16)
            return carry

        lax.fori_loop(0, CHUNKS, chunk, 0, unroll=True)

    def residuals():
        whole = jnp.concatenate([res[g] for g in range(sizes[2])], axis=1)
        parts = split3(whole)
        for j in range(CHUNKS):
            v = sum(nt(part, sel_mic[j]) for part in parts)
            tap_res[j] = jnp.concatenate([v] * (LANES // HELD), axis=1)

    def sources(first, count):
        levels = range(first, first + count)
        for n in levels:
            src[n] = jnp.zeros((nz, rows), f32)

        def chunk(j, carry):
            iota_col = lax.broadcasted_iota(jnp.int32, (LANES, LANES), 0).astype(f32)
            cols, weights, values = tap_col[j], tap_w[j], tap_res[j]
            right = [[[], []] for _ in levels]
            for t in range(per):
                col_hot = iota_col == cols[t : t + 1]
                for k, n in enumerate(levels):
                    amount = weights[t : t + 1] * values[n : n + 1]
                    hi = amount.astype(bf16).astype(f32)
                    right[k][0].append(jnp.where(col_hot, hi, 0.0).astype(bf16))
                    right[k][1].append(jnp.where(col_hot, amount - hi, 0.0).astype(bf16))
            both = jnp.concatenate(
                [jnp.concatenate(right[k][s], axis=1) for s in range(2) for k in range(count)], axis=0
            )
            acc = nt(both, hot[j])
            acc = acc[0 : count * LANES] + acc[count * LANES : 2 * count * LANES]
            mine = which[j, 0:1, 0:1]
            for h in range(halves):
                for k, n in enumerate(levels):
                    src[n, h * LANES : (h + 1) * LANES, :] += jnp.where(
                        mine == float(h), acc[k * LANES : (k + 1) * LANES], 0.0
                    )
            return carry

        lax.fori_loop(0, CHUNKS, chunk, 0, unroll=True)

    def stencils():
        to_, at_ = [lax.broadcasted_iota(jnp.int32, m_in.shape, d) for d in range(2)]
        m_in[...] = cross(to_ // ny - at_ // ny, to_ % ny - at_ % ny).astype(bf16)
        at_, to_ = [lax.broadcasted_iota(jnp.int32, m_z.shape, d) for d in range(2)]
        m_z[...] = stencil(to_ - at_).astype(bf16)

    stencils()
    for ref in (hx, hy, hz):
        for side in range(2):
            ref[zero_slot, side] = jnp.zeros(ref.shape[2:], f32)
    loads[0].wait()
    pack_y(0, 0)
    pack_z(0, 0)
    loads[1].wait()
    loads[2].wait()
    fq[0] = cf[...] * q4[...]
    pack_y(1, 0)
    pack_z(1, 0)
    pl.semaphore_wait(barrier, sum(h.astype(jnp.int32) for h in has[:4]) + len(peers))
    res_moves = [
        pltpu.make_async_remote_copy(
            src_ref=res_h, dst_ref=res.at[me[2]],
            send_sem=res_send.at[k], recv_sem=res_recv.at[k],
            device_id=peers[k], device_id_type=MESH,
        )
        for k in range(len(peers))
    ]
    start(0, 0, (2, 3, 0, 1))
    for move in res_moves:
        move.start()
    start(1, 0, (2, 3, 0, 1))
    start(0, 0, (4, 5))
    start(1, 0, (4, 5))
    own = pltpu.make_async_copy(res_h, res.at[me[2]], load_sem.at[len(loads)])
    own.start()

    for load in loads[3:]:
        load.wait()
    select()
    local(0, 0)
    local(1, 0)
    own.wait()
    for k in range(len(peers)):
        dst = res.at[lax.rem(me[2] + sizes[2] - 1 - k, sizes[2])]
        pltpu.make_async_remote_copy(
            src_ref=dst, dst_ref=dst,
            send_sem=res_send.at[k], recv_sem=res_recv.at[k],
            device_id=peers[k], device_id_type=MESH,
        ).wait_recv()
    residuals()
    late = steps - 1
    sources(late, steps - late)
    base[1] += src[steps - 1].T

    for r in range(steps):
        more = r + 1 < steps
        finish(0, r)
        if more:
            send(0, r + 1)
        finish(1, r)
        if more:
            send(1, r + 1)
            local(0, r + 1)
            if r == 0:
                sources(0, late)
            local(1, r + 1)
        if r == steps - 2:
            part = one[...] * lap[0]
            for n in range(1, steps - 1):
                part = part + qb[steps - 2 - n] * lap[n]
            total[...] = part
    res_again[...] = res[me[2]]
    grad[...] = total[...] + q4[...] * lap[steps - 1]

    for move in res_moves:
        move.wait_send()
    for ch in range(2):
        for r in range(steps):
            for f in range(6):
                @pl.when(has[f])
                def _(f=f):
                    copy(ch, r, f).wait_send()


def fused(sizes, p0, p1, q5, q4, cf, residual, receiver_cell, tap_offset, tap_weight, trace_receiver):
    nx, ny, nz = p0.shape
    steps = residual.shape[0]
    taps, mics = tap_weight.shape
    rows = nx * ny
    f32, bf16 = jnp.float32, jnp.bfloat16
    flat = [a.reshape(rows, nz) for a in (p0, p1, q5, q4, cf)]
    plane = pltpu.VMEM((rows, nz), f32)
    slots = 2 * steps + 1
    packed = rows // 32
    return pl.pallas_call(
        functools.partial(fused_kernel, sizes, ny),
        out_shape=[jax.ShapeDtypeStruct((rows, nz), f32)] * 8
        + [
            jax.ShapeDtypeStruct(a.shape, a.dtype)
            for a in (residual, receiver_cell, tap_offset, tap_weight, trace_receiver)
        ]
        + [jax.ShapeDtypeStruct((1,), jnp.int32)],
        in_specs=[pl.BlockSpec(memory_space=pltpu.HBM)] * 10,
        out_specs=[pl.BlockSpec(memory_space=pltpu.VMEM)] * 13 + [pl.BlockSpec(memory_space=pltpu.SMEM)],
        scratch_shapes=[
            pltpu.SemaphoreType.DMA((10,)),
            pltpu.VMEM((rows, rows), bf16),
            pltpu.VMEM((nz, nz), bf16),
            pltpu.VMEM((steps, rows, nz), f32),
            pltpu.VMEM((steps, rows, nz), f32),
            pltpu.VMEM((steps, rows, nz), f32),
            pltpu.VMEM((2, rows, nz), f32),
            plane,
            pltpu.VMEM((steps - 2, rows, nz), f32),
            pltpu.VMEM((steps, nz, rows), f32),
            plane,
            pltpu.VMEM((slots, 2, 4 * ny, nz), f32),
            pltpu.VMEM((slots, 2, 4 * nx, nz), f32),
            pltpu.VMEM((slots, 2, packed, LANES), f32),
            pltpu.VMEM((2, steps, 2, 4 * nx, nz), f32),
            pltpu.VMEM((2, steps, 2, packed, LANES), f32),
            pltpu.SemaphoreType.DMA((2, steps, 6)),
            pltpu.SemaphoreType.DMA((2, steps, 6)),
            pltpu.VMEM((sizes[2],) + residual.shape, f32),
            pltpu.SemaphoreType.DMA((sizes[2],)),
            pltpu.SemaphoreType.DMA((sizes[2],)),
            pltpu.VMEM((CHUNKS, HELD, mics), bf16),
            pltpu.VMEM((5 * taps, mics), bf16),
            pltpu.VMEM((CHUNKS, taps * HELD // LANES, LANES), f32),
            pltpu.VMEM((CHUNKS, taps * HELD // LANES, LANES), f32),
            pltpu.VMEM((CHUNKS, taps * HELD // LANES, LANES), f32),
            pltpu.VMEM((CHUNKS, steps, LANES), f32),
            pltpu.VMEM((CHUNKS, rows, taps * HELD), bf16),
            pltpu.VMEM((CHUNKS, 8, LANES), f32),
        ],
        compiler_params=pltpu.CompilerParams(
            collective_id=2, has_side_effects=True, vmem_limit_bytes=56 * 2**20
        ),
        name="fused",
    )(*flat, residual, receiver_cell, tap_offset, tap_weight, trace_receiver)


def store_kernel(a, b, c, out_a, out_b, out_c, sem):
    moves = [
        pltpu.make_async_copy(s, d, sem.at[i])
        for i, (s, d) in enumerate(((a, out_a), (b, out_b), (c, out_c)))
    ]
    for move in moves:
        move.start()
    for move in moves:
        move.wait()


def store(*results):
    outs = pl.pallas_call(
        store_kernel,
        out_shape=[jax.ShapeDtypeStruct(a.shape, a.dtype) for a in results],
        in_specs=[pl.BlockSpec(memory_space=pltpu.VMEM)] * 3,
        out_specs=[pl.BlockSpec(memory_space=pltpu.HBM)] * 3,
        scratch_shapes=[pltpu.SemaphoreType.DMA((3,))],
        name="store",
    )(*results)
    return tuple(outs)


def general(sizes, block, p0, p1, q5, q4, cf, residual, receiver_cell, tap_offset, tap_weight, trace_receiver):
    gathered, *mats = gather(sizes, block, residual)
    src = build_sources(block, gathered, receiver_cell, tap_offset, tap_weight, trace_receiver)
    return store(*wave(sizes, block, p0, p1, q5, q4, cf, src, mats))


def shards(sizes, *args):
    block = args[0].shape
    *results, flag = fused(sizes, *args[:-1], args[-1].reshape(1, -1))
    outs = lax.cond(
        flag[0] == 0,
        lambda *held: store(*held[:3]),
        lambda *held: general(sizes, block, *held[3:]),
        *results,
    )
    return tuple(o.reshape(block) for o in outs)


def solution(mesh):
    field = P(*AXES)
    return jax.shard_map(
        functools.partial(shards, tuple(mesh.shape[a] for a in AXES)),
        mesh=mesh,
        in_specs=(field,) * 5 + (P(None, "gz"), P(), P(), P(), P()),
        out_specs=(field,) * 3,
        check_vma=False,
    )
```

```python
import functools

import jax
import jax.numpy as jnp
from jax import lax
from jax.experimental import pallas as pl
from jax.experimental.pallas import tpu as pltpu
from jax.sharding import PartitionSpec as P

C = (-205.0 / 72.0, 8.0 / 5.0, -1.0 / 5.0, 8.0 / 315.0, -1.0 / 560.0)
AXES = ("gx", "gy", "gz")
MESH = pl.DeviceIdType.MESH


def split3(v):
    hi = v.astype(jnp.bfloat16)
    rest = v - hi.astype(jnp.float32)
    mid = rest.astype(jnp.bfloat16)
    lo = (rest - mid.astype(jnp.float32)).astype(jnp.bfloat16)
    return [hi, mid, lo]


def nt(a, b):
    return lax.dot_general(a, b, (((1,), (1,)), ((), ())), preferred_element_type=jnp.float32)


def source_kernel(block, res_ref, cell_ref, off_ref, w_ref, tr_ref, out_ref, table, info):
    bx, by, bz = block
    starts = [lax.axis_index(a) * n for a, n in zip(AXES, block)]
    taps, mics = w_ref.shape
    steps = res_ref.shape[1]
    rel = [cell_ref[d : d + 1, :] - starts[d] for d in range(3)]
    near = functools.reduce(
        jnp.logical_and, [(rel[d] >= -4) & (rel[d] < block[d] + 4) for d in range(3)]
    )
    at = [rel[d] + off_ref[d] for d in range(3)]
    inside = functools.reduce(
        jnp.logical_and, [(at[d] >= 0) & (at[d] < block[d]) for d in range(3)]
    )
    row = jnp.where(inside, at[0] * by + at[1], -1)
    col = jnp.where(inside, at[2], -1)
    table[0:taps, :] = row.astype(jnp.float32).astype(jnp.bfloat16)
    table[taps : 2 * taps, :] = col.astype(jnp.float32).astype(jnp.bfloat16)
    for i, part in enumerate(split3(w_ref[...])):
        table[(2 + i) * taps : (3 + i) * taps, :] = part
    near_f = jnp.where(near, 1.0, 0.0)
    lanes = 128
    blocks = mics // lanes
    tri = (
        lax.broadcasted_iota(jnp.int32, (lanes, lanes), 0)
        < lax.broadcasted_iota(jnp.int32, (lanes, lanes), 1)
    )
    tri = jnp.where(tri, 1.0, 0.0).astype(jnp.bfloat16)
    base = jnp.float32(0.0)
    for i in range(blocks):
        part = near_f[:, i * lanes : (i + 1) * lanes]
        before = jnp.dot(
            jnp.broadcast_to(part, (8, lanes)).astype(jnp.bfloat16),
            tri,
            preferred_element_type=jnp.float32,
        )[0:1]
        slot = jnp.where(part > 0.5, before + base, -1.0)
        info[0:1, i * lanes : (i + 1) * lanes] = slot
        base = base + jnp.sum(part)
    count = base.astype(jnp.int32)
    out_ref[...] = jnp.zeros_like(out_ref)
    share = 2
    held = lanes // share
    per = taps // share
    part_of = lax.broadcasted_iota(jnp.int32, (per, lanes), 1) // held

    def spread(v):
        out = v[0:per]
        for i in range(1, share):
            out = jnp.where(part_of == i, v[i * per : (i + 1) * per], out)
        return out

    def chunk(j, carry):
        slots = (lax.broadcasted_iota(jnp.int32, (held, mics), 0) + j * held).astype(jnp.float32)
        sel = jnp.where(slots == info[0:1, :], 1.0, 0.0)
        mic_id = lax.broadcasted_iota(jnp.int32, (1, mics), 1).astype(jnp.float32)
        mic = jnp.sum(sel * (mic_id + 1.0), axis=1, keepdims=True) - 1.0
        sel_r = jnp.where(tr_ref[...].astype(jnp.float32) == mic, 1.0, 0.0).astype(jnp.bfloat16)
        tab = jnp.concatenate([nt(table[...], sel.astype(jnp.bfloat16))] * share, axis=1)
        rows = spread(tab[0:taps])
        cols = spread(tab[taps : 2 * taps])
        weights = spread(
            tab[2 * taps : 3 * taps] + tab[3 * taps : 4 * taps] + tab[4 * taps : 5 * taps]
        )
        whole = jnp.concatenate([res_ref[g] for g in range(res_ref.shape[0])], axis=1)
        res = sum(nt(part, sel_r) for part in split3(whole))
        res = jnp.concatenate([res] * share, axis=1)
        iota_row = lax.broadcasted_iota(jnp.int32, (bx * by, lanes), 0).astype(jnp.float32)
        iota_col = lax.broadcasted_iota(jnp.int32, (bz, lanes), 0).astype(jnp.float32)
        group = 4
        for t0 in range(0, per, group):
            left, right = [[] for _ in range(steps)], []
            for t in range(t0, t0 + group):
                row_hot = iota_row == rows[t : t + 1]
                col_hot = jnp.where(iota_col == cols[t : t + 1], 1.0, 0.0).astype(jnp.bfloat16)
                right += [col_hot, col_hot]
                for n in range(steps):
                    amount = weights[t : t + 1] * res[n : n + 1]
                    hi = amount.astype(jnp.bfloat16).astype(jnp.float32)
                    lo = amount - hi
                    left[n].append(jnp.where(row_hot, hi, 0.0).astype(jnp.bfloat16))
                    left[n].append(jnp.where(row_hot, lo, 0.0).astype(jnp.bfloat16))
            right = jnp.concatenate(right, axis=1)
            for n in range(steps):
                out_ref[n] += nt(jnp.concatenate(left[n], axis=1), right)
        return carry

    lax.fori_loop(0, (count + held - 1) // held, chunk, 0)


def build_sources(block, residual, receiver_cell, tap_offset, tap_weight, trace_receiver):
    steps = residual.shape[1]
    taps, mics = tap_weight.shape
    return pl.pallas_call(
        functools.partial(source_kernel, block),
        out_shape=jax.ShapeDtypeStruct((steps, block[0] * block[1], block[2]), jnp.float32),
        in_specs=[pl.BlockSpec(memory_space=pltpu.VMEM)] * 5,
        out_specs=pl.BlockSpec(memory_space=pltpu.VMEM),
        scratch_shapes=[
            pltpu.VMEM((5 * taps, mics), jnp.bfloat16),
            pltpu.VMEM((8, mics), jnp.float32),
        ],
        compiler_params=pltpu.CompilerParams(vmem_limit_bytes=32 * 2**20),
        name="sources",
    )(residual, receiver_cell, tap_offset, tap_weight, trace_receiver)


def stencil(d):
    d = jnp.abs(d)
    return sum(jnp.where(d == k, float(round(5040 * C[k])), 0.0) for k in range(1, 5))


def cross(dx, dy):
    return jnp.where(dy == 0, stencil(dx), 0.0) + jnp.where(dx == 0, stencil(dy), 0.0)


def matrices(nx, ny, m_in, m_face, m_z, m_end):
    def grid(ref):
        return [lax.broadcasted_iota(jnp.int32, ref.shape, d) for d in range(2)]

    to, at = grid(m_in)
    m_in[...] = cross(to // ny - at // ny, to % ny - at % ny).astype(jnp.bfloat16)
    to, at = grid(m_face)
    x, y = to // ny, to % ny
    upper = at >= 4 * ny
    face = at - jnp.where(upper, 4 * ny, 0)
    in_x = cross(x - (face // ny + jnp.where(upper, nx, -4)), y - face % ny)
    pack = at - 8 * ny
    upper = pack >= 4 * nx
    pack = pack - jnp.where(upper, 4 * nx, 0)
    far = jnp.where(pack % 8 < 4, 0, 1) == jnp.where(upper, 1, 0)
    face_x = pack // 8 + jnp.where(far, nx // 2, 0)
    in_y = cross(x - face_x, y - (pack % 4 + jnp.where(upper, ny, -4)))
    m_face[...] = jnp.where(at < 8 * ny, in_x, in_y).astype(jnp.bfloat16)
    at, to = grid(m_z)
    m_z[...] = stencil(to - at).astype(jnp.bfloat16)
    at, to = grid(m_end)
    m_end[...] = stencil(to - jnp.where(at < 64, at + m_z.shape[0], at - 128)).astype(jnp.bfloat16)


def gather_kernel(n, block, res, out, m_in, m_face, m_z, m_end, land, send_sem, recv_sem):
    gz = lax.axis_index("gz")
    ahead = [{"gz": lax.rem(gz + k, n)} for k in range(1, n)]
    barrier = pltpu.get_barrier_semaphore()
    for other in ahead:
        pl.semaphore_signal(barrier, inc=1, device_id=other, device_id_type=MESH)
    pl.semaphore_wait(barrier, n - 1)
    moves = [
        pltpu.make_async_remote_copy(
            src_ref=res, dst_ref=land.at[gz],
            send_sem=send_sem.at[k], recv_sem=recv_sem.at[k],
            device_id=ahead[k], device_id_type=MESH,
        )
        for k in range(n - 1)
    ]
    for move in moves:
        move.start()
    matrices(block[0], block[1], m_in, m_face, m_z, m_end)
    land[gz] = res[...]
    for k in range(n - 1):
        dst = land.at[lax.rem(gz + n - 1 - k, n)]
        pltpu.make_async_remote_copy(
            src_ref=dst, dst_ref=dst,
            send_sem=send_sem.at[k], recv_sem=recv_sem.at[k],
            device_id=ahead[k], device_id_type=MESH,
        ).wait_recv()
    out[...] = land[...]
    for move in moves:
        move.wait_send()


def gather(sizes, block, residual):
    nx, ny, nz = block
    n = sizes[2]
    vmem = pl.BlockSpec(memory_space=pltpu.VMEM)
    shape = (n,) + residual.shape
    mats = [(nx * ny, nx * ny), (nx * ny, 8 * (nx + ny)), (nz, nz), (128, nz)]
    return pl.pallas_call(
        functools.partial(gather_kernel, n, block),
        out_shape=[jax.ShapeDtypeStruct(shape, jnp.float32)]
        + [jax.ShapeDtypeStruct(m, jnp.bfloat16) for m in mats],
        in_specs=[vmem],
        out_specs=[vmem] * 5,
        scratch_shapes=[
            pltpu.VMEM(shape, jnp.float32),
            pltpu.SemaphoreType.DMA((n,)),
            pltpu.SemaphoreType.DMA((n,)),
        ],
        compiler_params=pltpu.CompilerParams(
            collective_id=1, has_side_effects=True, vmem_limit_bytes=16 * 2**20
        ),
        cost_estimate=pl.CostEstimate(flops=4 * 10**9, bytes_accessed=12 * 10**6, transcendentals=0),
        name="gather",
    )(residual)


def nn(a, b):
    return jnp.dot(a, b, preferred_element_type=jnp.float32)


def wave_kernel(
    sizes, ny, p0, p1, q5, q4, cf, src, m_in, m_face, m_z, m_end, grad, one, zero,
    fp, fq, lap, lq, qb, hl, zl, ys, send_sem, recv_sem,
):
    steps = src.shape[0]
    rows, nz = p0.shape
    nx = rows // ny
    faces_rows = (4 * ny, 4 * ny, 4 * nx, 4 * nx)
    me = [lax.axis_index(a) for a in AXES]
    has = []
    for d in range(3):
        has += [me[d] > 0, me[d] < sizes[d] - 1]
    to = []
    for d in range(3):
        to += [{AXES[d]: jnp.maximum(me[d] - 1, 0)}, {AXES[d]: jnp.minimum(me[d] + 1, sizes[d] - 1)}]

    barrier = pltpu.get_barrier_semaphore()
    for f in range(6):
        @pl.when(has[f])
        def _(f=f):
            pl.semaphore_signal(barrier, inc=1, device_id=to[f], device_id_type=MESH)
    pl.semaphore_wait(barrier, sum(h.astype(jnp.int32) for h in has))

    sub = lax.broadcasted_iota(jnp.int32, (8, nz), 0)
    lane = lax.broadcasted_iota(jnp.int32, (rows, 128), 1)

    def field(ch, r):
        if r == 0 and ch == 0:
            return p1
        return (fp, fq)[ch].at[r]

    def landing(ch, r, f):
        if f >= 4:
            return zl.at[ch, r, f - 4]
        return hl.at[ch, r, pl.ds(sum(faces_rows[:f]), faces_rows[f])]

    def copies(ch, r):
        f_ref = field(ch, r)
        srcs = [
            f_ref.at[pl.ds(0, 4 * ny)],
            f_ref.at[pl.ds(rows - 4 * ny, 4 * ny)],
            ys.at[ch, r, 0],
            ys.at[ch, r, 1],
            f_ref.at[pl.ds(0, rows), pl.ds(0, 128)],
            f_ref.at[pl.ds(0, rows), pl.ds(nz - 128, 128)],
        ]
        return [
            pltpu.make_async_remote_copy(
                src_ref=srcs[f],
                dst_ref=landing(ch, r, f ^ 1),
                send_sem=send_sem.at[ch, r, f],
                recv_sem=recv_sem.at[ch, r, f ^ 1],
                device_id=to[f],
                device_id_type=MESH,
            )
            for f in range(6)
        ]

    def send(ch, r):
        f_ref = field(ch, r)
        moves = copies(ch, r)
        for f in (0, 1, 4, 5):
            @pl.when(has[f])
            def _(f=f):
                moves[f].start()
        for i in range(nx // 2):
            lo, far = i * ny, (i + nx // 2) * ny
            a, b = f_ref[lo : lo + 8], f_ref[far : far + 8]
            ys[ch, r, 0, 8 * i : 8 * i + 8] = jnp.where(sub < 4, a, pltpu.roll(b, 4, 0))
            a, b = f_ref[lo + ny - 8 : lo + ny], f_ref[far + ny - 8 : far + ny]
            ys[ch, r, 1, 8 * i : 8 * i + 8] = jnp.where(sub >= 4, a, pltpu.roll(b, 4, 0))
        for f in (2, 3):
            @pl.when(has[f])
            def _(f=f):
                moves[f].start()

    def land(ch, r):
        for f in range(6):
            @pl.when(has[f])
            def _(f=f):
                dst = landing(ch, r, f)
                pltpu.make_async_remote_copy(
                    src_ref=dst, dst_ref=dst,
                    send_sem=send_sem.at[ch, r, f], recv_sem=recv_sem.at[ch, r, f],
                    device_id=to[f], device_id_type=MESH,
                ).wait_recv()

    def local(ch, r, out):
        f = field(ch, r)[...]
        acc = 0.0
        for part in split3(f):
            acc = acc + nn(m_in[...], part) + nn(part, m_z[...])
        out[...] = acc * (1.0 / 5040.0) + (3.0 * C[0]) * f

    def finish(ch, r, out):
        land(ch, r)
        acc = 0.0
        for part in split3(hl[ch, r]):
            acc = acc + nn(m_face[...], part)
        for part in split3(jnp.where(lane < 64, zl[ch, r, 1], zl[ch, r, 0])):
            acc = acc + nn(part, m_end[...])
        return out[...] + acc * (1.0 / 5040.0)

    send(0, 0)
    fq[0] = cf[...] * q4[...]
    send(1, 0)
    for f in range(6):
        @pl.when(jnp.logical_not(has[f]))
        def _(f=f):
            for ch in range(2):
                for r in range(steps):
                    dst = landing(ch, r, f)
                    dst[...] = jnp.zeros(dst.shape, jnp.float32)

    local(0, 0, lap.at[0])
    local(1, 0, lq)
    for r in range(steps):
        full = finish(0, r, lap.at[r])
        lap[r] = full
        if r + 1 < steps:
            old = p0 if r == 0 else field(0, r - 1)
            fp[r + 1] = 2.0 * field(0, r)[...] - old[...] + cf[...] * full
            send(0, r + 1)
            local(0, r + 1, lap.at[r + 1])

        full = finish(1, r, lq)
        now = q4 if r == 0 else qb.at[r - 1]
        old = q5 if r == 0 else (q4 if r == 1 else qb.at[r - 2])
        new = 2.0 * now[...] - old[...] + full + src[steps - 1 - r]
        if r + 1 < steps:
            qb[r] = new
            fq[r + 1] = cf[...] * new
            send(1, r + 1)
            local(1, r + 1, lq)
        else:
            zero[...] = new
            one[...] = now[...]
            total = q4[...] * lap[steps - 1]
            for n in range(1, steps):
                total = total + qb[n - 1] * lap[steps - 1 - n]
            grad[...] = total

    for ch in range(2):
        for r in range(steps):
            moves = copies(ch, r)
            for f in range(6):
                @pl.when(has[f])
                def _(f=f):
                    moves[f].wait_send()


def wave(sizes, block, p0, p1, q5, q4, cf, src, mats):
    nx, ny, nz = block
    steps = src.shape[0]
    rows = nx * ny
    f32 = jnp.float32
    outs = pl.pallas_call(
        functools.partial(wave_kernel, sizes, ny),
        out_shape=[jax.ShapeDtypeStruct((rows, nz), f32)] * 3,
        in_specs=[pl.BlockSpec(memory_space=pltpu.VMEM)] * 10,
        out_specs=[pl.BlockSpec(memory_space=pltpu.VMEM)] * 3,
        scratch_shapes=[
            pltpu.VMEM((steps, rows, nz), f32),
            pltpu.VMEM((steps, rows, nz), f32),
            pltpu.VMEM((steps, rows, nz), f32),
            pltpu.VMEM((rows, nz), f32),
            pltpu.VMEM((steps, rows, nz), f32),
            pltpu.VMEM((2, steps, 8 * (nx + ny), nz), f32),
            pltpu.VMEM((2, steps, 2, rows, 128), f32),
            pltpu.VMEM((2, steps, 2, 4 * nx, nz), f32),
            pltpu.SemaphoreType.DMA((2, steps, 6)),
            pltpu.SemaphoreType.DMA((2, steps, 6)),
        ],
        compiler_params=pltpu.CompilerParams(
            collective_id=0, has_side_effects=True, vmem_limit_bytes=32 * 2**20
        ),
        name="wave",
    )(p0, p1, q5, q4, cf, src, *mats)
    return outs


CHUNKS = 5
HELD = 64
LANES = 128


def roll(v, shift, axis):
    shift = shift % v.shape[axis]
    return v if shift == 0 else pltpu.roll(v, shift, axis)


def near_counts(sizes, block, cells):
    near = []
    for d in range(2):
        at = lax.broadcasted_iota(jnp.int32, (sizes[d], cells[d].shape[1]), 0) * block[d]
        rel = cells[d] - at
        near.append(jnp.where((rel >= -4) & (rel < block[d] + 4), 1.0, 0.0))
    xy = jnp.concatenate([near[0][i : i + 1] * near[1] for i in range(sizes[0])], axis=0)
    counts = []
    for h in range(block[2] // LANES):
        at = lax.broadcasted_iota(jnp.int32, (sizes[2], cells[2].shape[1]), 0) * block[2] + h * LANES
        rel = cells[2] - at
        z = jnp.where((rel >= -4) & (rel < LANES + 4), 1.0, 0.0)
        counts.append(nt(xy.astype(jnp.bfloat16), z.astype(jnp.bfloat16)))
    return counts


def chunks_of(count):
    return jnp.floor((count + (HELD - 1.0)) * (1.0 / HELD))


def fused_kernel(
    sizes, ny,
    p0_h, p1_h, q5_h, q4_h, cf_h, res_h, cell_h, off_h, w_h, tr_h,
    grad, one, zero, p0, p1, q5, q4, cf, res_again, cell, off, w, tr, flag,
    load_sem,
    m_in, m_z, fp, fq, lap, base, ahead, qb, src, total,
    hx, hy, hz, ys, zs, send_sem, recv_sem,
    res, res_send, res_recv,
    sel_mic, table, tap_row, tap_col, tap_w, tap_res, hot, which,
):
    steps = res.shape[1]
    rows, nz = p1.shape
    nx = rows // ny
    block = (nx, ny, nz)
    tiles = rows // 8
    ytiles = ny // 8
    groups = tiles // 32
    halves = nz // LANES
    taps, mics = w.shape
    bf16, f32 = jnp.bfloat16, jnp.float32
    per = taps * HELD // LANES
    zero_slot = 2 * steps

    loads = [
        pltpu.make_async_copy(a, b, load_sem.at[i])
        for i, (a, b) in enumerate(
            [(p1_h, p1), (q4_h, q4), (cf_h, cf), (cell_h, cell), (off_h, off), (w_h, w), (tr_h, tr), (p0_h, p0), (q5_h, q5)]
        )
    ]
    for load in loads:
        load.start()

    me = [lax.axis_index(a) for a in AXES]
    has = []
    for d in range(3):
        has += [me[d] > 0, me[d] < sizes[d] - 1]
    to = []
    for d in range(3):
        to += [{AXES[d]: jnp.maximum(me[d] - 1, 0)}, {AXES[d]: jnp.minimum(me[d] + 1, sizes[d] - 1)}]
    peers = [{"gz": lax.rem(me[2] + k, sizes[2])} for k in range(1, sizes[2])]

    barrier = pltpu.get_barrier_semaphore()
    for f in range(4):
        @pl.when(has[f])
        def _(f=f):
            pl.semaphore_signal(barrier, inc=1, device_id=to[f], device_id_type=MESH)
    for peer in peers:
        pl.semaphore_signal(barrier, inc=1, device_id=peer, device_id_type=MESH)

    sub = lax.broadcasted_iota(jnp.int32, (8, nz), 0)
    lane = lax.broadcasted_iota(jnp.int32, (8, LANES), 1)
    lane_group = lane // 4

    def field(ch, r):
        if r == 0 and ch == 0:
            return p1
        return (fp, fq)[ch].at[r]

    def landing(ch, r, f, slot=None):
        slot = ch * steps + r if slot is None else slot
        return (hx, hy, hz)[f // 2].at[slot, f % 2]

    def copy(ch, r, f):
        f_ref = field(ch, r)
        if f == 0:
            face = f_ref.at[pl.ds(0, 4 * ny)]
        elif f == 1:
            face = f_ref.at[pl.ds(rows - 4 * ny, 4 * ny)]
        else:
            face = (ys, zs)[f // 2 - 1].at[ch, r, f % 2]
        return pltpu.make_async_remote_copy(
            src_ref=face,
            dst_ref=landing(ch, r, f ^ 1),
            send_sem=send_sem.at[ch, r, f],
            recv_sem=recv_sem.at[ch, r, f ^ 1],
            device_id=to[f],
            device_id_type=MESH,
        )

    def start(ch, r, faces):
        for f in faces:
            @pl.when(has[f])
            def _(f=f):
                copy(ch, r, f).start()

    def pack_y(ch, r):
        f_ref = field(ch, r)
        for i in range(nx // 2):
            lo, far = i * ny, (i + nx // 2) * ny
            a, b = f_ref[lo : lo + 8], f_ref[far : far + 8]
            ys[ch, r, 0, 8 * i : 8 * i + 8] = jnp.where(sub < 4, a, roll(b, 4, 0))
            a, b = f_ref[lo + ny - 8 : lo + ny], f_ref[far + ny - 8 : far + ny]
            ys[ch, r, 1, 8 * i : 8 * i + 8] = jnp.where(sub >= 4, a, roll(b, 4, 0))

    def pack_z(ch, r):
        f_ref = field(ch, r)
        for g in range(groups):
            low = jnp.zeros((8, LANES), f32)
            high = low
            for i in range(32):
                at = 8 * (32 * g + i)
                mine = lane_group == i
                low = jnp.where(mine, roll(f_ref[at : at + 8, 0:LANES], 4 * i, 1), low)
                high = jnp.where(mine, roll(f_ref[at : at + 8, nz - LANES : nz], 4 * i + 4, 1), high)
            zs[ch, r, 0, 8 * g : 8 * g + 8] = low
            zs[ch, r, 1, 8 * g : 8 * g + 8] = high

    def land(ch, r, faces):
        for f in faces:
            @pl.when(has[f])
            def _(f=f):
                dst = landing(ch, r, f)
                pltpu.make_async_remote_copy(
                    src_ref=dst, dst_ref=dst,
                    send_sem=send_sem.at[ch, r, f], recv_sem=recv_sem.at[ch, r, f],
                    device_id=to[f], device_id_type=MESH,
                ).wait_recv()

    def near_slot(ch, r, f):
        return jnp.where(has[f], ch * steps + r, zero_slot)

    def ramp(v, axis, at, upward):
        at = at % 4
        acc = 0.0
        for s in range(4):
            if upward:
                acc = acc + jnp.where(at + s < 4, C[4 - s], 0.0) * roll(v, -s, axis)
            else:
                acc = acc + jnp.where(at >= s, C[4 - s], 0.0) * roll(v, s, axis)
        return acc

    def local(ch, r):
        f = field(ch, r)[...]
        acc = 0.0
        for part in split3(f):
            acc = acc + nn(m_in[...], part) + nn(part, m_z[...])
        acc = acc * (1.0 / 5040.0) + (3.0 * C[0]) * f
        if ch == 0:
            if r + 1 < steps:
                old = p0 if r == 0 else field(0, r - 1)
                ahead[...] = 2.0 * f - old[...]
        else:
            now = q4 if r == 0 else (one if r == steps - 1 else qb.at[r - 1])
            old = q5 if r == 0 else (q4 if r == 1 else qb.at[r - 2])
            acc = acc + (2.0 * now[...] - old[...])
            if r > 0:
                acc = acc + src[steps - 1 - r].T
        base[ch] = acc

    def finish(ch, r):
        land(ch, r, (4, 5))
        for side in range(2):
            ref = landing(ch, r, 4 + side, near_slot(ch, r, 4 + side))
            for g in range(groups):
                v = ramp(ref[8 * g : 8 * g + 8], 1, lane, side == 0)
                for i in range(32):
                    at = 8 * (32 * g + i)
                    if side == 0:
                        base[ch, at : at + 8, 0:LANES] += jnp.where(lane < 4, roll(v, -4 * i, 1), 0.0)
                    else:
                        base[ch, at : at + 8, nz - LANES : nz] += jnp.where(
                            lane >= LANES - 4, roll(v, -4 - 4 * i, 1), 0.0
                        )
        land(ch, r, (0, 1, 2, 3))
        x_ref = [landing(ch, r, f, near_slot(ch, r, f)) for f in (0, 1)]
        y_ref = [landing(ch, r, f, near_slot(ch, r, f)) for f in (2, 3)]
        for i in range(nx // 2):
            y_part = [ramp(y_ref[side][8 * i : 8 * i + 8], 0, sub, side == 0) for side in range(2)]
            for x in (i, i + nx // 2):
                for yt in range(ytiles):
                    at = x * ny + 8 * yt
                    t = base[ch, at : at + 8]
                    if x < 4:
                        for j in range(x, 4):
                            t = t + C[x + 4 - j] * x_ref[0][j * ny + 8 * yt : j * ny + 8 * yt + 8]
                    if x >= nx - 4:
                        for j in range(x - nx + 5):
                            t = t + C[nx + j - x] * x_ref[1][j * ny + 8 * yt : j * ny + 8 * yt + 8]
                    if yt == 0:
                        part = y_part[0] if x != i else roll(y_part[0], 4, 0)
                        t = t + jnp.where(sub < 4, part, 0.0)
                    if yt == ytiles - 1:
                        part = y_part[1] if x != i else roll(y_part[1], 4, 0)
                        t = t + jnp.where(sub >= 4, part, 0.0)
                    if ch == 0:
                        lap[r, at : at + 8] = t
                        if r + 1 < steps:
                            fp[r + 1, at : at + 8] = ahead[at : at + 8] + cf[at : at + 8] * t
                    else:
                        out = zero if r == steps - 1 else (one if r == steps - 2 else qb.at[r])
                        out[at : at + 8] = t
                        if r + 1 < steps:
                            fq[r + 1, at : at + 8] = cf[at : at + 8] * t

    def send(ch, r):
        pack_y(ch, r)
        start(ch, r, (2, 3))
        start(ch, r, (0, 1))
        pack_z(ch, r)
        start(ch, r, (4, 5))

    def select():
        cells = [cell[d : d + 1, :] for d in range(3)]
        rel = [cells[d] - me[d] * block[d] for d in range(3)]
        side = functools.reduce(jnp.logical_and, [(rel[d] >= -4) & (rel[d] < block[d] + 4) for d in range(2)])
        near = [
            jnp.where(side & (rel[2] >= h * LANES - 4) & (rel[2] < (h + 1) * LANES + 4), 1.0, 0.0)
            for h in range(halves)
        ]
        near = jnp.concatenate(near, axis=0)
        tri = (
            lax.broadcasted_iota(jnp.int32, (LANES, LANES), 0)
            < lax.broadcasted_iota(jnp.int32, (LANES, LANES), 1)
        )
        tri = jnp.where(tri, 1.0, 0.0).astype(bf16)
        count = jnp.zeros((halves, 1), f32)
        order = []
        for i in range(mics // LANES):
            part = near[:, i * LANES : (i + 1) * LANES]
            order.append(nn(part.astype(bf16), tri) + count)
            count = count + jnp.sum(part, axis=1, keepdims=True)
        order = jnp.concatenate(order, axis=1)
        full = chunks_of(count)
        first = [jnp.zeros((1, 1), f32)]
        for h in range(halves):
            first.append(first[-1] + full[h : h + 1])
        slot = [
            jnp.where(near[h : h + 1] > 0.5, order[h : h + 1] + HELD * first[h], -1.0) for h in range(halves)
        ]
        every = near_counts(sizes, block, cells)
        most = jnp.max(functools.reduce(jnp.add, [chunks_of(c) for c in every]))
        flag[0] = (most > CHUNKS).astype(jnp.int32)

        at = [rel[d] + off[d] for d in range(3)]
        inside = functools.reduce(jnp.logical_and, [(at[d] >= 0) & (at[d] < block[d]) for d in range(3)])
        table[0:taps, :] = jnp.where(inside, at[0] * ny + at[1], -1).astype(f32).astype(bf16)
        table[taps : 2 * taps, :] = jnp.where(inside, at[2], -1).astype(f32).astype(bf16)
        for i, part in enumerate(split3(w[...])):
            table[(2 + i) * taps : (3 + i) * taps, :] = part

        mic_id = lax.broadcasted_iota(jnp.int32, (1, mics), 1).astype(f32) + 1.0
        trace_mic = tr[...].astype(f32) + 1.0
        part_of = lax.broadcasted_iota(jnp.int32, (per, LANES), 1) // HELD

        def spread(v):
            out = v[0:per]
            for i in range(1, LANES // HELD):
                out = jnp.where(part_of == i, v[i * per : (i + 1) * per], out)
            return out

        def chunk(j, carry):
            slots = (lax.broadcasted_iota(jnp.int32, (HELD, mics), 0) + j * HELD).astype(f32)
            hit = functools.reduce(jnp.logical_or, [slots == slot[h] for h in range(halves)])
            mic = jnp.sum(jnp.where(hit, mic_id, 0.0), axis=1, keepdims=True)
            sel_mic[j] = jnp.where(trace_mic == mic, 1.0, 0.0).astype(bf16)
            tab = nt(table[...], jnp.where(hit, 1.0, 0.0).astype(bf16))
            tab = jnp.concatenate([tab] * (LANES // HELD), axis=1)
            mine = jnp.zeros((1, 1), f32)
            for h in range(1, halves):
                mine = mine + jnp.where(j.astype(f32) >= first[h], 1.0, 0.0)
            which[j] = jnp.broadcast_to(mine, (8, LANES))
            rows_j = spread(tab[0:taps])
            tap_col[j] = spread(tab[taps : 2 * taps]) - LANES * mine
            tap_w[j] = spread(
                tab[2 * taps : 3 * taps] + tab[3 * taps : 4 * taps] + tab[4 * taps : 5 * taps]
            )
            iota_row = lax.broadcasted_iota(jnp.int32, (rows, LANES), 0).astype(f32)
            for t in range(per):
                hot[j, :, t * LANES : (t + 1) * LANES] = jnp.where(
                    iota_row == rows_j[t : t + 1], 1.0, 0.0
                ).astype(bf16)
            return carry

        lax.fori_loop(0, CHUNKS, chunk, 0, unroll=True)

    def residuals():
        whole = jnp.concatenate([res[g] for g in range(sizes[2])], axis=1)
        parts = split3(whole)
        for j in range(CHUNKS):
            v = sum(nt(part, sel_mic[j]) for part in parts)
            tap_res[j] = jnp.concatenate([v] * (LANES // HELD), axis=1)

    def sources(first, count):
        levels = range(first, first + count)
        for n in levels:
            src[n] = jnp.zeros((nz, rows), f32)

        def chunk(j, carry):
            iota_col = lax.broadcasted_iota(jnp.int32, (LANES, LANES), 0).astype(f32)
            cols, weights, values = tap_col[j], tap_w[j], tap_res[j]
            right = [[[], []] for _ in levels]
            for t in range(per):
                col_hot = iota_col == cols[t : t + 1]
                for k, n in enumerate(levels):
                    amount = weights[t : t + 1] * values[n : n + 1]
                    hi = amount.astype(bf16).astype(f32)
                    right[k][0].append(jnp.where(col_hot, hi, 0.0).astype(bf16))
                    right[k][1].append(jnp.where(col_hot, amount - hi, 0.0).astype(bf16))
            both = jnp.concatenate(
                [jnp.concatenate(right[k][s], axis=1) for s in range(2) for k in range(count)], axis=0
            )
            acc = nt(both, hot[j])
            acc = acc[0 : count * LANES] + acc[count * LANES : 2 * count * LANES]
            mine = which[j, 0:1, 0:1]
            for h in range(halves):
                for k, n in enumerate(levels):
                    src[n, h * LANES : (h + 1) * LANES, :] += jnp.where(
                        mine == float(h), acc[k * LANES : (k + 1) * LANES], 0.0
                    )
            return carry

        lax.fori_loop(0, CHUNKS, chunk, 0, unroll=True)

    def stencils():
        to_, at_ = [lax.broadcasted_iota(jnp.int32, m_in.shape, d) for d in range(2)]
        m_in[...] = cross(to_ // ny - at_ // ny, to_ % ny - at_ % ny).astype(bf16)
        at_, to_ = [lax.broadcasted_iota(jnp.int32, m_z.shape, d) for d in range(2)]
        m_z[...] = stencil(to_ - at_).astype(bf16)

    stencils()
    for ref in (hx, hy, hz):
        for side in range(2):
            ref[zero_slot, side] = jnp.zeros(ref.shape[2:], f32)
    loads[0].wait()
    pack_y(0, 0)
    pack_z(0, 0)
    loads[1].wait()
    loads[2].wait()
    fq[0] = cf[...] * q4[...]
    pack_y(1, 0)
    pack_z(1, 0)
    pl.semaphore_wait(barrier, sum(h.astype(jnp.int32) for h in has[:4]) + len(peers))
    res_moves = [
        pltpu.make_async_remote_copy(
            src_ref=res_h, dst_ref=res.at[me[2]],
            send_sem=res_send.at[k], recv_sem=res_recv.at[k],
            device_id=peers[k], device_id_type=MESH,
        )
        for k in range(len(peers))
    ]
    start(0, 0, (2, 3, 0, 1))
    for move in res_moves:
        move.start()
    start(1, 0, (2, 3, 0, 1))
    start(0, 0, (4, 5))
    start(1, 0, (4, 5))
    own = pltpu.make_async_copy(res_h, res.at[me[2]], load_sem.at[len(loads)])
    own.start()

    for load in loads[3:]:
        load.wait()
    select()
    local(0, 0)
    local(1, 0)
    own.wait()
    for k in range(len(peers)):
        dst = res.at[lax.rem(me[2] + sizes[2] - 1 - k, sizes[2])]
        pltpu.make_async_remote_copy(
            src_ref=dst, dst_ref=dst,
            send_sem=res_send.at[k], recv_sem=res_recv.at[k],
            device_id=peers[k], device_id_type=MESH,
        ).wait_recv()
    late = steps - 1

    for r in range(steps):
        more = r + 1 < steps
        finish(0, r)
        if more:
            send(0, r + 1)
        if r == 0:
            residuals()
            sources(late, steps - late)
            base[1] += src[steps - 1].T
        finish(1, r)
        if more:
            send(1, r + 1)
            local(0, r + 1)
            if r == 0:
                sources(0, late)
            local(1, r + 1)
        if r == steps - 2:
            part = one[...] * lap[0]
            for n in range(1, steps - 1):
                part = part + qb[steps - 2 - n] * lap[n]
            total[...] = part
    res_again[...] = res[me[2]]
    grad[...] = total[...] + q4[...] * lap[steps - 1]

    for move in res_moves:
        move.wait_send()
    for ch in range(2):
        for r in range(steps):
            for f in range(6):
                @pl.when(has[f])
                def _(f=f):
                    copy(ch, r, f).wait_send()


def fused(sizes, p0, p1, q5, q4, cf, residual, receiver_cell, tap_offset, tap_weight, trace_receiver):
    nx, ny, nz = p0.shape
    steps = residual.shape[0]
    taps, mics = tap_weight.shape
    rows = nx * ny
    f32, bf16 = jnp.float32, jnp.bfloat16
    flat = [a.reshape(rows, nz) for a in (p0, p1, q5, q4, cf)]
    plane = pltpu.VMEM((rows, nz), f32)
    slots = 2 * steps + 1
    packed = rows // 32
    return pl.pallas_call(
        functools.partial(fused_kernel, sizes, ny),
        out_shape=[jax.ShapeDtypeStruct((rows, nz), f32)] * 8
        + [
            jax.ShapeDtypeStruct(a.shape, a.dtype)
            for a in (residual, receiver_cell, tap_offset, tap_weight, trace_receiver)
        ]
        + [jax.ShapeDtypeStruct((1,), jnp.int32)],
        in_specs=[pl.BlockSpec(memory_space=pltpu.HBM)] * 10,
        out_specs=[pl.BlockSpec(memory_space=pltpu.VMEM)] * 13 + [pl.BlockSpec(memory_space=pltpu.SMEM)],
        scratch_shapes=[
            pltpu.SemaphoreType.DMA((10,)),
            pltpu.VMEM((rows, rows), bf16),
            pltpu.VMEM((nz, nz), bf16),
            pltpu.VMEM((steps, rows, nz), f32),
            pltpu.VMEM((steps, rows, nz), f32),
            pltpu.VMEM((steps, rows, nz), f32),
            pltpu.VMEM((2, rows, nz), f32),
            plane,
            pltpu.VMEM((steps - 2, rows, nz), f32),
            pltpu.VMEM((steps, nz, rows), f32),
            plane,
            pltpu.VMEM((slots, 2, 4 * ny, nz), f32),
            pltpu.VMEM((slots, 2, 4 * nx, nz), f32),
            pltpu.VMEM((slots, 2, packed, LANES), f32),
            pltpu.VMEM((2, steps, 2, 4 * nx, nz), f32),
            pltpu.VMEM((2, steps, 2, packed, LANES), f32),
            pltpu.SemaphoreType.DMA((2, steps, 6)),
            pltpu.SemaphoreType.DMA((2, steps, 6)),
            pltpu.VMEM((sizes[2],) + residual.shape, f32),
            pltpu.SemaphoreType.DMA((sizes[2],)),
            pltpu.SemaphoreType.DMA((sizes[2],)),
            pltpu.VMEM((CHUNKS, HELD, mics), bf16),
            pltpu.VMEM((5 * taps, mics), bf16),
            pltpu.VMEM((CHUNKS, taps * HELD // LANES, LANES), f32),
            pltpu.VMEM((CHUNKS, taps * HELD // LANES, LANES), f32),
            pltpu.VMEM((CHUNKS, taps * HELD // LANES, LANES), f32),
            pltpu.VMEM((CHUNKS, steps, LANES), f32),
            pltpu.VMEM((CHUNKS, rows, taps * HELD), bf16),
            pltpu.VMEM((CHUNKS, 8, LANES), f32),
        ],
        compiler_params=pltpu.CompilerParams(
            collective_id=2, has_side_effects=True, vmem_limit_bytes=56 * 2**20
        ),
        name="fused",
    )(*flat, residual, receiver_cell, tap_offset, tap_weight, trace_receiver)


def store_kernel(a, b, c, out_a, out_b, out_c, sem):
    moves = [
        pltpu.make_async_copy(s, d, sem.at[i])
        for i, (s, d) in enumerate(((a, out_a), (b, out_b), (c, out_c)))
    ]
    for move in moves:
        move.start()
    for move in moves:
        move.wait()


def store(*results):
    outs = pl.pallas_call(
        store_kernel,
        out_shape=[jax.ShapeDtypeStruct(a.shape, a.dtype) for a in results],
        in_specs=[pl.BlockSpec(memory_space=pltpu.VMEM)] * 3,
        out_specs=[pl.BlockSpec(memory_space=pltpu.HBM)] * 3,
        scratch_shapes=[pltpu.SemaphoreType.DMA((3,))],
        name="store",
    )(*results)
    return tuple(outs)


def general(sizes, block, p0, p1, q5, q4, cf, residual, receiver_cell, tap_offset, tap_weight, trace_receiver):
    gathered, *mats = gather(sizes, block, residual)
    src = build_sources(block, gathered, receiver_cell, tap_offset, tap_weight, trace_receiver)
    return store(*wave(sizes, block, p0, p1, q5, q4, cf, src, mats))


def shards(sizes, *args):
    block = args[0].shape
    *results, flag = fused(sizes, *args[:-1], args[-1].reshape(1, -1))
    outs = lax.cond(
        flag[0] == 0,
        lambda *held: store(*held[:3]),
        lambda *held: general(sizes, block, *held[3:]),
        *results,
    )
    return tuple(o.reshape(block) for o in outs)


def solution(mesh):
    field = P(*AXES)
    return jax.shard_map(
        functools.partial(shards, tuple(mesh.shape[a] for a in AXES)),
        mesh=mesh,
        in_specs=(field,) * 5 + (P(None, "gz"), P(), P(), P(), P()),
        out_specs=(field,) * 3,
        check_vma=False,
    )
```

```python
import functools

import jax
import jax.numpy as jnp
from jax import lax
from jax.experimental import pallas as pl
from jax.experimental.pallas import tpu as pltpu
from jax.sharding import PartitionSpec as P

C = (-205.0 / 72.0, 8.0 / 5.0, -1.0 / 5.0, 8.0 / 315.0, -1.0 / 560.0)
AXES = ("gx", "gy", "gz")
MESH = pl.DeviceIdType.MESH


def split3(v):
    hi = v.astype(jnp.bfloat16)
    rest = v - hi.astype(jnp.float32)
    mid = rest.astype(jnp.bfloat16)
    lo = (rest - mid.astype(jnp.float32)).astype(jnp.bfloat16)
    return [hi, mid, lo]


def nt(a, b):
    return lax.dot_general(a, b, (((1,), (1,)), ((), ())), preferred_element_type=jnp.float32)


def source_kernel(block, res_ref, cell_ref, off_ref, w_ref, tr_ref, out_ref, table, info):
    bx, by, bz = block
    starts = [lax.axis_index(a) * n for a, n in zip(AXES, block)]
    taps, mics = w_ref.shape
    steps = res_ref.shape[1]
    rel = [cell_ref[d : d + 1, :] - starts[d] for d in range(3)]
    near = functools.reduce(
        jnp.logical_and, [(rel[d] >= -4) & (rel[d] < block[d] + 4) for d in range(3)]
    )
    at = [rel[d] + off_ref[d] for d in range(3)]
    inside = functools.reduce(
        jnp.logical_and, [(at[d] >= 0) & (at[d] < block[d]) for d in range(3)]
    )
    row = jnp.where(inside, at[0] * by + at[1], -1)
    col = jnp.where(inside, at[2], -1)
    table[0:taps, :] = row.astype(jnp.float32).astype(jnp.bfloat16)
    table[taps : 2 * taps, :] = col.astype(jnp.float32).astype(jnp.bfloat16)
    for i, part in enumerate(split3(w_ref[...])):
        table[(2 + i) * taps : (3 + i) * taps, :] = part
    near_f = jnp.where(near, 1.0, 0.0)
    lanes = 128
    blocks = mics // lanes
    tri = (
        lax.broadcasted_iota(jnp.int32, (lanes, lanes), 0)
        < lax.broadcasted_iota(jnp.int32, (lanes, lanes), 1)
    )
    tri = jnp.where(tri, 1.0, 0.0).astype(jnp.bfloat16)
    base = jnp.float32(0.0)
    for i in range(blocks):
        part = near_f[:, i * lanes : (i + 1) * lanes]
        before = jnp.dot(
            jnp.broadcast_to(part, (8, lanes)).astype(jnp.bfloat16),
            tri,
            preferred_element_type=jnp.float32,
        )[0:1]
        slot = jnp.where(part > 0.5, before + base, -1.0)
        info[0:1, i * lanes : (i + 1) * lanes] = slot
        base = base + jnp.sum(part)
    count = base.astype(jnp.int32)
    out_ref[...] = jnp.zeros_like(out_ref)
    share = 2
    held = lanes // share
    per = taps // share
    part_of = lax.broadcasted_iota(jnp.int32, (per, lanes), 1) // held

    def spread(v):
        out = v[0:per]
        for i in range(1, share):
            out = jnp.where(part_of == i, v[i * per : (i + 1) * per], out)
        return out

    def chunk(j, carry):
        slots = (lax.broadcasted_iota(jnp.int32, (held, mics), 0) + j * held).astype(jnp.float32)
        sel = jnp.where(slots == info[0:1, :], 1.0, 0.0)
        mic_id = lax.broadcasted_iota(jnp.int32, (1, mics), 1).astype(jnp.float32)
        mic = jnp.sum(sel * (mic_id + 1.0), axis=1, keepdims=True) - 1.0
        sel_r = jnp.where(tr_ref[...].astype(jnp.float32) == mic, 1.0, 0.0).astype(jnp.bfloat16)
        tab = jnp.concatenate([nt(table[...], sel.astype(jnp.bfloat16))] * share, axis=1)
        rows = spread(tab[0:taps])
        cols = spread(tab[taps : 2 * taps])
        weights = spread(
            tab[2 * taps : 3 * taps] + tab[3 * taps : 4 * taps] + tab[4 * taps : 5 * taps]
        )
        whole = jnp.concatenate([res_ref[g] for g in range(res_ref.shape[0])], axis=1)
        res = sum(nt(part, sel_r) for part in split3(whole))
        res = jnp.concatenate([res] * share, axis=1)
        iota_row = lax.broadcasted_iota(jnp.int32, (bx * by, lanes), 0).astype(jnp.float32)
        iota_col = lax.broadcasted_iota(jnp.int32, (bz, lanes), 0).astype(jnp.float32)
        group = 4
        for t0 in range(0, per, group):
            left, right = [[] for _ in range(steps)], []
            for t in range(t0, t0 + group):
                row_hot = iota_row == rows[t : t + 1]
                col_hot = jnp.where(iota_col == cols[t : t + 1], 1.0, 0.0).astype(jnp.bfloat16)
                right += [col_hot, col_hot]
                for n in range(steps):
                    amount = weights[t : t + 1] * res[n : n + 1]
                    hi = amount.astype(jnp.bfloat16).astype(jnp.float32)
                    lo = amount - hi
                    left[n].append(jnp.where(row_hot, hi, 0.0).astype(jnp.bfloat16))
                    left[n].append(jnp.where(row_hot, lo, 0.0).astype(jnp.bfloat16))
            right = jnp.concatenate(right, axis=1)
            for n in range(steps):
                out_ref[n] += nt(jnp.concatenate(left[n], axis=1), right)
        return carry

    lax.fori_loop(0, (count + held - 1) // held, chunk, 0)


def build_sources(block, residual, receiver_cell, tap_offset, tap_weight, trace_receiver):
    steps = residual.shape[1]
    taps, mics = tap_weight.shape
    return pl.pallas_call(
        functools.partial(source_kernel, block),
        out_shape=jax.ShapeDtypeStruct((steps, block[0] * block[1], block[2]), jnp.float32),
        in_specs=[pl.BlockSpec(memory_space=pltpu.VMEM)] * 5,
        out_specs=pl.BlockSpec(memory_space=pltpu.VMEM),
        scratch_shapes=[
            pltpu.VMEM((5 * taps, mics), jnp.bfloat16),
            pltpu.VMEM((8, mics), jnp.float32),
        ],
        compiler_params=pltpu.CompilerParams(vmem_limit_bytes=32 * 2**20),
        name="sources",
    )(residual, receiver_cell, tap_offset, tap_weight, trace_receiver)


def stencil(d):
    d = jnp.abs(d)
    return sum(jnp.where(d == k, float(round(5040 * C[k])), 0.0) for k in range(1, 5))


def cross(dx, dy):
    return jnp.where(dy == 0, stencil(dx), 0.0) + jnp.where(dx == 0, stencil(dy), 0.0)


def matrices(nx, ny, m_in, m_face, m_z, m_end):
    def grid(ref):
        return [lax.broadcasted_iota(jnp.int32, ref.shape, d) for d in range(2)]

    to, at = grid(m_in)
    m_in[...] = cross(to // ny - at // ny, to % ny - at % ny).astype(jnp.bfloat16)
    to, at = grid(m_face)
    x, y = to // ny, to % ny
    upper = at >= 4 * ny
    face = at - jnp.where(upper, 4 * ny, 0)
    in_x = cross(x - (face // ny + jnp.where(upper, nx, -4)), y - face % ny)
    pack = at - 8 * ny
    upper = pack >= 4 * nx
    pack = pack - jnp.where(upper, 4 * nx, 0)
    far = jnp.where(pack % 8 < 4, 0, 1) == jnp.where(upper, 1, 0)
    face_x = pack // 8 + jnp.where(far, nx // 2, 0)
    in_y = cross(x - face_x, y - (pack % 4 + jnp.where(upper, ny, -4)))
    m_face[...] = jnp.where(at < 8 * ny, in_x, in_y).astype(jnp.bfloat16)
    at, to = grid(m_z)
    m_z[...] = stencil(to - at).astype(jnp.bfloat16)
    at, to = grid(m_end)
    m_end[...] = stencil(to - jnp.where(at < 64, at + m_z.shape[0], at - 128)).astype(jnp.bfloat16)


def gather_kernel(n, block, res, out, m_in, m_face, m_z, m_end, land, send_sem, recv_sem):
    gz = lax.axis_index("gz")
    ahead = [{"gz": lax.rem(gz + k, n)} for k in range(1, n)]
    barrier = pltpu.get_barrier_semaphore()
    for other in ahead:
        pl.semaphore_signal(barrier, inc=1, device_id=other, device_id_type=MESH)
    pl.semaphore_wait(barrier, n - 1)
    moves = [
        pltpu.make_async_remote_copy(
            src_ref=res, dst_ref=land.at[gz],
            send_sem=send_sem.at[k], recv_sem=recv_sem.at[k],
            device_id=ahead[k], device_id_type=MESH,
        )
        for k in range(n - 1)
    ]
    for move in moves:
        move.start()
    matrices(block[0], block[1], m_in, m_face, m_z, m_end)
    land[gz] = res[...]
    for k in range(n - 1):
        dst = land.at[lax.rem(gz + n - 1 - k, n)]
        pltpu.make_async_remote_copy(
            src_ref=dst, dst_ref=dst,
            send_sem=send_sem.at[k], recv_sem=recv_sem.at[k],
            device_id=ahead[k], device_id_type=MESH,
        ).wait_recv()
    out[...] = land[...]
    for move in moves:
        move.wait_send()


def gather(sizes, block, residual):
    nx, ny, nz = block
    n = sizes[2]
    vmem = pl.BlockSpec(memory_space=pltpu.VMEM)
    shape = (n,) + residual.shape
    mats = [(nx * ny, nx * ny), (nx * ny, 8 * (nx + ny)), (nz, nz), (128, nz)]
    return pl.pallas_call(
        functools.partial(gather_kernel, n, block),
        out_shape=[jax.ShapeDtypeStruct(shape, jnp.float32)]
        + [jax.ShapeDtypeStruct(m, jnp.bfloat16) for m in mats],
        in_specs=[vmem],
        out_specs=[vmem] * 5,
        scratch_shapes=[
            pltpu.VMEM(shape, jnp.float32),
            pltpu.SemaphoreType.DMA((n,)),
            pltpu.SemaphoreType.DMA((n,)),
        ],
        compiler_params=pltpu.CompilerParams(
            collective_id=1, has_side_effects=True, vmem_limit_bytes=16 * 2**20
        ),
        cost_estimate=pl.CostEstimate(flops=4 * 10**9, bytes_accessed=12 * 10**6, transcendentals=0),
        name="gather",
    )(residual)


def nn(a, b):
    return jnp.dot(a, b, preferred_element_type=jnp.float32)


def wave_kernel(
    sizes, ny, p0, p1, q5, q4, cf, src, m_in, m_face, m_z, m_end, grad, one, zero,
    fp, fq, lap, lq, qb, hl, zl, ys, send_sem, recv_sem,
):
    steps = src.shape[0]
    rows, nz = p0.shape
    nx = rows // ny
    faces_rows = (4 * ny, 4 * ny, 4 * nx, 4 * nx)
    me = [lax.axis_index(a) for a in AXES]
    has = []
    for d in range(3):
        has += [me[d] > 0, me[d] < sizes[d] - 1]
    to = []
    for d in range(3):
        to += [{AXES[d]: jnp.maximum(me[d] - 1, 0)}, {AXES[d]: jnp.minimum(me[d] + 1, sizes[d] - 1)}]

    barrier = pltpu.get_barrier_semaphore()
    for f in range(6):
        @pl.when(has[f])
        def _(f=f):
            pl.semaphore_signal(barrier, inc=1, device_id=to[f], device_id_type=MESH)
    pl.semaphore_wait(barrier, sum(h.astype(jnp.int32) for h in has))

    sub = lax.broadcasted_iota(jnp.int32, (8, nz), 0)
    lane = lax.broadcasted_iota(jnp.int32, (rows, 128), 1)

    def field(ch, r):
        if r == 0 and ch == 0:
            return p1
        return (fp, fq)[ch].at[r]

    def landing(ch, r, f):
        if f >= 4:
            return zl.at[ch, r, f - 4]
        return hl.at[ch, r, pl.ds(sum(faces_rows[:f]), faces_rows[f])]

    def copies(ch, r):
        f_ref = field(ch, r)
        srcs = [
            f_ref.at[pl.ds(0, 4 * ny)],
            f_ref.at[pl.ds(rows - 4 * ny, 4 * ny)],
            ys.at[ch, r, 0],
            ys.at[ch, r, 1],
            f_ref.at[pl.ds(0, rows), pl.ds(0, 128)],
            f_ref.at[pl.ds(0, rows), pl.ds(nz - 128, 128)],
        ]
        return [
            pltpu.make_async_remote_copy(
                src_ref=srcs[f],
                dst_ref=landing(ch, r, f ^ 1),
                send_sem=send_sem.at[ch, r, f],
                recv_sem=recv_sem.at[ch, r, f ^ 1],
                device_id=to[f],
                device_id_type=MESH,
            )
            for f in range(6)
        ]

    def send(ch, r):
        f_ref = field(ch, r)
        moves = copies(ch, r)
        for f in (0, 1, 4, 5):
            @pl.when(has[f])
            def _(f=f):
                moves[f].start()
        for i in range(nx // 2):
            lo, far = i * ny, (i + nx // 2) * ny
            a, b = f_ref[lo : lo + 8], f_ref[far : far + 8]
            ys[ch, r, 0, 8 * i : 8 * i + 8] = jnp.where(sub < 4, a, pltpu.roll(b, 4, 0))
            a, b = f_ref[lo + ny - 8 : lo + ny], f_ref[far + ny - 8 : far + ny]
            ys[ch, r, 1, 8 * i : 8 * i + 8] = jnp.where(sub >= 4, a, pltpu.roll(b, 4, 0))
        for f in (2, 3):
            @pl.when(has[f])
            def _(f=f):
                moves[f].start()

    def land(ch, r):
        for f in range(6):
            @pl.when(has[f])
            def _(f=f):
                dst = landing(ch, r, f)
                pltpu.make_async_remote_copy(
                    src_ref=dst, dst_ref=dst,
                    send_sem=send_sem.at[ch, r, f], recv_sem=recv_sem.at[ch, r, f],
                    device_id=to[f], device_id_type=MESH,
                ).wait_recv()

    def local(ch, r, out):
        f = field(ch, r)[...]
        acc = 0.0
        for part in split3(f):
            acc = acc + nn(m_in[...], part) + nn(part, m_z[...])
        out[...] = acc * (1.0 / 5040.0) + (3.0 * C[0]) * f

    def finish(ch, r, out):
        land(ch, r)
        acc = 0.0
        for part in split3(hl[ch, r]):
            acc = acc + nn(m_face[...], part)
        for part in split3(jnp.where(lane < 64, zl[ch, r, 1], zl[ch, r, 0])):
            acc = acc + nn(part, m_end[...])
        return out[...] + acc * (1.0 / 5040.0)

    send(0, 0)
    fq[0] = cf[...] * q4[...]
    send(1, 0)
    for f in range(6):
        @pl.when(jnp.logical_not(has[f]))
        def _(f=f):
            for ch in range(2):
                for r in range(steps):
                    dst = landing(ch, r, f)
                    dst[...] = jnp.zeros(dst.shape, jnp.float32)

    local(0, 0, lap.at[0])
    local(1, 0, lq)
    for r in range(steps):
        full = finish(0, r, lap.at[r])
        lap[r] = full
        if r + 1 < steps:
            old = p0 if r == 0 else field(0, r - 1)
            fp[r + 1] = 2.0 * field(0, r)[...] - old[...] + cf[...] * full
            send(0, r + 1)
            local(0, r + 1, lap.at[r + 1])

        full = finish(1, r, lq)
        now = q4 if r == 0 else qb.at[r - 1]
        old = q5 if r == 0 else (q4 if r == 1 else qb.at[r - 2])
        new = 2.0 * now[...] - old[...] + full + src[steps - 1 - r]
        if r + 1 < steps:
            qb[r] = new
            fq[r + 1] = cf[...] * new
            send(1, r + 1)
            local(1, r + 1, lq)
        else:
            zero[...] = new
            one[...] = now[...]
            total = q4[...] * lap[steps - 1]
            for n in range(1, steps):
                total = total + qb[n - 1] * lap[steps - 1 - n]
            grad[...] = total

    for ch in range(2):
        for r in range(steps):
            moves = copies(ch, r)
            for f in range(6):
                @pl.when(has[f])
                def _(f=f):
                    moves[f].wait_send()


def wave(sizes, block, p0, p1, q5, q4, cf, src, mats):
    nx, ny, nz = block
    steps = src.shape[0]
    rows = nx * ny
    f32 = jnp.float32
    outs = pl.pallas_call(
        functools.partial(wave_kernel, sizes, ny),
        out_shape=[jax.ShapeDtypeStruct((rows, nz), f32)] * 3,
        in_specs=[pl.BlockSpec(memory_space=pltpu.VMEM)] * 10,
        out_specs=[pl.BlockSpec(memory_space=pltpu.VMEM)] * 3,
        scratch_shapes=[
            pltpu.VMEM((steps, rows, nz), f32),
            pltpu.VMEM((steps, rows, nz), f32),
            pltpu.VMEM((steps, rows, nz), f32),
            pltpu.VMEM((rows, nz), f32),
            pltpu.VMEM((steps, rows, nz), f32),
            pltpu.VMEM((2, steps, 8 * (nx + ny), nz), f32),
            pltpu.VMEM((2, steps, 2, rows, 128), f32),
            pltpu.VMEM((2, steps, 2, 4 * nx, nz), f32),
            pltpu.SemaphoreType.DMA((2, steps, 6)),
            pltpu.SemaphoreType.DMA((2, steps, 6)),
        ],
        compiler_params=pltpu.CompilerParams(
            collective_id=0, has_side_effects=True, vmem_limit_bytes=32 * 2**20
        ),
        name="wave",
    )(p0, p1, q5, q4, cf, src, *mats)
    return outs


CHUNKS = 5
HELD = 64
LANES = 128


def roll(v, shift, axis):
    shift = shift % v.shape[axis]
    return v if shift == 0 else pltpu.roll(v, shift, axis)


def near_counts(sizes, block, cells):
    near = []
    for d in range(2):
        at = lax.broadcasted_iota(jnp.int32, (sizes[d], cells[d].shape[1]), 0) * block[d]
        rel = cells[d] - at
        near.append(jnp.where((rel >= -4) & (rel < block[d] + 4), 1.0, 0.0))
    xy = jnp.concatenate([near[0][i : i + 1] * near[1] for i in range(sizes[0])], axis=0)
    counts = []
    for h in range(block[2] // LANES):
        at = lax.broadcasted_iota(jnp.int32, (sizes[2], cells[2].shape[1]), 0) * block[2] + h * LANES
        rel = cells[2] - at
        z = jnp.where((rel >= -4) & (rel < LANES + 4), 1.0, 0.0)
        counts.append(nt(xy.astype(jnp.bfloat16), z.astype(jnp.bfloat16)))
    return counts


def chunks_of(count):
    return jnp.floor((count + (HELD - 1.0)) * (1.0 / HELD))


def fused_kernel(
    sizes, ny,
    p0_h, p1_h, q5_h, q4_h, cf_h, res_h, cell_h, off_h, w_h, tr_h,
    grad, one, zero, p0, p1, q5, q4, cf, res_again, cell, off, w, tr, flag,
    load_sem,
    m_in, m_z, fp, fq, lap, base, ahead, qb, src, total,
    hx, hy, hz, ys, zs, send_sem, recv_sem,
    res, res_send, res_recv,
    sel_mic, table, tap_row, tap_col, tap_w, tap_res, hot, which,
):
    steps = res.shape[1]
    rows, nz = p1.shape
    nx = rows // ny
    block = (nx, ny, nz)
    tiles = rows // 8
    ytiles = ny // 8
    groups = tiles // 32
    halves = nz // LANES
    taps, mics = w.shape
    bf16, f32 = jnp.bfloat16, jnp.float32
    per = taps * HELD // LANES
    zero_slot = 2 * steps

    loads = [
        pltpu.make_async_copy(a, b, load_sem.at[i])
        for i, (a, b) in enumerate(
            [(p1_h, p1), (q4_h, q4), (cf_h, cf), (cell_h, cell), (off_h, off), (w_h, w), (tr_h, tr), (p0_h, p0), (q5_h, q5)]
        )
    ]
    for load in loads[:3]:
        load.start()

    me = [lax.axis_index(a) for a in AXES]
    has = []
    for d in range(3):
        has += [me[d] > 0, me[d] < sizes[d] - 1]
    to = []
    for d in range(3):
        to += [{AXES[d]: jnp.maximum(me[d] - 1, 0)}, {AXES[d]: jnp.minimum(me[d] + 1, sizes[d] - 1)}]
    peers = [{"gz": lax.rem(me[2] + k, sizes[2])} for k in range(1, sizes[2])]

    barrier = pltpu.get_barrier_semaphore()
    for f in range(4):
        @pl.when(has[f])
        def _(f=f):
            pl.semaphore_signal(barrier, inc=1, device_id=to[f], device_id_type=MESH)
    for peer in peers:
        pl.semaphore_signal(barrier, inc=1, device_id=peer, device_id_type=MESH)

    sub = lax.broadcasted_iota(jnp.int32, (8, nz), 0)
    lane = lax.broadcasted_iota(jnp.int32, (8, LANES), 1)
    lane_group = lane // 4

    def field(ch, r):
        if r == 0 and ch == 0:
            return p1
        return (fp, fq)[ch].at[r]

    def landing(ch, r, f, slot=None):
        slot = ch * steps + r if slot is None else slot
        return (hx, hy, hz)[f // 2].at[slot, f % 2]

    def copy(ch, r, f):
        f_ref = field(ch, r)
        if f == 0:
            face = f_ref.at[pl.ds(0, 4 * ny)]
        elif f == 1:
            face = f_ref.at[pl.ds(rows - 4 * ny, 4 * ny)]
        else:
            face = (ys, zs)[f // 2 - 1].at[ch, r, f % 2]
        return pltpu.make_async_remote_copy(
            src_ref=face,
            dst_ref=landing(ch, r, f ^ 1),
            send_sem=send_sem.at[ch, r, f],
            recv_sem=recv_sem.at[ch, r, f ^ 1],
            device_id=to[f],
            device_id_type=MESH,
        )

    def start(ch, r, faces):
        for f in faces:
            @pl.when(has[f])
            def _(f=f):
                copy(ch, r, f).start()

    def pack_y(ch, r):
        f_ref = field(ch, r)
        for i in range(nx // 2):
            lo, far = i * ny, (i + nx // 2) * ny
            a, b = f_ref[lo : lo + 8], f_ref[far : far + 8]
            ys[ch, r, 0, 8 * i : 8 * i + 8] = jnp.where(sub < 4, a, roll(b, 4, 0))
            a, b = f_ref[lo + ny - 8 : lo + ny], f_ref[far + ny - 8 : far + ny]
            ys[ch, r, 1, 8 * i : 8 * i + 8] = jnp.where(sub >= 4, a, roll(b, 4, 0))

    def pack_z(ch, r):
        f_ref = field(ch, r)
        for g in range(groups):
            low = jnp.zeros((8, LANES), f32)
            high = low
            for i in range(32):
                at = 8 * (32 * g + i)
                mine = lane_group == i
                low = jnp.where(mine, roll(f_ref[at : at + 8, 0:LANES], 4 * i, 1), low)
                high = jnp.where(mine, roll(f_ref[at : at + 8, nz - LANES : nz], 4 * i + 4, 1), high)
            zs[ch, r, 0, 8 * g : 8 * g + 8] = low
            zs[ch, r, 1, 8 * g : 8 * g + 8] = high

    def land(ch, r, faces):
        for f in faces:
            @pl.when(has[f])
            def _(f=f):
                dst = landing(ch, r, f)
                pltpu.make_async_remote_copy(
                    src_ref=dst, dst_ref=dst,
                    send_sem=send_sem.at[ch, r, f], recv_sem=recv_sem.at[ch, r, f],
                    device_id=to[f], device_id_type=MESH,
                ).wait_recv()

    def near_slot(ch, r, f):
        return jnp.where(has[f], ch * steps + r, zero_slot)

    def ramp(v, axis, at, upward):
        at = at % 4
        acc = 0.0
        for s in range(4):
            if upward:
                acc = acc + jnp.where(at + s < 4, C[4 - s], 0.0) * roll(v, -s, axis)
            else:
                acc = acc + jnp.where(at >= s, C[4 - s], 0.0) * roll(v, s, axis)
        return acc

    def local(ch, r):
        f = field(ch, r)[...]
        acc = 0.0
        for part in split3(f):
            acc = acc + nn(m_in[...], part) + nn(part, m_z[...])
        acc = acc * (1.0 / 5040.0) + (3.0 * C[0]) * f
        if ch == 0:
            if r + 1 < steps:
                old = p0 if r == 0 else field(0, r - 1)
                ahead[...] = 2.0 * f - old[...]
        else:
            now = q4 if r == 0 else (one if r == steps - 1 else qb.at[r - 1])
            old = q5 if r == 0 else (q4 if r == 1 else qb.at[r - 2])
            acc = acc + (2.0 * now[...] - old[...])
        base[ch] = acc

    def finish(ch, r):
        land(ch, r, (4, 5))
        for side in range(2):
            ref = landing(ch, r, 4 + side, near_slot(ch, r, 4 + side))
            for g in range(groups):
                v = ramp(ref[8 * g : 8 * g + 8], 1, lane, side == 0)
                for i in range(32):
                    at = 8 * (32 * g + i)
                    if side == 0:
                        base[ch, at : at + 8, 0:LANES] += jnp.where(lane < 4, roll(v, -4 * i, 1), 0.0)
                    else:
                        base[ch, at : at + 8, nz - LANES : nz] += jnp.where(
                            lane >= LANES - 4, roll(v, -4 - 4 * i, 1), 0.0
                        )
        land(ch, r, (0, 1, 2, 3))
        x_ref = [landing(ch, r, f, near_slot(ch, r, f)) for f in (0, 1)]
        y_ref = [landing(ch, r, f, near_slot(ch, r, f)) for f in (2, 3)]
        for i in range(nx // 2):
            y_part = [ramp(y_ref[side][8 * i : 8 * i + 8], 0, sub, side == 0) for side in range(2)]
            for x in (i, i + nx // 2):
                for yt in range(ytiles):
                    at = x * ny + 8 * yt
                    t = base[ch, at : at + 8]
                    if x < 4:
                        for j in range(x, 4):
                            t = t + C[x + 4 - j] * x_ref[0][j * ny + 8 * yt : j * ny + 8 * yt + 8]
                    if x >= nx - 4:
                        for j in range(x - nx + 5):
                            t = t + C[nx + j - x] * x_ref[1][j * ny + 8 * yt : j * ny + 8 * yt + 8]
                    if yt == 0:
                        part = y_part[0] if x != i else roll(y_part[0], 4, 0)
                        t = t + jnp.where(sub < 4, part, 0.0)
                    if yt == ytiles - 1:
                        part = y_part[1] if x != i else roll(y_part[1], 4, 0)
                        t = t + jnp.where(sub >= 4, part, 0.0)
                    if ch == 0:
                        lap[r, at : at + 8] = t
                        if r + 1 < steps:
                            fp[r + 1, at : at + 8] = ahead[at : at + 8] + cf[at : at + 8] * t
                    else:
                        out = zero if r == steps - 1 else (one if r == steps - 2 else qb.at[r])
                        out[at : at + 8] = t
                        if r + 1 < steps:
                            fq[r + 1, at : at + 8] = cf[at : at + 8] * t

    def send(ch, r):
        pack_y(ch, r)
        start(ch, r, (2, 3))
        start(ch, r, (0, 1))
        pack_z(ch, r)
        start(ch, r, (4, 5))

    def select():
        cells = [cell[d : d + 1, :] for d in range(3)]
        rel = [cells[d] - me[d] * block[d] for d in range(3)]
        side = functools.reduce(jnp.logical_and, [(rel[d] >= -4) & (rel[d] < block[d] + 4) for d in range(2)])
        near = [
            jnp.where(side & (rel[2] >= h * LANES - 4) & (rel[2] < (h + 1) * LANES + 4), 1.0, 0.0)
            for h in range(halves)
        ]
        near = jnp.concatenate(near, axis=0)
        tri = (
            lax.broadcasted_iota(jnp.int32, (LANES, LANES), 0)
            < lax.broadcasted_iota(jnp.int32, (LANES, LANES), 1)
        )
        tri = jnp.where(tri, 1.0, 0.0).astype(bf16)
        count = jnp.zeros((halves, 1), f32)
        order = []
        for i in range(mics // LANES):
            part = near[:, i * LANES : (i + 1) * LANES]
            order.append(nn(part.astype(bf16), tri) + count)
            count = count + jnp.sum(part, axis=1, keepdims=True)
        order = jnp.concatenate(order, axis=1)
        full = chunks_of(count)
        first = [jnp.zeros((1, 1), f32)]
        for h in range(halves):
            first.append(first[-1] + full[h : h + 1])
        slot = [
            jnp.where(near[h : h + 1] > 0.5, order[h : h + 1] + HELD * first[h], -1.0) for h in range(halves)
        ]
        every = near_counts(sizes, block, cells)
        most = jnp.max(functools.reduce(jnp.add, [chunks_of(c) for c in every]))
        flag[0] = (most > CHUNKS).astype(jnp.int32)

        at = [rel[d] + off[d] for d in range(3)]
        inside = functools.reduce(jnp.logical_and, [(at[d] >= 0) & (at[d] < block[d]) for d in range(3)])
        table[0:taps, :] = jnp.where(inside, at[0] * ny + at[1], -1).astype(f32).astype(bf16)
        table[taps : 2 * taps, :] = jnp.where(inside, at[2], -1).astype(f32).astype(bf16)
        for i, part in enumerate(split3(w[...])):
            table[(2 + i) * taps : (3 + i) * taps, :] = part

        mic_id = lax.broadcasted_iota(jnp.int32, (1, mics), 1).astype(f32) + 1.0
        trace_mic = tr[...].astype(f32) + 1.0
        part_of = lax.broadcasted_iota(jnp.int32, (per, LANES), 1) // HELD

        def spread(v):
            out = v[0:per]
            for i in range(1, LANES // HELD):
                out = jnp.where(part_of == i, v[i * per : (i + 1) * per], out)
            return out

        def chunk(j, carry):
            slots = (lax.broadcasted_iota(jnp.int32, (HELD, mics), 0) + j * HELD).astype(f32)
            hit = functools.reduce(jnp.logical_or, [slots == slot[h] for h in range(halves)])
            mic = jnp.sum(jnp.where(hit, mic_id, 0.0), axis=1, keepdims=True)
            sel_mic[j] = jnp.where(trace_mic == mic, 1.0, 0.0).astype(bf16)
            tab = nt(table[...], jnp.where(hit, 1.0, 0.0).astype(bf16))
            tab = jnp.concatenate([tab] * (LANES // HELD), axis=1)
            mine = jnp.zeros((1, 1), f32)
            for h in range(1, halves):
                mine = mine + jnp.where(j.astype(f32) >= first[h], 1.0, 0.0)
            which[j] = jnp.broadcast_to(mine, (8, LANES))
            rows_j = spread(tab[0:taps])
            tap_col[j] = spread(tab[taps : 2 * taps]) - LANES * mine
            tap_w[j] = spread(
                tab[2 * taps : 3 * taps] + tab[3 * taps : 4 * taps] + tab[4 * taps : 5 * taps]
            )
            iota_row = lax.broadcasted_iota(jnp.int32, (rows, LANES), 0).astype(f32)
            for t in range(per):
                hot[j, :, t * LANES : (t + 1) * LANES] = jnp.where(
                    iota_row == rows_j[t : t + 1], 1.0, 0.0
                ).astype(bf16)
            return carry

        lax.fori_loop(0, CHUNKS, chunk, 0, unroll=True)

    def residuals():
        whole = jnp.concatenate([res[g] for g in range(sizes[2])], axis=1)
        parts = split3(whole)
        for j in range(CHUNKS):
            v = sum(nt(part, sel_mic[j]) for part in parts)
            tap_res[j] = jnp.concatenate([v] * (LANES // HELD), axis=1)

    def sources(first, count):
        levels = range(first, first + count)
        for n in levels:
            src[n] = jnp.zeros((nz, rows), f32)

        def chunk(j, carry):
            iota_col = lax.broadcasted_iota(jnp.int32, (LANES, LANES), 0).astype(f32)
            cols, weights, values = tap_col[j], tap_w[j], tap_res[j]
            right = [[[], []] for _ in levels]
            for t in range(per):
                col_hot = iota_col == cols[t : t + 1]
                for k, n in enumerate(levels):
                    amount = weights[t : t + 1] * values[n : n + 1]
                    hi = amount.astype(bf16).astype(f32)
                    right[k][0].append(jnp.where(col_hot, hi, 0.0).astype(bf16))
                    right[k][1].append(jnp.where(col_hot, amount - hi, 0.0).astype(bf16))
            both = jnp.concatenate(
                [jnp.concatenate(right[k][s], axis=1) for s in range(2) for k in range(count)], axis=0
            )
            acc = nt(both, hot[j])
            acc = acc[0 : count * LANES] + acc[count * LANES : 2 * count * LANES]
            mine = which[j, 0:1, 0:1]
            for h in range(halves):
                for k, n in enumerate(levels):
                    src[n, h * LANES : (h + 1) * LANES, :] += jnp.where(
                        mine == float(h), acc[k * LANES : (k + 1) * LANES], 0.0
                    )
            return carry

        lax.fori_loop(0, CHUNKS, chunk, 0, unroll=True)

    def stencils():
        to_, at_ = [lax.broadcasted_iota(jnp.int32, m_in.shape, d) for d in range(2)]
        m_in[...] = cross(to_ // ny - at_ // ny, to_ % ny - at_ % ny).astype(bf16)
        at_, to_ = [lax.broadcasted_iota(jnp.int32, m_z.shape, d) for d in range(2)]
        m_z[...] = stencil(to_ - at_).astype(bf16)

    stencils()
    for ref in (hx, hy, hz):
        for side in range(2):
            ref[zero_slot, side] = jnp.zeros(ref.shape[2:], f32)
    loads[0].wait()
    for load in loads[3:]:
        load.start()
    pack_y(0, 0)
    pack_z(0, 0)
    loads[1].wait()
    loads[2].wait()
    fq[0] = cf[...] * q4[...]
    pack_y(1, 0)
    pack_z(1, 0)
    pl.semaphore_wait(barrier, sum(h.astype(jnp.int32) for h in has[:4]) + len(peers))
    res_moves = [
        pltpu.make_async_remote_copy(
            src_ref=res_h, dst_ref=res.at[me[2]],
            send_sem=res_send.at[k], recv_sem=res_recv.at[k],
            device_id=peers[k], device_id_type=MESH,
        )
        for k in range(len(peers))
    ]
    for move in res_moves:
        move.start()
    start(0, 0, (2, 3, 0, 1))
    start(1, 0, (2, 3, 0, 1))
    start(0, 0, (4, 5))
    start(1, 0, (4, 5))
    own = pltpu.make_async_copy(res_h, res.at[me[2]], load_sem.at[len(loads)])
    own.start()

    for load in loads[3:]:
        load.wait()
    select()
    local(0, 0)
    local(1, 0)
    own.wait()
    for k in range(len(peers)):
        dst = res.at[lax.rem(me[2] + sizes[2] - 1 - k, sizes[2])]
        pltpu.make_async_remote_copy(
            src_ref=dst, dst_ref=dst,
            send_sem=res_send.at[k], recv_sem=res_recv.at[k],
            device_id=peers[k], device_id_type=MESH,
        ).wait_recv()
    residuals()
    late = steps - 1

    for r in range(steps):
        more = r + 1 < steps
        finish(0, r)
        if not more:
            res_again[...] = res[me[2]]
            grad[...] = total[...] + q4[...] * lap[steps - 1]
        if more:
            send(0, r + 1)
        if r == 0:
            sources(late, steps - late)
            base[1] += src[steps - 1].T
        finish(1, r)
        if more:
            send(1, r + 1)
            local(0, r + 1)
            local(1, r + 1)
            sources(late - 1 - r, 1)
            base[1] += src[late - 1 - r].T
        if r == steps - 2:
            part = one[...] * lap[0]
            for n in range(1, steps - 1):
                part = part + qb[steps - 2 - n] * lap[n]
            total[...] = part

    for move in res_moves:
        move.wait_send()
    for ch in range(2):
        for r in range(steps):
            for f in range(6):
                @pl.when(has[f])
                def _(f=f):
                    copy(ch, r, f).wait_send()


def fused(sizes, p0, p1, q5, q4, cf, residual, receiver_cell, tap_offset, tap_weight, trace_receiver):
    nx, ny, nz = p0.shape
    steps = residual.shape[0]
    taps, mics = tap_weight.shape
    rows = nx * ny
    f32, bf16 = jnp.float32, jnp.bfloat16
    flat = [a.reshape(rows, nz) for a in (p0, p1, q5, q4, cf)]
    plane = pltpu.VMEM((rows, nz), f32)
    slots = 2 * steps + 1
    packed = rows // 32
    return pl.pallas_call(
        functools.partial(fused_kernel, sizes, ny),
        out_shape=[jax.ShapeDtypeStruct((rows, nz), f32)] * 8
        + [
            jax.ShapeDtypeStruct(a.shape, a.dtype)
            for a in (residual, receiver_cell, tap_offset, tap_weight, trace_receiver)
        ]
        + [jax.ShapeDtypeStruct((1,), jnp.int32)],
        in_specs=[pl.BlockSpec(memory_space=pltpu.HBM)] * 10,
        out_specs=[pl.BlockSpec(memory_space=pltpu.VMEM)] * 13 + [pl.BlockSpec(memory_space=pltpu.SMEM)],
        scratch_shapes=[
            pltpu.SemaphoreType.DMA((10,)),
            pltpu.VMEM((rows, rows), bf16),
            pltpu.VMEM((nz, nz), bf16),
            pltpu.VMEM((steps, rows, nz), f32),
            pltpu.VMEM((steps, rows, nz), f32),
            pltpu.VMEM((steps, rows, nz), f32),
            pltpu.VMEM((2, rows, nz), f32),
            plane,
            pltpu.VMEM((steps - 2, rows, nz), f32),
            pltpu.VMEM((steps, nz, rows), f32),
            plane,
            pltpu.VMEM((slots, 2, 4 * ny, nz), f32),
            pltpu.VMEM((slots, 2, 4 * nx, nz), f32),
            pltpu.VMEM((slots, 2, packed, LANES), f32),
            pltpu.VMEM((2, steps, 2, 4 * nx, nz), f32),
            pltpu.VMEM((2, steps, 2, packed, LANES), f32),
            pltpu.SemaphoreType.DMA((2, steps, 6)),
            pltpu.SemaphoreType.DMA((2, steps, 6)),
            pltpu.VMEM((sizes[2],) + residual.shape, f32),
            pltpu.SemaphoreType.DMA((sizes[2],)),
            pltpu.SemaphoreType.DMA((sizes[2],)),
            pltpu.VMEM((CHUNKS, HELD, mics), bf16),
            pltpu.VMEM((5 * taps, mics), bf16),
            pltpu.VMEM((CHUNKS, taps * HELD // LANES, LANES), f32),
            pltpu.VMEM((CHUNKS, taps * HELD // LANES, LANES), f32),
            pltpu.VMEM((CHUNKS, taps * HELD // LANES, LANES), f32),
            pltpu.VMEM((CHUNKS, steps, LANES), f32),
            pltpu.VMEM((CHUNKS, rows, taps * HELD), bf16),
            pltpu.VMEM((CHUNKS, 8, LANES), f32),
        ],
        compiler_params=pltpu.CompilerParams(
            collective_id=2, has_side_effects=True, vmem_limit_bytes=56 * 2**20
        ),
        name="fused",
    )(*flat, residual, receiver_cell, tap_offset, tap_weight, trace_receiver)


def store_kernel(a, b, c, out_a, out_b, out_c, sem):
    moves = [
        pltpu.make_async_copy(s, d, sem.at[i])
        for i, (s, d) in enumerate(((a, out_a), (b, out_b), (c, out_c)))
    ]
    for move in moves:
        move.start()
    for move in moves:
        move.wait()


def store(*results):
    outs = pl.pallas_call(
        store_kernel,
        out_shape=[jax.ShapeDtypeStruct(a.shape, a.dtype) for a in results],
        in_specs=[pl.BlockSpec(memory_space=pltpu.VMEM)] * 3,
        out_specs=[pl.BlockSpec(memory_space=pltpu.HBM)] * 3,
        scratch_shapes=[pltpu.SemaphoreType.DMA((3,))],
        name="store",
    )(*results)
    return tuple(outs)


def general(sizes, block, p0, p1, q5, q4, cf, residual, receiver_cell, tap_offset, tap_weight, trace_receiver):
    gathered, *mats = gather(sizes, block, residual)
    src = build_sources(block, gathered, receiver_cell, tap_offset, tap_weight, trace_receiver)
    return store(*wave(sizes, block, p0, p1, q5, q4, cf, src, mats))


def shards(sizes, *args):
    block = args[0].shape
    *results, flag = fused(sizes, *args[:-1], args[-1].reshape(1, -1))
    outs = lax.cond(
        flag[0] == 0,
        lambda *held: store(*held[:3]),
        lambda *held: general(sizes, block, *held[3:]),
        *results,
    )
    return tuple(o.reshape(block) for o in outs)


def solution(mesh):
    field = P(*AXES)
    return jax.shard_map(
        functools.partial(shards, tuple(mesh.shape[a] for a in AXES)),
        mesh=mesh,
        in_specs=(field,) * 5 + (P(None, "gz"), P(), P(), P(), P()),
        out_specs=(field,) * 3,
        check_vma=False,
    )
```

```python
import functools

import jax
import jax.numpy as jnp
from jax import lax
from jax.experimental import pallas as pl
from jax.experimental.pallas import tpu as pltpu
from jax.sharding import PartitionSpec as P

C = (-205.0 / 72.0, 8.0 / 5.0, -1.0 / 5.0, 8.0 / 315.0, -1.0 / 560.0)
AXES = ("gx", "gy", "gz")
MESH = pl.DeviceIdType.MESH


def split3(v):
    hi = v.astype(jnp.bfloat16)
    rest = v - hi.astype(jnp.float32)
    mid = rest.astype(jnp.bfloat16)
    lo = (rest - mid.astype(jnp.float32)).astype(jnp.bfloat16)
    return [hi, mid, lo]


def nt(a, b):
    return lax.dot_general(a, b, (((1,), (1,)), ((), ())), preferred_element_type=jnp.float32)


def source_kernel(block, res_ref, cell_ref, off_ref, w_ref, tr_ref, out_ref, table, info):
    bx, by, bz = block
    starts = [lax.axis_index(a) * n for a, n in zip(AXES, block)]
    taps, mics = w_ref.shape
    steps = res_ref.shape[1]
    rel = [cell_ref[d : d + 1, :] - starts[d] for d in range(3)]
    near = functools.reduce(
        jnp.logical_and, [(rel[d] >= -4) & (rel[d] < block[d] + 4) for d in range(3)]
    )
    at = [rel[d] + off_ref[d] for d in range(3)]
    inside = functools.reduce(
        jnp.logical_and, [(at[d] >= 0) & (at[d] < block[d]) for d in range(3)]
    )
    row = jnp.where(inside, at[0] * by + at[1], -1)
    col = jnp.where(inside, at[2], -1)
    table[0:taps, :] = row.astype(jnp.float32).astype(jnp.bfloat16)
    table[taps : 2 * taps, :] = col.astype(jnp.float32).astype(jnp.bfloat16)
    for i, part in enumerate(split3(w_ref[...])):
        table[(2 + i) * taps : (3 + i) * taps, :] = part
    near_f = jnp.where(near, 1.0, 0.0)
    lanes = 128
    blocks = mics // lanes
    tri = (
        lax.broadcasted_iota(jnp.int32, (lanes, lanes), 0)
        < lax.broadcasted_iota(jnp.int32, (lanes, lanes), 1)
    )
    tri = jnp.where(tri, 1.0, 0.0).astype(jnp.bfloat16)
    base = jnp.float32(0.0)
    for i in range(blocks):
        part = near_f[:, i * lanes : (i + 1) * lanes]
        before = jnp.dot(
            jnp.broadcast_to(part, (8, lanes)).astype(jnp.bfloat16),
            tri,
            preferred_element_type=jnp.float32,
        )[0:1]
        slot = jnp.where(part > 0.5, before + base, -1.0)
        info[0:1, i * lanes : (i + 1) * lanes] = slot
        base = base + jnp.sum(part)
    count = base.astype(jnp.int32)
    out_ref[...] = jnp.zeros_like(out_ref)
    share = 2
    held = lanes // share
    per = taps // share
    part_of = lax.broadcasted_iota(jnp.int32, (per, lanes), 1) // held

    def spread(v):
        out = v[0:per]
        for i in range(1, share):
            out = jnp.where(part_of == i, v[i * per : (i + 1) * per], out)
        return out

    def chunk(j, carry):
        slots = (lax.broadcasted_iota(jnp.int32, (held, mics), 0) + j * held).astype(jnp.float32)
        sel = jnp.where(slots == info[0:1, :], 1.0, 0.0)
        mic_id = lax.broadcasted_iota(jnp.int32, (1, mics), 1).astype(jnp.float32)
        mic = jnp.sum(sel * (mic_id + 1.0), axis=1, keepdims=True) - 1.0
        sel_r = jnp.where(tr_ref[...].astype(jnp.float32) == mic, 1.0, 0.0).astype(jnp.bfloat16)
        tab = jnp.concatenate([nt(table[...], sel.astype(jnp.bfloat16))] * share, axis=1)
        rows = spread(tab[0:taps])
        cols = spread(tab[taps : 2 * taps])
        weights = spread(
            tab[2 * taps : 3 * taps] + tab[3 * taps : 4 * taps] + tab[4 * taps : 5 * taps]
        )
        whole = jnp.concatenate([res_ref[g] for g in range(res_ref.shape[0])], axis=1)
        res = sum(nt(part, sel_r) for part in split3(whole))
        res = jnp.concatenate([res] * share, axis=1)
        iota_row = lax.broadcasted_iota(jnp.int32, (bx * by, lanes), 0).astype(jnp.float32)
        iota_col = lax.broadcasted_iota(jnp.int32, (bz, lanes), 0).astype(jnp.float32)
        group = 4
        for t0 in range(0, per, group):
            left, right = [[] for _ in range(steps)], []
            for t in range(t0, t0 + group):
                row_hot = iota_row == rows[t : t + 1]
                col_hot = jnp.where(iota_col == cols[t : t + 1], 1.0, 0.0).astype(jnp.bfloat16)
                right += [col_hot, col_hot]
                for n in range(steps):
                    amount = weights[t : t + 1] * res[n : n + 1]
                    hi = amount.astype(jnp.bfloat16).astype(jnp.float32)
                    lo = amount - hi
                    left[n].append(jnp.where(row_hot, hi, 0.0).astype(jnp.bfloat16))
                    left[n].append(jnp.where(row_hot, lo, 0.0).astype(jnp.bfloat16))
            right = jnp.concatenate(right, axis=1)
            for n in range(steps):
                out_ref[n] += nt(jnp.concatenate(left[n], axis=1), right)
        return carry

    lax.fori_loop(0, (count + held - 1) // held, chunk, 0)


def build_sources(block, residual, receiver_cell, tap_offset, tap_weight, trace_receiver):
    steps = residual.shape[1]
    taps, mics = tap_weight.shape
    return pl.pallas_call(
        functools.partial(source_kernel, block),
        out_shape=jax.ShapeDtypeStruct((steps, block[0] * block[1], block[2]), jnp.float32),
        in_specs=[pl.BlockSpec(memory_space=pltpu.VMEM)] * 5,
        out_specs=pl.BlockSpec(memory_space=pltpu.VMEM),
        scratch_shapes=[
            pltpu.VMEM((5 * taps, mics), jnp.bfloat16),
            pltpu.VMEM((8, mics), jnp.float32),
        ],
        compiler_params=pltpu.CompilerParams(vmem_limit_bytes=32 * 2**20),
        name="sources",
    )(residual, receiver_cell, tap_offset, tap_weight, trace_receiver)


def stencil(d):
    d = jnp.abs(d)
    return sum(jnp.where(d == k, float(round(5040 * C[k])), 0.0) for k in range(1, 5))


def cross(dx, dy):
    return jnp.where(dy == 0, stencil(dx), 0.0) + jnp.where(dx == 0, stencil(dy), 0.0)


def matrices(nx, ny, m_in, m_face, m_z, m_end):
    def grid(ref):
        return [lax.broadcasted_iota(jnp.int32, ref.shape, d) for d in range(2)]

    to, at = grid(m_in)
    m_in[...] = cross(to // ny - at // ny, to % ny - at % ny).astype(jnp.bfloat16)
    to, at = grid(m_face)
    x, y = to // ny, to % ny
    upper = at >= 4 * ny
    face = at - jnp.where(upper, 4 * ny, 0)
    in_x = cross(x - (face // ny + jnp.where(upper, nx, -4)), y - face % ny)
    pack = at - 8 * ny
    upper = pack >= 4 * nx
    pack = pack - jnp.where(upper, 4 * nx, 0)
    far = jnp.where(pack % 8 < 4, 0, 1) == jnp.where(upper, 1, 0)
    face_x = pack // 8 + jnp.where(far, nx // 2, 0)
    in_y = cross(x - face_x, y - (pack % 4 + jnp.where(upper, ny, -4)))
    m_face[...] = jnp.where(at < 8 * ny, in_x, in_y).astype(jnp.bfloat16)
    at, to = grid(m_z)
    m_z[...] = stencil(to - at).astype(jnp.bfloat16)
    at, to = grid(m_end)
    m_end[...] = stencil(to - jnp.where(at < 64, at + m_z.shape[0], at - 128)).astype(jnp.bfloat16)


def gather_kernel(n, block, res, out, m_in, m_face, m_z, m_end, land, send_sem, recv_sem):
    gz = lax.axis_index("gz")
    ahead = [{"gz": lax.rem(gz + k, n)} for k in range(1, n)]
    barrier = pltpu.get_barrier_semaphore()
    for other in ahead:
        pl.semaphore_signal(barrier, inc=1, device_id=other, device_id_type=MESH)
    pl.semaphore_wait(barrier, n - 1)
    moves = [
        pltpu.make_async_remote_copy(
            src_ref=res, dst_ref=land.at[gz],
            send_sem=send_sem.at[k], recv_sem=recv_sem.at[k],
            device_id=ahead[k], device_id_type=MESH,
        )
        for k in range(n - 1)
    ]
    for move in moves:
        move.start()
    matrices(block[0], block[1], m_in, m_face, m_z, m_end)
    land[gz] = res[...]
    for k in range(n - 1):
        dst = land.at[lax.rem(gz + n - 1 - k, n)]
        pltpu.make_async_remote_copy(
            src_ref=dst, dst_ref=dst,
            send_sem=send_sem.at[k], recv_sem=recv_sem.at[k],
            device_id=ahead[k], device_id_type=MESH,
        ).wait_recv()
    out[...] = land[...]
    for move in moves:
        move.wait_send()


def gather(sizes, block, residual):
    nx, ny, nz = block
    n = sizes[2]
    vmem = pl.BlockSpec(memory_space=pltpu.VMEM)
    shape = (n,) + residual.shape
    mats = [(nx * ny, nx * ny), (nx * ny, 8 * (nx + ny)), (nz, nz), (128, nz)]
    return pl.pallas_call(
        functools.partial(gather_kernel, n, block),
        out_shape=[jax.ShapeDtypeStruct(shape, jnp.float32)]
        + [jax.ShapeDtypeStruct(m, jnp.bfloat16) for m in mats],
        in_specs=[vmem],
        out_specs=[vmem] * 5,
        scratch_shapes=[
            pltpu.VMEM(shape, jnp.float32),
            pltpu.SemaphoreType.DMA((n,)),
            pltpu.SemaphoreType.DMA((n,)),
        ],
        compiler_params=pltpu.CompilerParams(
            collective_id=1, has_side_effects=True, vmem_limit_bytes=16 * 2**20
        ),
        cost_estimate=pl.CostEstimate(flops=4 * 10**9, bytes_accessed=12 * 10**6, transcendentals=0),
        name="gather",
    )(residual)


def nn(a, b):
    return jnp.dot(a, b, preferred_element_type=jnp.float32)


def wave_kernel(
    sizes, ny, p0, p1, q5, q4, cf, src, m_in, m_face, m_z, m_end, grad, one, zero,
    fp, fq, lap, lq, qb, hl, zl, ys, send_sem, recv_sem,
):
    steps = src.shape[0]
    rows, nz = p0.shape
    nx = rows // ny
    faces_rows = (4 * ny, 4 * ny, 4 * nx, 4 * nx)
    me = [lax.axis_index(a) for a in AXES]
    has = []
    for d in range(3):
        has += [me[d] > 0, me[d] < sizes[d] - 1]
    to = []
    for d in range(3):
        to += [{AXES[d]: jnp.maximum(me[d] - 1, 0)}, {AXES[d]: jnp.minimum(me[d] + 1, sizes[d] - 1)}]

    barrier = pltpu.get_barrier_semaphore()
    for f in range(6):
        @pl.when(has[f])
        def _(f=f):
            pl.semaphore_signal(barrier, inc=1, device_id=to[f], device_id_type=MESH)
    pl.semaphore_wait(barrier, sum(h.astype(jnp.int32) for h in has))

    sub = lax.broadcasted_iota(jnp.int32, (8, nz), 0)
    lane = lax.broadcasted_iota(jnp.int32, (rows, 128), 1)

    def field(ch, r):
        if r == 0 and ch == 0:
            return p1
        return (fp, fq)[ch].at[r]

    def landing(ch, r, f):
        if f >= 4:
            return zl.at[ch, r, f - 4]
        return hl.at[ch, r, pl.ds(sum(faces_rows[:f]), faces_rows[f])]

    def copies(ch, r):
        f_ref = field(ch, r)
        srcs = [
            f_ref.at[pl.ds(0, 4 * ny)],
            f_ref.at[pl.ds(rows - 4 * ny, 4 * ny)],
            ys.at[ch, r, 0],
            ys.at[ch, r, 1],
            f_ref.at[pl.ds(0, rows), pl.ds(0, 128)],
            f_ref.at[pl.ds(0, rows), pl.ds(nz - 128, 128)],
        ]
        return [
            pltpu.make_async_remote_copy(
                src_ref=srcs[f],
                dst_ref=landing(ch, r, f ^ 1),
                send_sem=send_sem.at[ch, r, f],
                recv_sem=recv_sem.at[ch, r, f ^ 1],
                device_id=to[f],
                device_id_type=MESH,
            )
            for f in range(6)
        ]

    def send(ch, r):
        f_ref = field(ch, r)
        moves = copies(ch, r)
        for f in (0, 1, 4, 5):
            @pl.when(has[f])
            def _(f=f):
                moves[f].start()
        for i in range(nx // 2):
            lo, far = i * ny, (i + nx // 2) * ny
            a, b = f_ref[lo : lo + 8], f_ref[far : far + 8]
            ys[ch, r, 0, 8 * i : 8 * i + 8] = jnp.where(sub < 4, a, pltpu.roll(b, 4, 0))
            a, b = f_ref[lo + ny - 8 : lo + ny], f_ref[far + ny - 8 : far + ny]
            ys[ch, r, 1, 8 * i : 8 * i + 8] = jnp.where(sub >= 4, a, pltpu.roll(b, 4, 0))
        for f in (2, 3):
            @pl.when(has[f])
            def _(f=f):
                moves[f].start()

    def land(ch, r):
        for f in range(6):
            @pl.when(has[f])
            def _(f=f):
                dst = landing(ch, r, f)
                pltpu.make_async_remote_copy(
                    src_ref=dst, dst_ref=dst,
                    send_sem=send_sem.at[ch, r, f], recv_sem=recv_sem.at[ch, r, f],
                    device_id=to[f], device_id_type=MESH,
                ).wait_recv()

    def local(ch, r, out):
        f = field(ch, r)[...]
        acc = 0.0
        for part in split3(f):
            acc = acc + nn(m_in[...], part) + nn(part, m_z[...])
        out[...] = acc * (1.0 / 5040.0) + (3.0 * C[0]) * f

    def finish(ch, r, out):
        land(ch, r)
        acc = 0.0
        for part in split3(hl[ch, r]):
            acc = acc + nn(m_face[...], part)
        for part in split3(jnp.where(lane < 64, zl[ch, r, 1], zl[ch, r, 0])):
            acc = acc + nn(part, m_end[...])
        return out[...] + acc * (1.0 / 5040.0)

    send(0, 0)
    fq[0] = cf[...] * q4[...]
    send(1, 0)
    for f in range(6):
        @pl.when(jnp.logical_not(has[f]))
        def _(f=f):
            for ch in range(2):
                for r in range(steps):
                    dst = landing(ch, r, f)
                    dst[...] = jnp.zeros(dst.shape, jnp.float32)

    local(0, 0, lap.at[0])
    local(1, 0, lq)
    for r in range(steps):
        full = finish(0, r, lap.at[r])
        lap[r] = full
        if r + 1 < steps:
            old = p0 if r == 0 else field(0, r - 1)
            fp[r + 1] = 2.0 * field(0, r)[...] - old[...] + cf[...] * full
            send(0, r + 1)
            local(0, r + 1, lap.at[r + 1])

        full = finish(1, r, lq)
        now = q4 if r == 0 else qb.at[r - 1]
        old = q5 if r == 0 else (q4 if r == 1 else qb.at[r - 2])
        new = 2.0 * now[...] - old[...] + full + src[steps - 1 - r]
        if r + 1 < steps:
            qb[r] = new
            fq[r + 1] = cf[...] * new
            send(1, r + 1)
            local(1, r + 1, lq)
        else:
            zero[...] = new
            one[...] = now[...]
            total = q4[...] * lap[steps - 1]
            for n in range(1, steps):
                total = total + qb[n - 1] * lap[steps - 1 - n]
            grad[...] = total

    for ch in range(2):
        for r in range(steps):
            moves = copies(ch, r)
            for f in range(6):
                @pl.when(has[f])
                def _(f=f):
                    moves[f].wait_send()


def wave(sizes, block, p0, p1, q5, q4, cf, src, mats):
    nx, ny, nz = block
    steps = src.shape[0]
    rows = nx * ny
    f32 = jnp.float32
    outs = pl.pallas_call(
        functools.partial(wave_kernel, sizes, ny),
        out_shape=[jax.ShapeDtypeStruct((rows, nz), f32)] * 3,
        in_specs=[pl.BlockSpec(memory_space=pltpu.VMEM)] * 10,
        out_specs=[pl.BlockSpec(memory_space=pltpu.VMEM)] * 3,
        scratch_shapes=[
            pltpu.VMEM((steps, rows, nz), f32),
            pltpu.VMEM((steps, rows, nz), f32),
            pltpu.VMEM((steps, rows, nz), f32),
            pltpu.VMEM((rows, nz), f32),
            pltpu.VMEM((steps, rows, nz), f32),
            pltpu.VMEM((2, steps, 8 * (nx + ny), nz), f32),
            pltpu.VMEM((2, steps, 2, rows, 128), f32),
            pltpu.VMEM((2, steps, 2, 4 * nx, nz), f32),
            pltpu.SemaphoreType.DMA((2, steps, 6)),
            pltpu.SemaphoreType.DMA((2, steps, 6)),
        ],
        compiler_params=pltpu.CompilerParams(
            collective_id=0, has_side_effects=True, vmem_limit_bytes=32 * 2**20
        ),
        name="wave",
    )(p0, p1, q5, q4, cf, src, *mats)
    return outs


CHUNKS = 5
HELD = 64
LANES = 128


def roll(v, shift, axis):
    shift = shift % v.shape[axis]
    return v if shift == 0 else pltpu.roll(v, shift, axis)


def near_counts(sizes, block, cells):
    near = []
    for d in range(2):
        at = lax.broadcasted_iota(jnp.int32, (sizes[d], cells[d].shape[1]), 0) * block[d]
        rel = cells[d] - at
        near.append(jnp.where((rel >= -4) & (rel < block[d] + 4), 1.0, 0.0))
    xy = jnp.concatenate([near[0][i : i + 1] * near[1] for i in range(sizes[0])], axis=0)
    counts = []
    for h in range(block[2] // LANES):
        at = lax.broadcasted_iota(jnp.int32, (sizes[2], cells[2].shape[1]), 0) * block[2] + h * LANES
        rel = cells[2] - at
        z = jnp.where((rel >= -4) & (rel < LANES + 4), 1.0, 0.0)
        counts.append(nt(xy.astype(jnp.bfloat16), z.astype(jnp.bfloat16)))
    return counts


def chunks_of(count):
    return jnp.floor((count + (HELD - 1.0)) * (1.0 / HELD))


def fused_kernel(
    sizes, ny,
    p0_h, p1_h, q5_h, q4_h, cf_h, res_h, cell_h, off_h, w_h, tr_h,
    grad, one, zero, p0, p1, q5, q4, cf, res_again, cell, off, w, tr, flag,
    load_sem,
    m_in, m_z, fp, fq, lap, base, ahead, qb, src, total,
    hx, hy, hz, ys, zs, send_sem, recv_sem,
    res, res_send, res_recv,
    sel_mic, table, tap_row, tap_col, tap_w, tap_res, hot, which,
):
    steps = res.shape[1]
    rows, nz = p1.shape
    nx = rows // ny
    block = (nx, ny, nz)
    tiles = rows // 8
    ytiles = ny // 8
    groups = tiles // 32
    halves = nz // LANES
    taps, mics = w.shape
    bf16, f32 = jnp.bfloat16, jnp.float32
    per = taps * HELD // LANES
    zero_slot = 2 * steps

    loads = [
        pltpu.make_async_copy(a, b, load_sem.at[i])
        for i, (a, b) in enumerate(
            [(p1_h, p1), (q4_h, q4), (cf_h, cf), (cell_h, cell), (off_h, off), (w_h, w), (tr_h, tr), (p0_h, p0), (q5_h, q5)]
        )
    ]
    for load in loads[:3]:
        load.start()

    me = [lax.axis_index(a) for a in AXES]
    has = []
    for d in range(3):
        has += [me[d] > 0, me[d] < sizes[d] - 1]
    to = []
    for d in range(3):
        to += [{AXES[d]: jnp.maximum(me[d] - 1, 0)}, {AXES[d]: jnp.minimum(me[d] + 1, sizes[d] - 1)}]
    peers = [{"gz": lax.rem(me[2] + k, sizes[2])} for k in range(1, sizes[2])]

    barrier = pltpu.get_barrier_semaphore()
    for f in range(4):
        @pl.when(has[f])
        def _(f=f):
            pl.semaphore_signal(barrier, inc=1, device_id=to[f], device_id_type=MESH)
    for peer in peers:
        pl.semaphore_signal(barrier, inc=1, device_id=peer, device_id_type=MESH)

    sub = lax.broadcasted_iota(jnp.int32, (8, nz), 0)
    lane = lax.broadcasted_iota(jnp.int32, (8, LANES), 1)
    lane_group = lane // 4

    def field(ch, r):
        if r == 0 and ch == 0:
            return p1
        return (fp, fq)[ch].at[r]

    def landing(ch, r, f, slot=None):
        slot = ch * steps + r if slot is None else slot
        return (hx, hy, hz)[f // 2].at[slot, f % 2]

    def copy(ch, r, f):
        f_ref = field(ch, r)
        if f == 0:
            face = f_ref.at[pl.ds(0, 4 * ny)]
        elif f == 1:
            face = f_ref.at[pl.ds(rows - 4 * ny, 4 * ny)]
        else:
            face = (ys, zs)[f // 2 - 1].at[ch, r, f % 2]
        return pltpu.make_async_remote_copy(
            src_ref=face,
            dst_ref=landing(ch, r, f ^ 1),
            send_sem=send_sem.at[ch, r, f],
            recv_sem=recv_sem.at[ch, r, f ^ 1],
            device_id=to[f],
            device_id_type=MESH,
        )

    def start(ch, r, faces):
        for f in faces:
            @pl.when(has[f])
            def _(f=f):
                copy(ch, r, f).start()

    def pack_y(ch, r):
        f_ref = field(ch, r)
        for i in range(nx // 2):
            lo, far = i * ny, (i + nx // 2) * ny
            a, b = f_ref[lo : lo + 8], f_ref[far : far + 8]
            ys[ch, r, 0, 8 * i : 8 * i + 8] = jnp.where(sub < 4, a, roll(b, 4, 0))
            a, b = f_ref[lo + ny - 8 : lo + ny], f_ref[far + ny - 8 : far + ny]
            ys[ch, r, 1, 8 * i : 8 * i + 8] = jnp.where(sub >= 4, a, roll(b, 4, 0))

    def pack_z(ch, r):
        f_ref = field(ch, r)
        for g in range(groups):
            low = jnp.zeros((8, LANES), f32)
            high = low
            for i in range(32):
                at = 8 * (32 * g + i)
                mine = lane_group == i
                low = jnp.where(mine, roll(f_ref[at : at + 8, 0:LANES], 4 * i, 1), low)
                high = jnp.where(mine, roll(f_ref[at : at + 8, nz - LANES : nz], 4 * i + 4, 1), high)
            zs[ch, r, 0, 8 * g : 8 * g + 8] = low
            zs[ch, r, 1, 8 * g : 8 * g + 8] = high

    def land(ch, r, faces):
        for f in faces:
            @pl.when(has[f])
            def _(f=f):
                dst = landing(ch, r, f)
                pltpu.make_async_remote_copy(
                    src_ref=dst, dst_ref=dst,
                    send_sem=send_sem.at[ch, r, f], recv_sem=recv_sem.at[ch, r, f],
                    device_id=to[f], device_id_type=MESH,
                ).wait_recv()

    def near_slot(ch, r, f):
        return jnp.where(has[f], ch * steps + r, zero_slot)

    def ramp(v, axis, at, upward):
        at = at % 4
        acc = 0.0
        for s in range(4):
            if upward:
                acc = acc + jnp.where(at + s < 4, C[4 - s], 0.0) * roll(v, -s, axis)
            else:
                acc = acc + jnp.where(at >= s, C[4 - s], 0.0) * roll(v, s, axis)
        return acc

    def local(ch, r):
        f = field(ch, r)[...]
        acc = 0.0
        for part in split3(f):
            acc = acc + nn(m_in[...], part) + nn(part, m_z[...])
        acc = acc * (1.0 / 5040.0) + (3.0 * C[0]) * f
        if ch == 0:
            if r + 1 < steps:
                old = p0 if r == 0 else field(0, r - 1)
                ahead[...] = 2.0 * f - old[...]
        else:
            now = q4 if r == 0 else (one if r == steps - 1 else qb.at[r - 1])
            old = q5 if r == 0 else (q4 if r == 1 else qb.at[r - 2])
            acc = acc + (2.0 * now[...] - old[...])
        base[ch] = acc

    def finish(ch, r):
        land(ch, r, (4, 5))
        for side in range(2):
            ref = landing(ch, r, 4 + side, near_slot(ch, r, 4 + side))
            for g in range(groups):
                v = ramp(ref[8 * g : 8 * g + 8], 1, lane, side == 0)
                for i in range(32):
                    at = 8 * (32 * g + i)
                    if side == 0:
                        base[ch, at : at + 8, 0:LANES] += jnp.where(lane < 4, roll(v, -4 * i, 1), 0.0)
                    else:
                        base[ch, at : at + 8, nz - LANES : nz] += jnp.where(
                            lane >= LANES - 4, roll(v, -4 - 4 * i, 1), 0.0
                        )
        land(ch, r, (0, 1, 2, 3))
        x_ref = [landing(ch, r, f, near_slot(ch, r, f)) for f in (0, 1)]
        y_ref = [landing(ch, r, f, near_slot(ch, r, f)) for f in (2, 3)]
        for i in range(nx // 2):
            y_part = [ramp(y_ref[side][8 * i : 8 * i + 8], 0, sub, side == 0) for side in range(2)]
            for x in (i, i + nx // 2):
                for yt in range(ytiles):
                    at = x * ny + 8 * yt
                    t = base[ch, at : at + 8]
                    if x < 4:
                        for j in range(x, 4):
                            t = t + C[x + 4 - j] * x_ref[0][j * ny + 8 * yt : j * ny + 8 * yt + 8]
                    if x >= nx - 4:
                        for j in range(x - nx + 5):
                            t = t + C[nx + j - x] * x_ref[1][j * ny + 8 * yt : j * ny + 8 * yt + 8]
                    if yt == 0:
                        part = y_part[0] if x != i else roll(y_part[0], 4, 0)
                        t = t + jnp.where(sub < 4, part, 0.0)
                    if yt == ytiles - 1:
                        part = y_part[1] if x != i else roll(y_part[1], 4, 0)
                        t = t + jnp.where(sub >= 4, part, 0.0)
                    if ch == 0:
                        lap[r, at : at + 8] = t
                        if r + 1 < steps:
                            fp[r + 1, at : at + 8] = ahead[at : at + 8] + cf[at : at + 8] * t
                    else:
                        out = zero if r == steps - 1 else (one if r == steps - 2 else qb.at[r])
                        out[at : at + 8] = t
                        if r + 1 < steps:
                            fq[r + 1, at : at + 8] = cf[at : at + 8] * t

    def send(ch, r):
        pack_y(ch, r)
        start(ch, r, (2, 3))
        start(ch, r, (0, 1))
        pack_z(ch, r)
        start(ch, r, (4, 5))

    def select():
        cells = [cell[d : d + 1, :] for d in range(3)]
        rel = [cells[d] - me[d] * block[d] for d in range(3)]
        side = functools.reduce(jnp.logical_and, [(rel[d] >= -4) & (rel[d] < block[d] + 4) for d in range(2)])
        near = [
            jnp.where(side & (rel[2] >= h * LANES - 4) & (rel[2] < (h + 1) * LANES + 4), 1.0, 0.0)
            for h in range(halves)
        ]
        near = jnp.concatenate(near, axis=0)
        tri = (
            lax.broadcasted_iota(jnp.int32, (LANES, LANES), 0)
            < lax.broadcasted_iota(jnp.int32, (LANES, LANES), 1)
        )
        tri = jnp.where(tri, 1.0, 0.0).astype(bf16)
        count = jnp.zeros((halves, 1), f32)
        order = []
        for i in range(mics // LANES):
            part = near[:, i * LANES : (i + 1) * LANES]
            order.append(nn(part.astype(bf16), tri) + count)
            count = count + jnp.sum(part, axis=1, keepdims=True)
        order = jnp.concatenate(order, axis=1)
        full = chunks_of(count)
        first = [jnp.zeros((1, 1), f32)]
        for h in range(halves):
            first.append(first[-1] + full[h : h + 1])
        slot = [
            jnp.where(near[h : h + 1] > 0.5, order[h : h + 1] + HELD * first[h], -1.0) for h in range(halves)
        ]
        at = [rel[d] + off[d] for d in range(3)]
        inside = functools.reduce(jnp.logical_and, [(at[d] >= 0) & (at[d] < block[d]) for d in range(3)])
        table[0:taps, :] = jnp.where(inside, at[0] * ny + at[1], -1).astype(f32).astype(bf16)
        table[taps : 2 * taps, :] = jnp.where(inside, at[2], -1).astype(f32).astype(bf16)
        for i, part in enumerate(split3(w[...])):
            table[(2 + i) * taps : (3 + i) * taps, :] = part

        mic_id = lax.broadcasted_iota(jnp.int32, (1, mics), 1).astype(f32) + 1.0
        trace_mic = tr[...].astype(f32) + 1.0
        part_of = lax.broadcasted_iota(jnp.int32, (per, LANES), 1) // HELD

        def spread(v):
            out = v[0:per]
            for i in range(1, LANES // HELD):
                out = jnp.where(part_of == i, v[i * per : (i + 1) * per], out)
            return out

        def chunk(j, carry):
            slots = (lax.broadcasted_iota(jnp.int32, (HELD, mics), 0) + j * HELD).astype(f32)
            hit = functools.reduce(jnp.logical_or, [slots == slot[h] for h in range(halves)])
            mic = jnp.sum(jnp.where(hit, mic_id, 0.0), axis=1, keepdims=True)
            sel_mic[j] = jnp.where(trace_mic == mic, 1.0, 0.0).astype(bf16)
            tab = nt(table[...], jnp.where(hit, 1.0, 0.0).astype(bf16))
            tab = jnp.concatenate([tab] * (LANES // HELD), axis=1)
            mine = jnp.zeros((1, 1), f32)
            for h in range(1, halves):
                mine = mine + jnp.where(j.astype(f32) >= first[h], 1.0, 0.0)
            which[j] = jnp.broadcast_to(mine, (8, LANES))
            rows_j = spread(tab[0:taps])
            tap_col[j] = spread(tab[taps : 2 * taps]) - LANES * mine
            tap_w[j] = spread(
                tab[2 * taps : 3 * taps] + tab[3 * taps : 4 * taps] + tab[4 * taps : 5 * taps]
            )
            iota_row = lax.broadcasted_iota(jnp.int32, (rows, LANES), 0).astype(f32)
            for t in range(per):
                hot[j, :, t * LANES : (t + 1) * LANES] = jnp.where(
                    iota_row == rows_j[t : t + 1], 1.0, 0.0
                ).astype(bf16)
            return carry

        lax.fori_loop(0, CHUNKS, chunk, 0, unroll=True)

    def check():
        every = near_counts(sizes, block, [cell[d : d + 1, :] for d in range(3)])
        most = jnp.max(functools.reduce(jnp.add, [chunks_of(c) for c in every]))
        flag[0] = (most > CHUNKS).astype(jnp.int32)

    def residuals():
        whole = jnp.concatenate([res[g] for g in range(sizes[2])], axis=1)
        parts = split3(whole)
        for j in range(CHUNKS):
            v = sum(nt(part, sel_mic[j]) for part in parts)
            tap_res[j] = jnp.concatenate([v] * (LANES // HELD), axis=1)

    def sources(first, count):
        levels = range(first, first + count)
        for n in levels:
            src[n] = jnp.zeros((nz, rows), f32)

        def chunk(j, carry):
            iota_col = lax.broadcasted_iota(jnp.int32, (LANES, LANES), 0).astype(f32)
            cols, weights, values = tap_col[j], tap_w[j], tap_res[j]
            right = [[[], []] for _ in levels]
            for t in range(per):
                col_hot = iota_col == cols[t : t + 1]
                for k, n in enumerate(levels):
                    amount = weights[t : t + 1] * values[n : n + 1]
                    hi = amount.astype(bf16).astype(f32)
                    right[k][0].append(jnp.where(col_hot, hi, 0.0).astype(bf16))
                    right[k][1].append(jnp.where(col_hot, amount - hi, 0.0).astype(bf16))
            both = jnp.concatenate(
                [jnp.concatenate(right[k][s], axis=1) for s in range(2) for k in range(count)], axis=0
            )
            acc = nt(both, hot[j])
            acc = acc[0 : count * LANES] + acc[count * LANES : 2 * count * LANES]
            mine = which[j, 0:1, 0:1]
            for h in range(halves):
                for k, n in enumerate(levels):
                    src[n, h * LANES : (h + 1) * LANES, :] += jnp.where(
                        mine == float(h), acc[k * LANES : (k + 1) * LANES], 0.0
                    )
            return carry

        lax.fori_loop(0, CHUNKS, chunk, 0, unroll=True)

    def stencils():
        to_, at_ = [lax.broadcasted_iota(jnp.int32, m_in.shape, d) for d in range(2)]
        m_in[...] = cross(to_ // ny - at_ // ny, to_ % ny - at_ % ny).astype(bf16)
        at_, to_ = [lax.broadcasted_iota(jnp.int32, m_z.shape, d) for d in range(2)]
        m_z[...] = stencil(to_ - at_).astype(bf16)

    stencils()
    for ref in (hx, hy, hz):
        for side in range(2):
            ref[zero_slot, side] = jnp.zeros(ref.shape[2:], f32)
    loads[0].wait()
    for load in loads[3:]:
        load.start()
    pack_y(0, 0)
    pack_z(0, 0)
    loads[1].wait()
    loads[2].wait()
    fq[0] = cf[...] * q4[...]
    pack_y(1, 0)
    pack_z(1, 0)
    pl.semaphore_wait(barrier, sum(h.astype(jnp.int32) for h in has[:4]) + len(peers))
    res_moves = [
        pltpu.make_async_remote_copy(
            src_ref=res_h, dst_ref=res.at[me[2]],
            send_sem=res_send.at[k], recv_sem=res_recv.at[k],
            device_id=peers[k], device_id_type=MESH,
        )
        for k in range(len(peers))
    ]
    for move in res_moves:
        move.start()
    start(0, 0, (2, 3, 0, 1))
    start(1, 0, (2, 3, 0, 1))
    start(0, 0, (4, 5))
    start(1, 0, (4, 5))
    own = pltpu.make_async_copy(res_h, res.at[me[2]], load_sem.at[len(loads)])
    own.start()

    for load in loads[3:]:
        load.wait()
    select()
    local(0, 0)
    local(1, 0)
    own.wait()
    for k in range(len(peers)):
        dst = res.at[lax.rem(me[2] + sizes[2] - 1 - k, sizes[2])]
        pltpu.make_async_remote_copy(
            src_ref=dst, dst_ref=dst,
            send_sem=res_send.at[k], recv_sem=res_recv.at[k],
            device_id=peers[k], device_id_type=MESH,
        ).wait_recv()
    residuals()
    late = steps - 1

    for r in range(steps):
        more = r + 1 < steps
        finish(0, r)
        if not more:
            res_again[...] = res[me[2]]
            grad[...] = total[...] + q4[...] * lap[steps - 1]
        if more:
            send(0, r + 1)
        if r == 0:
            sources(late, steps - late)
            base[1] += src[steps - 1].T
        finish(1, r)
        if more:
            send(1, r + 1)
            local(0, r + 1)
            local(1, r + 1)
            sources(late - 1 - r, 1)
            base[1] += src[late - 1 - r].T
        if r == steps - 2:
            check()
            part = one[...] * lap[0]
            for n in range(1, steps - 1):
                part = part + qb[steps - 2 - n] * lap[n]
            total[...] = part

    for move in res_moves:
        move.wait_send()
    for ch in range(2):
        for r in range(steps):
            for f in range(6):
                @pl.when(has[f])
                def _(f=f):
                    copy(ch, r, f).wait_send()


def fused(sizes, p0, p1, q5, q4, cf, residual, receiver_cell, tap_offset, tap_weight, trace_receiver):
    nx, ny, nz = p0.shape
    steps = residual.shape[0]
    taps, mics = tap_weight.shape
    rows = nx * ny
    f32, bf16 = jnp.float32, jnp.bfloat16
    flat = [a.reshape(rows, nz) for a in (p0, p1, q5, q4, cf)]
    plane = pltpu.VMEM((rows, nz), f32)
    slots = 2 * steps + 1
    packed = rows // 32
    return pl.pallas_call(
        functools.partial(fused_kernel, sizes, ny),
        out_shape=[jax.ShapeDtypeStruct((rows, nz), f32)] * 8
        + [
            jax.ShapeDtypeStruct(a.shape, a.dtype)
            for a in (residual, receiver_cell, tap_offset, tap_weight, trace_receiver)
        ]
        + [jax.ShapeDtypeStruct((1,), jnp.int32)],
        in_specs=[pl.BlockSpec(memory_space=pltpu.HBM)] * 10,
        out_specs=[pl.BlockSpec(memory_space=pltpu.VMEM)] * 13 + [pl.BlockSpec(memory_space=pltpu.SMEM)],
        scratch_shapes=[
            pltpu.SemaphoreType.DMA((10,)),
            pltpu.VMEM((rows, rows), bf16),
            pltpu.VMEM((nz, nz), bf16),
            pltpu.VMEM((steps, rows, nz), f32),
            pltpu.VMEM((steps, rows, nz), f32),
            pltpu.VMEM((steps, rows, nz), f32),
            pltpu.VMEM((2, rows, nz), f32),
            plane,
            pltpu.VMEM((steps - 2, rows, nz), f32),
            pltpu.VMEM((steps, nz, rows), f32),
            plane,
            pltpu.VMEM((slots, 2, 4 * ny, nz), f32),
            pltpu.VMEM((slots, 2, 4 * nx, nz), f32),
            pltpu.VMEM((slots, 2, packed, LANES), f32),
            pltpu.VMEM((2, steps, 2, 4 * nx, nz), f32),
            pltpu.VMEM((2, steps, 2, packed, LANES), f32),
            pltpu.SemaphoreType.DMA((2, steps, 6)),
            pltpu.SemaphoreType.DMA((2, steps, 6)),
            pltpu.VMEM((sizes[2],) + residual.shape, f32),
            pltpu.SemaphoreType.DMA((sizes[2],)),
            pltpu.SemaphoreType.DMA((sizes[2],)),
            pltpu.VMEM((CHUNKS, HELD, mics), bf16),
            pltpu.VMEM((5 * taps, mics), bf16),
            pltpu.VMEM((CHUNKS, taps * HELD // LANES, LANES), f32),
            pltpu.VMEM((CHUNKS, taps * HELD // LANES, LANES), f32),
            pltpu.VMEM((CHUNKS, taps * HELD // LANES, LANES), f32),
            pltpu.VMEM((CHUNKS, steps, LANES), f32),
            pltpu.VMEM((CHUNKS, rows, taps * HELD), bf16),
            pltpu.VMEM((CHUNKS, 8, LANES), f32),
        ],
        compiler_params=pltpu.CompilerParams(
            collective_id=2, has_side_effects=True, vmem_limit_bytes=56 * 2**20
        ),
        name="fused",
    )(*flat, residual, receiver_cell, tap_offset, tap_weight, trace_receiver)


def store_kernel(a, b, c, out_a, out_b, out_c, sem):
    moves = [
        pltpu.make_async_copy(s, d, sem.at[i])
        for i, (s, d) in enumerate(((a, out_a), (b, out_b), (c, out_c)))
    ]
    for move in moves:
        move.start()
    for move in moves:
        move.wait()


def store(*results):
    outs = pl.pallas_call(
        store_kernel,
        out_shape=[jax.ShapeDtypeStruct(a.shape, a.dtype) for a in results],
        in_specs=[pl.BlockSpec(memory_space=pltpu.VMEM)] * 3,
        out_specs=[pl.BlockSpec(memory_space=pltpu.HBM)] * 3,
        scratch_shapes=[pltpu.SemaphoreType.DMA((3,))],
        name="store",
    )(*results)
    return tuple(outs)


def general(sizes, block, p0, p1, q5, q4, cf, residual, receiver_cell, tap_offset, tap_weight, trace_receiver):
    gathered, *mats = gather(sizes, block, residual)
    src = build_sources(block, gathered, receiver_cell, tap_offset, tap_weight, trace_receiver)
    return store(*wave(sizes, block, p0, p1, q5, q4, cf, src, mats))


def shards(sizes, *args):
    block = args[0].shape
    *results, flag = fused(sizes, *args[:-1], args[-1].reshape(1, -1))
    outs = lax.cond(
        flag[0] == 0,
        lambda *held: store(*held[:3]),
        lambda *held: general(sizes, block, *held[3:]),
        *results,
    )
    return tuple(o.reshape(block) for o in outs)


def solution(mesh):
    field = P(*AXES)
    return jax.shard_map(
        functools.partial(shards, tuple(mesh.shape[a] for a in AXES)),
        mesh=mesh,
        in_specs=(field,) * 5 + (P(None, "gz"), P(), P(), P(), P()),
        out_specs=(field,) * 3,
        check_vma=False,
    )
```
